32 devices in a mesh: dp: 8 (over z, y), head: 4 (over x, core).
Axes of the slice: x: 2, y: 2, z: 4, core: 2. Of those that a mesh axis runs over, the one named last changes fastest.
Arguments:
- tokens: bfloat16 [24, 1024, 1024], P('dp', 'head'), may hold values from -6 to 6
- out_cotangent: bfloat16 [24, 1024, 1024], P('dp', 'head'), may hold values from -6 to 6
- lengths: int32 [24], P('dp'), may hold values from 256 to 1024, as said below
- qkv_weight: bfloat16 [1024, 3072], P('dp'), may hold values from -0.1875 to 0.1875
- out_weight: bfloat16 [1024, 1024], P('dp'), may hold values from -1.5 to 1.5
- ffn_in_weight: bfloat16 [1024, 4096], P('dp'), may hold values from -0.1875 to 0.1875
- ffn_out_weight: bfloat16 [4096, 1024], P('dp'), may hold values from -0.09375 to 0.09375
- qv_bias: float32 [2, 1024], replicated, may hold values from -0.3 to 0.3
- out_bias: float32 [1024], replicated, may hold values from -1.8 to 1.8
- ln1_gain: float32 [1024], replicated, may hold values from 0.25 to 1.75
- ln1_bias: float32 [1024], replicated, may hold values from -1.8 to 1.8
- ffn_in_bias: float32 [4096], replicated, may hold values from -3 to 3
- ffn_out_bias: float32 [1024], replicated, may hold values from -1.8 to 1.8
- ln2_gain: float32 [1024], replicated, may hold values from 0.25 to 1.75
- ln2_bias: float32 [1024], replicated, may hold values from -1.8 to 1.8
Outputs:
- layer_output: bfloat16 [24, 1024, 1024], P('dp', 'head')
- input_grad: bfloat16 [24, 1024, 1024], P('dp', 'head')
- qv_bias_grad: float32 [2, 1024], replicated
- out_bias_grad: float32 [1024], replicated
- ln1_bias_grad: float32 [1024], replicated
- ffn_in_bias_grad: float32 [4096], replicated
- ffn_out_bias_grad: float32 [1024], replicated
- ln2_bias_grad: float32 [1024], replicated
The draws below stay inside these ranges and needn't reach their ends.
Inputs may be any that keep to these rules, and one draw needn't show every extreme that they name: `lengths`: in each aligned group of 3 sequences (those of one index of dp) one sequence has length 1024 and another 1024 // 4.
All inputs are finite; a program needn't handle non-finite values.
Results may differ from the reference program's by a relative error of at most 0.014.
Values may be sent and summed in bfloat16 or wider, within the bound.
A program may use at most 128 MiB of HBM per device.

```python
import math
import jax
import jax.numpy as jnp
from jax import lax

D = 1024
HEADS = 16
HEAD_DIM = 64
FF = 4096
SEQ = 1024
SEQS_DEV = 3
SEQS = 24


def draw_lengths(key, part):
    key_base, key_order = jax.random.split(jax.random.fold_in(key, 7))
    groups = SEQS // SEQS_DEV
    base = jax.random.randint(key_base, (groups, SEQS_DEV), SEQ // 4, SEQ + 1)
    ranks_raw = jax.random.randint(key_order, (groups, SEQS_DEV), 0, 1 << 20) * SEQS_DEV
    ranks_raw = ranks_raw + jnp.arange(SEQS_DEV, dtype=jnp.int32)[None, :]
    order = jnp.argsort(ranks_raw, axis=1)
    ranking = jnp.argsort(order, axis=1)
    lengths = jnp.where(ranking == 0, SEQ, jnp.where(ranking == 1, SEQ // 4, base))
    return lengths.reshape(SEQS).astype(jnp.int32)


def levels(key, dims, pieces, least, largest):
    loudness, own = 1.0, jax.random.fold_in(key, 6)
    for position, blocks in pieces:
        steps = jnp.exp(jax.random.uniform(jax.random.fold_in(own, position), (blocks,), jnp.float32, least / len(pieces), largest / len(pieces)))
        loudness = loudness * jnp.repeat(steps, dims[position] // blocks).reshape([-1 if axis == position else 1 for axis in range(len(dims))])
    return loudness


def gaussian(rng, dims, scale, reach, pieces=(), kind=jnp.bfloat16):
    values = jax.random.normal(rng, dims, jnp.float32) * scale
    if len(pieces) > 0:
        values = levels(rng, dims, pieces, -0.22, 0.18) * values
    return jnp.clip(values, min=-reach, max=reach).astype(kind)


def setup_inputs(seed: int = 0) -> dict:
    arg_keys = jax.random.split(jax.random.key(seed), 16)
    tokens = gaussian(arg_keys[0], (SEQS, SEQ, D), 1.0, 6.0, ((0, 8), (1, 4)))
    out_cotangent = gaussian(arg_keys[1], (SEQS, SEQ, D), 1.0, 6.0, ((0, 8), (1, 4)))
    lengths = draw_lengths(jax.random.fold_in(arg_keys[15], 71), 0)
    qkv_weight = gaussian(arg_keys[3], (D, 3 * D), D ** -0.5, 0.1875, ((0, 8),))
    out_weight = gaussian(arg_keys[4], (D, D), (16 * D // SEQ) ** -0.5, 1.5, ((0, 8),))
    ffn_in_weight = gaussian(arg_keys[5], (D, FF), D ** -0.5, 0.1875, ((0, 8),))
    ffn_out_weight = gaussian(arg_keys[6], (FF, D), FF ** -0.5, 0.09375, ((0, 8),))
    qv_bias = gaussian(arg_keys[7], (2, D), 0.05, 0.3, (), jnp.float32)
    out_bias = gaussian(arg_keys[8], (D,), 0.3, 1.8, (), jnp.float32)
    ln1_gain = jnp.clip(1.0 + 0.15 * jax.random.normal(arg_keys[9], (D,), jnp.float32), 0.25, 1.75)
    ln1_bias = gaussian(arg_keys[10], (D,), 0.3, 1.8, (), jnp.float32)
    ffn_in_bias = gaussian(arg_keys[11], (FF,), 0.5, 3.0, (), jnp.float32)
    ffn_out_bias = gaussian(arg_keys[12], (D,), 0.3, 1.8, (), jnp.float32)
    ln2_gain = jnp.clip(1.0 + 0.15 * jax.random.normal(arg_keys[13], (D,), jnp.float32), 0.25, 1.75)
    ln2_bias = gaussian(arg_keys[14], (D,), 0.3, 1.8, (), jnp.float32)
    return {"tokens": tokens, "out_cotangent": out_cotangent, "lengths": lengths, "qkv_weight": qkv_weight, "out_weight": out_weight, "ffn_in_weight": ffn_in_weight, "ffn_out_weight": ffn_out_weight, "qv_bias": qv_bias, "out_bias": out_bias, "ln1_gain": ln1_gain, "ln1_bias": ln1_bias, "ffn_in_bias": ffn_in_bias, "ffn_out_bias": ffn_out_bias, "ln2_gain": ln2_gain, "ln2_bias": ln2_bias}


precise = lax.Precision.HIGHEST
epsilon = 1e-12

@jax.custom_vjp
def low(v):
    return lax.optimization_barrier(v.astype(jnp.bfloat16)).astype(jnp.float32)

@jax.custom_vjp
def low_back(v):
    return v

def low_keep(v):
    return (low(v), None)

def low_pass(kept, grad):
    return (grad,)

def back_keep(v):
    return (v, None)

def back_low(kept, grad):
    return (low(grad),)
low.defvjp(low_keep, low_pass)
low_back.defvjp(back_keep, back_low)

def matmul(left, right):
    return jnp.dot(left, right, precision=precise)

def layer_norm(inputs, gain, shift):
    centre = inputs - lax.optimization_barrier(jnp.mean(inputs, axis=-1, keepdims=True))
    spread = lax.optimization_barrier(jnp.mean(centre * centre, axis=-1, keepdims=True))
    return centre * lax.rsqrt(spread + epsilon) * gain + shift

def gelu_exact(inputs):
    return 0.5 * inputs * (1.0 + jax.scipy.special.erf(inputs * 0.7071067811865476))

def group_forward(x_group, len_group, biases, weights):
    qv_bias, out_bias, ln1_bias, ffn_in_bias, ffn_out_bias, ln2_bias = biases
    qkv_weight, out_weight, ffn_in_weight, ffn_out_weight, ln1_gain, ln2_gain = weights
    group_count = x_group.shape[0]
    flat_rows = x_group.reshape(group_count * SEQ, D)
    projected = matmul(flat_rows, qkv_weight)
    queries = low(low_back(projected[:, :D] + qv_bias[0]))
    keys_all = low(low_back(projected[:, D:2 * D]))
    values = low(low_back(projected[:, 2 * D:] + qv_bias[1]))
    head_shape = (group_count, SEQ, HEADS, HEAD_DIM)
    scores = jnp.einsum('gqhd,gkhd->ghqk', queries.reshape(head_shape), keys_all.reshape(head_shape), precision=precise) * (1.0 / math.sqrt(HEAD_DIM))
    scores = low_back(scores)
    visible = jnp.arange(SEQ, dtype=jnp.int32)[None, :] < len_group[:, None]
    scores = jnp.where(visible[:, None, None, :], scores, -1000000000.0)
    attn_probs = low(jax.nn.softmax(scores, axis=-1))
    attended = jnp.einsum('ghqk,gkhd->gqhd', attn_probs, values.reshape(head_shape), precision=precise)
    attended = low(low_back(attended.reshape(group_count * SEQ, D)))
    branch = low_back(matmul(attended, out_weight) + out_bias)
    normed_one = layer_norm(flat_rows + branch, ln1_gain, ln1_bias)
    hidden = low_back(matmul(low(normed_one), ffn_in_weight) + ffn_in_bias)
    ffn_out = low_back(matmul(low(gelu_exact(hidden)), ffn_out_weight) + ffn_out_bias)
    result = layer_norm(normed_one + ffn_out, ln2_gain, ln2_bias)
    return result.reshape(group_count, SEQ, D)

def reference(tokens, out_cotangent, lengths, qkv_weight, out_weight, ffn_in_weight, ffn_out_weight, qv_bias, out_bias, ln1_gain, ln1_bias, ffn_in_bias, ffn_out_bias, ln2_gain, ln2_bias):
    weights = (qkv_weight.astype(jnp.float32), out_weight.astype(jnp.float32), ffn_in_weight.astype(jnp.float32), ffn_out_weight.astype(jnp.float32), ln1_gain.astype(jnp.float32), ln2_gain.astype(jnp.float32))
    group_size = math.gcd(SEQS, max(1, 4096 // SEQ))
    x_groups = tokens.astype(jnp.float32).reshape(SEQS // group_size, group_size, SEQ, D)
    len_groups = lengths.astype(jnp.int32).reshape(SEQS // group_size, group_size)
    biases = (qv_bias.astype(jnp.float32), out_bias.astype(jnp.float32), ln1_bias.astype(jnp.float32), ffn_in_bias.astype(jnp.float32), ffn_out_bias.astype(jnp.float32), ln2_bias.astype(jnp.float32))
    step_fn = jax.checkpoint(group_forward)

    def forward(x_all, bias_all):
        return lax.map(lambda group_pair: step_fn(group_pair[0], group_pair[1], bias_all, weights), (x_all, len_groups))
    result, pullback = jax.vjp(forward, x_groups, biases)
    grad_x, grad_biases = pullback(out_cotangent.astype(jnp.float32).reshape(result.shape))
    return (result.reshape(SEQS, SEQ, D).astype(jnp.bfloat16), grad_x.reshape(SEQS, SEQ, D).astype(jnp.bfloat16), grad_biases[0], grad_biases[1], grad_biases[2], grad_biases[3], grad_biases[4], grad_biases[5])
```

```python
import functools
import math

import jax
import jax.numpy as jnp
from jax import lax
from jax.experimental import pallas as pl
from jax.experimental.pallas import tpu as pltpu
from jax.sharding import PartitionSpec as P

HEAD_DIM = 64


epsilon = 1e-12


def layer_norm(inputs, gain, shift):
    centre = inputs - jnp.mean(inputs, axis=-1, keepdims=True)
    spread = jnp.mean(centre * centre, axis=-1, keepdims=True)
    return centre * lax.rsqrt(spread + epsilon) * gain + shift


def gelu_exact(inputs):
    return 0.5 * inputs * (1.0 + jax.scipy.special.erf(inputs * 0.7071067811865476))


def back_product(grads, weight):
    return lax.dot_general(
        grads, weight, (((1,), (1,)), ((), ())), preferred_element_type=jnp.float32
    )


def on_device(
    tokens,
    out_cotangent,
    lengths,
    qkv_weight,
    out_weight,
    ffn_in_weight,
    ffn_out_weight,
    qv_bias,
    out_bias,
    ln1_gain,
    ln1_bias,
    ffn_in_bias,
    ffn_out_bias,
    ln2_gain,
    ln2_bias,
):
    seqs_here, tok_part, width = tokens.shape
    row_count = seqs_here * tok_part
    flat_rows = tokens.reshape(row_count, width)
    gathered = (
        lax.all_gather(qkv_weight, "dp", axis=0, tiled=True),
        lax.all_gather(out_weight, "dp", axis=0, tiled=True),
        lax.all_gather(ffn_in_weight, "dp", axis=0, tiled=True),
        lax.all_gather(ffn_out_weight, "dp", axis=0, tiled=True),
    )
    qkv_full, attn_full, first_full, second_full = gathered
    projected = jnp.dot(flat_rows, qkv_full, preferred_element_type=jnp.float32)
    tok_shape = (seqs_here, tok_part, width)
    queries = (projected[:, :width] + qv_bias[0]).astype(jnp.bfloat16).reshape(tok_shape)
    keys_tok = projected[:, width : 2 * width].astype(jnp.bfloat16).reshape(tok_shape)
    values_tok = (projected[:, 2 * width :] + qv_bias[1]).astype(jnp.bfloat16).reshape(tok_shape)
    head_q, head_k, head_v = (
        lax.all_to_all(queries, "head", split_axis=2, concat_axis=1, tiled=True),
        lax.all_to_all(keys_tok, "head", split_axis=2, concat_axis=1, tiled=True),
        lax.all_to_all(values_tok, "head", split_axis=2, concat_axis=1, tiled=True),
    )
    seq_len = head_q.shape[1]
    head_part = head_q.shape[2]
    local_heads = head_part // HEAD_DIM
    block_rows = min(512, seq_len)
    block_count = seq_len // block_rows
    score_scale = 1.0 / math.sqrt(HEAD_DIM)
    head_shape = (seqs_here, seq_len, local_heads, HEAD_DIM)
    query_heads = head_q.reshape(head_shape)
    key_heads = head_k.reshape(head_shape)
    value_heads = head_v.reshape(head_shape)
    key_index = lax.iota(jnp.int32, seq_len)

    def seq_forward(seq_items):
        query_seq, key_seq, value_seq, length = seq_items
        visible = key_index < length
        query_blocks = query_seq.reshape(block_count, block_rows, local_heads, HEAD_DIM)

        def block_forward(query_block):
            scores = (
                jnp.einsum("qhd,khd->hqk", query_block, key_seq, preferred_element_type=jnp.float32)
                * score_scale
            )
            scores = jnp.where(visible[None, None, :], scores, -1000000000.0)
            highest = jnp.max(scores, axis=-1, keepdims=True)
            raised = jnp.exp(scores - highest)
            totals = jnp.sum(raised, axis=-1, keepdims=True)
            attn_probs = (raised / totals).astype(jnp.bfloat16)
            attended = jnp.einsum(
                "hqk,khd->qhd", attn_probs, value_seq, preferred_element_type=jnp.float32
            )
            return (attended.astype(jnp.bfloat16), (highest + jnp.log(totals))[:, :, 0])

        attended, log_block = lax.map(block_forward, query_blocks)
        return (attended.reshape(seq_len, head_part), log_block)

    head_out, log_totals = lax.map(seq_forward, (query_heads, key_heads, value_heads, lengths))
    tok_attn = lax.all_to_all(head_out, "head", split_axis=1, concat_axis=2, tiled=True)
    branch = (
        jnp.dot(tok_attn.reshape(row_count, width), attn_full, preferred_element_type=jnp.float32)
        + out_bias
    )
    residual_one = flat_rows.astype(jnp.float32) + branch
    normed_one, norm_one_back = jax.vjp(
        lambda inputs: layer_norm(inputs, ln1_gain, ln1_bias), residual_one
    )
    hidden = (
        jnp.dot(normed_one.astype(jnp.bfloat16), first_full, preferred_element_type=jnp.float32)
        + ffn_in_bias
    )
    active, gelu_back = jax.vjp(gelu_exact, hidden)
    ffn_out = (
        jnp.dot(active.astype(jnp.bfloat16), second_full, preferred_element_type=jnp.float32)
        + ffn_out_bias
    )
    result, norm_two_back = jax.vjp(
        lambda inputs: layer_norm(inputs, ln2_gain, ln2_bias), normed_one + ffn_out
    )
    layer_output = result.astype(jnp.bfloat16).reshape(tok_shape)
    qkv_back, attn_back, first_back, second_back = (
        lax.all_gather(qkv_weight, "dp", axis=0, tiled=True),
        lax.all_gather(out_weight, "dp", axis=0, tiled=True),
        lax.all_gather(ffn_in_weight, "dp", axis=0, tiled=True),
        lax.all_gather(ffn_out_weight, "dp", axis=0, tiled=True),
    )
    grad_out = out_cotangent.reshape(row_count, width).astype(jnp.float32)
    grad_ln2_bias = jnp.sum(grad_out, axis=0)
    (grad_res_two,) = norm_two_back(grad_out)
    grad_ffn_out = grad_res_two.astype(jnp.bfloat16)
    grad_ffn_out_bias = jnp.sum(grad_ffn_out.astype(jnp.float32), axis=0)
    grad_active = back_product(grad_ffn_out, second_back)
    (grad_hidden,) = gelu_back(grad_active)
    grad_hidden = grad_hidden.astype(jnp.bfloat16)
    grad_ffn_in_bias = jnp.sum(grad_hidden.astype(jnp.float32), axis=0)
    grad_normed = back_product(grad_hidden, first_back) + grad_res_two
    grad_ln1_bias = jnp.sum(grad_normed, axis=0)
    (grad_res_one,) = norm_one_back(grad_normed)
    grad_branch = grad_res_one.astype(jnp.bfloat16)
    grad_out_bias = jnp.sum(grad_branch.astype(jnp.float32), axis=0)
    grad_attended = back_product(grad_branch, attn_back).astype(jnp.bfloat16).reshape(tok_shape)
    grad_heads = lax.all_to_all(
        grad_attended, "head", split_axis=2, concat_axis=1, tiled=True
    ).reshape(head_shape)

    def seq_backward(seq_items):
        query_seq, key_seq, value_seq, grad_seq, log_seq, length = seq_items
        visible = key_index < length
        query_blocks = query_seq.reshape(block_count, block_rows, local_heads, HEAD_DIM)
        grad_blocks = grad_seq.reshape(block_count, block_rows, local_heads, HEAD_DIM)

        def block_backward(carry, block_items):
            key_acc, value_acc = carry
            query_block, grad_block, log_block = block_items
            scores = (
                jnp.einsum("qhd,khd->hqk", query_block, key_seq, preferred_element_type=jnp.float32)
                * score_scale
            )
            scores = jnp.where(visible[None, None, :], scores, -1000000000.0)
            attn_probs = jnp.exp(scores - log_block[:, :, None])
            grad_probs = jnp.einsum(
                "qhd,khd->hqk", grad_block, value_seq, preferred_element_type=jnp.float32
            )
            centre = jnp.sum(attn_probs * grad_probs, axis=-1, keepdims=True)
            grad_scores = (attn_probs * (grad_probs - centre)).astype(jnp.bfloat16)
            grad_query = (
                jnp.einsum("hqk,khd->qhd", grad_scores, key_seq, preferred_element_type=jnp.float32)
                * score_scale
            )
            key_acc = key_acc + jnp.einsum(
                "hqk,qhd->khd", grad_scores, query_block, preferred_element_type=jnp.float32
            )
            value_acc = value_acc + jnp.einsum(
                "hqk,qhd->khd",
                attn_probs.astype(jnp.bfloat16),
                grad_block,
                preferred_element_type=jnp.float32,
            )
            return ((key_acc, value_acc), grad_query.astype(jnp.bfloat16))

        zero_acc = jnp.zeros((seq_len, local_heads, HEAD_DIM), jnp.float32)
        (key_acc, value_acc), grad_queries = lax.scan(
            block_backward, (zero_acc, zero_acc), (query_blocks, grad_blocks, log_seq)
        )
        return (
            grad_queries.reshape(seq_len, head_part),
            (key_acc * score_scale).astype(jnp.bfloat16).reshape(seq_len, head_part),
            value_acc.astype(jnp.bfloat16).reshape(seq_len, head_part),
        )

    grad_q_heads, grad_k_heads, grad_v_heads = lax.map(
        seq_backward, (query_heads, key_heads, value_heads, grad_heads, log_totals, lengths)
    )
    grad_q_tok, grad_k_tok, grad_v_tok = (
        lax.all_to_all(grad_q_heads, "head", split_axis=1, concat_axis=2, tiled=True),
        lax.all_to_all(grad_k_heads, "head", split_axis=1, concat_axis=2, tiled=True),
        lax.all_to_all(grad_v_heads, "head", split_axis=1, concat_axis=2, tiled=True),
    )
    grad_q_rows = grad_q_tok.reshape(row_count, width)
    grad_k_rows = grad_k_tok.reshape(row_count, width)
    grad_v_rows = grad_v_tok.reshape(row_count, width)
    grad_input = (
        grad_res_one
        + back_product(grad_q_rows, qkv_back[:, :width])
        + back_product(grad_k_rows, qkv_back[:, width : 2 * width])
        + back_product(grad_v_rows, qkv_back[:, 2 * width :])
    )
    grad_qv = jnp.stack(
        [
            jnp.sum(grad_q_rows.astype(jnp.float32), axis=0),
            jnp.sum(grad_v_rows.astype(jnp.float32), axis=0),
        ]
    )
    bias_totals = lax.psum(
        (grad_qv, grad_out_bias, grad_ln1_bias, grad_ffn_in_bias, grad_ffn_out_bias, grad_ln2_bias),
        ("dp", "head"),
    )
    return (
        layer_output,
        grad_input.astype(jnp.bfloat16).reshape(tok_shape),
        bias_totals[0],
        bias_totals[1],
        bias_totals[2],
        bias_totals[3],
        bias_totals[4],
        bias_totals[5],
    )


MESH_IDS = pl.DeviceIdType.MESH
BF16, F32 = jnp.bfloat16, jnp.float32
ANY = pl.BlockSpec(memory_space=pl.ANY)
LANES = 128
NT = (((1,), (1,)), ((), ()))


def mm(left, right):
    return jnp.dot(left, right, preferred_element_type=F32)


def mm_nt(left, right):
    return lax.dot_general(left, right, NT, preferred_element_type=F32)


def whole(shape, memory_space=pltpu.VMEM):
    return pl.BlockSpec(memory_space=memory_space)


def params(vmem, **more):
    return pltpu.CompilerParams(vmem_limit_bytes=vmem << 20, **more)


def order_of(lengths):
    count = lengths.shape[0]
    place = lax.iota(jnp.int32, count)
    before = (lengths[None, :] < lengths[:, None]) | (
        (lengths[None, :] == lengths[:, None]) & (place[None, :] < place[:, None])
    )
    rank = jnp.sum(before.astype(jnp.int32), axis=1)
    hit = rank[None, :] == place[:, None]
    perm = jnp.sum(jnp.where(hit, place[None, :], 0), axis=1)
    lens = jnp.sum(jnp.where(hit, lengths[None, :], 0), axis=1)
    return perm.astype(jnp.int32), lens.astype(jnp.int32)


def pair_copy_kernel(perm_ref, a_ref, b_ref, a_out, b_out):
    a_out[...] = a_ref[...]
    b_out[...] = b_ref[...]


def permute_pair(perm, first, second, scatter):
    count, rows, width = first.shape
    here = pl.BlockSpec((1, rows, width), lambda i, perm: (i, 0, 0))
    there = pl.BlockSpec((1, rows, width), lambda i, perm: (perm[i], 0, 0))
    ins, outs = (here, there) if scatter else (there, here)
    return pl.pallas_call(
        pair_copy_kernel,
        out_shape=[jax.ShapeDtypeStruct(first.shape, first.dtype)] * 2,
        grid_spec=pltpu.PrefetchScalarGridSpec(
            num_scalar_prefetch=1, grid=(count,), in_specs=[ins] * 2, out_specs=[outs] * 2
        ),
        name="unsort" if scatter else "sort",
    )(perm, first, second)


class Place:
    def __init__(self, z_count):
        self.dp, self.head = lax.axis_index("dp"), lax.axis_index("head")
        self.z, self.y = self.dp // 2, self.dp % 2
        self.x, self.core = self.head // 2, self.head % 2
        self.z_count = z_count

    def along_z(self, step):
        return (((self.z + step) % self.z_count) * 2 + self.y, self.head)

    def other_y(self):
        return (self.z * 2 + (1 - self.y), self.head)

    def other_x(self):
        return (self.dp, (1 - self.x) * 2 + self.core)

    def other_core(self):
        return (self.dp, self.x * 2 + (1 - self.core))

    def peers(self):
        steps = [self.along_z(step) for step in range(1, self.z_count)]
        return steps + [self.other_y(), self.other_x(), self.other_core()]


def meet(place):
    barrier = pltpu.get_barrier_semaphore()
    peers = place.peers()
    for peer in peers:
        pl.semaphore_signal(barrier, inc=1, device_id=peer, device_id_type=MESH_IDS)
    pl.semaphore_wait(barrier, len(peers))


def push(src, dst, send, recv, target):
    return pltpu.make_async_remote_copy(
        src_ref=src, dst_ref=dst, send_sem=send, recv_sem=recv, device_id=target, device_id_type=MESH_IDS
    )


def weight_chunks(shards, fulls, piece):
    chunks = []
    for shard, full in zip(shards, fulls):
        rows, cols = shard.shape
        row_step = min(rows, 128)
        col_step = max(LANES, min(cols, piece // row_step))
        for row in range(0, rows, row_step):
            for col in range(0, cols, col_step):
                chunks.append((shard, full, row, row_step, col, min(col_step, cols - col)))
    return chunks


def gather_kernel(z_count, piece, *refs):
    shards, (tok, cot), refs = refs[:4], refs[4:6], refs[6:]
    fulls, (tok_all, tok_short, cot_pair), refs = refs[:4], refs[4:7], refs[7:]
    z_send, z_recv, h_send, h_recv, local, t_send, t_recv, t_local = refs
    place = Place(z_count)
    x, core, z, y = place.x, place.core, place.z, place.y
    meet(place)
    started = []

    def go(copy):
        copy.start()
        started.append(copy)
        return copy

    keep, give = 2 - x, 1 + x
    tok_x = go(push(tok.at[give], tok_all.at[x, core], t_send.at[0], t_recv.at[0], place.other_x()))
    own_tok = pltpu.make_async_copy(tok.at[keep], tok_all.at[x, core], t_local.at[0])
    own_tok.start()
    own_cot = pltpu.make_async_copy(cot.at[keep], cot_pair.at[x], t_local.at[1])
    own_cot.start()
    first = (x == 0) & (core == 0)
    short_x = push(tok.at[0], tok_short, t_send.at[1], t_recv.at[1], place.other_x())
    short_own = pltpu.make_async_copy(tok.at[0], tok_short, t_local.at[2])
    short_core = push(tok_short, tok_short, t_send.at[2], t_recv.at[2], place.other_core())

    @pl.when(first)
    def _():
        short_x.start()
        short_own.start()

    chunks = weight_chunks(shards, fulls, piece)
    plans = []
    for number, (shard, full, row, rows, col, cols) in enumerate(chunks):
        base = row + core * (rows // 2)
        role = pl.ds(pl.multiple_of(base + x * (rows // 8), 16), rows * 3 // 8)
        own = pl.ds(pl.multiple_of(base + x * (rows * 3 // 8), 16), rows // 8)
        half = pl.ds(pl.multiple_of(base, 16), rows // 2)
        span = pl.ds(col, cols)
        along = [
            push(
                shard.at[role, span],
                full.at[z, y, role, span],
                z_send.at[number, step - 1],
                z_recv.at[number, step - 1],
                place.along_z(step),
            )
            for step in range(1, z_count)
        ]
        here = pltpu.make_async_copy(shard.at[role, span], full.at[z, y, role, span], local.at[number])
        col_y = full.at[:, y, role, span]
        to_y = push(col_y, col_y, h_send.at[number, 0], h_recv.at[number, 0], place.other_y())
        col_x = full.at[:, :, own, span]
        to_x = push(col_x, col_x, h_send.at[number, 1], h_recv.at[number, 1], place.other_x())
        col_c = full.at[:, :, half, span]
        to_c = push(col_c, col_c, h_send.at[number, 2], h_recv.at[number, 2], place.other_core())
        plans.append((along, here, to_y, to_x, to_c))
    count = len(plans)
    tok_core = push(
        tok_all.at[:, core], tok_all.at[:, core], t_send.at[3], t_recv.at[3], place.other_core()
    )
    cot_x = push(cot.at[give], cot_pair.at[x], t_send.at[4], t_recv.at[4], place.other_x())
    for step in range(count + 4):
        if step < count:
            for copy in plans[step][0]:
                copy.start()
            plans[step][1].start()
        if 0 <= step - 1 < count:
            along, here, to_y, _, _ = plans[step - 1]
            for copy in along:
                copy.wait_recv()
            here.wait()
            to_y.start()
        if 0 <= step - 2 < count:
            plans[step - 2][2].wait_recv()
            plans[step - 2][3].start()
        if 0 <= step - 3 < count:
            plans[step - 3][3].wait_recv()
            plans[step - 3][4].start()
        if step == 0:
            own_tok.wait()
            tok_x.wait_recv()
            tok_core.start()

            @pl.when((x == 1) & (core == 0))
            def _():
                short_x.wait_recv()

            @pl.when(first)
            def _():
                short_own.wait()

            @pl.when(core == 0)
            def _():
                short_core.start()

        if step == 3:
            cot_x.start()
    for along, here, to_y, to_x, to_c in plans:
        to_c.wait_recv()
        for copy in along:
            copy.wait_send()
        to_y.wait_send()
        to_x.wait_send()
        to_c.wait_send()
    own_cot.wait()
    cot_x.wait()
    tok_x.wait_send()
    tok_core.wait()

    @pl.when(first)
    def _():
        short_x.wait_send()

    @pl.when(core == 0)
    def _():
        short_core.wait_send()

    @pl.when(core == 1)
    def _():
        short_core.wait_recv()


def gather(shards, tok, cot, dp_count):
    z_count = dp_count // 2
    rows, width = tok.shape[1:]
    piece = 128 * 1024
    count = len(weight_chunks(shards, shards, piece))
    dma = pltpu.SemaphoreType.DMA
    return pl.pallas_call(
        functools.partial(gather_kernel, z_count, piece),
        out_shape=[jax.ShapeDtypeStruct((z_count, 2, *shard.shape), BF16) for shard in shards]
        + [
            jax.ShapeDtypeStruct((2, 2, rows, width), BF16),
            jax.ShapeDtypeStruct((rows, width), BF16),
            jax.ShapeDtypeStruct((2, rows, width), BF16),
        ],
        in_specs=[ANY] * 6,
        out_specs=[ANY] * 7,
        scratch_shapes=[
            dma((count, z_count - 1)),
            dma((count, z_count - 1)),
            dma((count, 3)),
            dma((count, 3)),
            dma((count,)),
            dma((5,)),
            dma((5,)),
            dma((3,)),
        ],
        compiler_params=params(48, collective_id=0, has_side_effects=True),
        name="gather",
    )(*shards, tok, cot)


def lane_row(pick):
    lane = lax.broadcasted_iota(jnp.int32, (1, LANES), 1)
    return jnp.where(pick(lane), 1.0, 0.0).astype(F32)


def head_lanes(half):
    return lane_row(lambda lane: (lane >= half * HEAD_DIM) & (lane < (half + 1) * HEAD_DIM))


def spare_lane(half, index):
    return (1 - half) * HEAD_DIM + index


def spare(half, index):
    return lane_row(lambda lane: lane == spare_lane(half, index))


def split_three(value):
    high = value.astype(BF16).astype(F32)
    rest = value - high
    middle = rest.astype(BF16).astype(F32)
    return high, middle, rest - middle


def mask_column(length, keys):
    return jnp.where(lax.broadcasted_iota(jnp.int32, (keys, 1), 0) < length, 0.0, -1000000000.0)


def forward_kernel(
    tile, lens_ref, tok_all, tok_own, tok_short, w_q, w_k, w_v, bias, q_out, k_out, v_out, o_out, q_tmp
):
    core = lax.axis_index("head") % 2
    length = lens_ref[2 - lax.axis_index("head") // 2]
    width = tok_own.shape[1]
    long_keys = 4 * tile
    wq, wk, wv = (w[...].reshape(width, w.shape[-1]) for w in (w_q, w_k, w_v))
    q_bias, v_bias = bias[0:1, :], bias[1:2, :]

    def project_kv(rows, at):
        at = pl.ds(at, tile)
        k_out[at, :] = mm(rows, wk).astype(BF16)
        v_out[at, :] = (mm(rows, wv) + v_bias).astype(BF16)

    for block in range(4):
        project_kv(tok_all[block // 2, block % 2], block * tile)
    project_kv(tok_short[...], long_keys)
    for block in range(3):
        rows = tok_own[...] if block == 2 else tok_all[block, core]
        query = (mm(rows, wq) + q_bias).astype(BF16).astype(F32) * (1.0 / math.sqrt(HEAD_DIM))
        q_tmp[pl.ds(block * tile, tile), :] = query.astype(BF16)

    masked = mask_column(length, long_keys)
    for pair in range(w_q.shape[-1] // LANES):
        columns = pl.ds(pair * LANES, LANES)
        for block in range(3):
            q_rows = pl.ds(block * tile, tile)
            k_rows = pl.ds(long_keys, tile) if block == 2 else pl.ds(0, long_keys)
            outs = []
            for half in range(2):
                mine = head_lanes(half)
                key = k_out[k_rows, columns].astype(F32) * mine
                if block < 2:
                    key = key + masked * spare(half, 0)
                value = (v_out[k_rows, columns].astype(F32) * mine + (1.0 - mine)).astype(BF16)
                query = q_tmp[q_rows, columns].astype(F32) * mine
                scores = mm_nt((query + spare(half, 0)).astype(BF16), key.astype(BF16))
                highest = jnp.max(scores, axis=-1, keepdims=True)
                raised = jnp.exp(scores - highest).astype(BF16)
                summed = mm(raised, value)
                outs.append(summed / pltpu.roll(summed, HEAD_DIM, 1))
                column = spare_lane(half, 0)
                log_total = highest + jnp.log(summed[:, column : column + 1])
                high, middle, low = split_three(-log_total)
                query = (
                    query
                    + high * spare(half, 0)
                    + middle * spare(half, 1)
                    + low * spare(half, 2)
                    + spare(half, 3)
                )
                q_out[2 * pair + half, q_rows, :] = query.astype(BF16)
            o_out[q_rows, columns] = jnp.where(head_lanes(0) > 0, outs[0], outs[1]).astype(BF16)


def attention_forward(lens, tok_all, tok_own, tok_short, qkv_full, qv_bias):
    tile, width = tok_own.shape
    quad = 4 * HEAD_DIM
    steps = width // quad
    depth = qkv_full.shape[2]
    lead = qkv_full.shape[:2]

    def fixed(shape):
        return pl.BlockSpec(shape, lambda i, lens: (0,) * len(shape), pipeline_mode=pl.Buffered(1))

    def weight(offset):
        return pl.BlockSpec((*lead, depth, quad), lambda i, lens: (0, 0, 0, offset + i))

    def columns(rows):
        return pl.BlockSpec((rows, quad), lambda i, lens: (0, i))

    return pl.pallas_call(
        functools.partial(forward_kernel, tile),
        out_shape=[
            jax.ShapeDtypeStruct((width // HEAD_DIM, 3 * tile, LANES), BF16),
            jax.ShapeDtypeStruct((5 * tile, width), BF16),
            jax.ShapeDtypeStruct((5 * tile, width), BF16),
            jax.ShapeDtypeStruct((3 * tile, width), BF16),
        ],
        grid_spec=pltpu.PrefetchScalarGridSpec(
            num_scalar_prefetch=1,
            grid=(steps,),
            in_specs=[
                fixed(tok_all.shape),
                fixed(tok_own.shape),
                fixed(tok_short.shape),
                weight(0),
                weight(steps),
                weight(2 * steps),
                columns(2),
            ],
            out_specs=[
                pl.BlockSpec((4, 3 * tile, LANES), lambda i, lens: (i, 0, 0)),
                columns(5 * tile),
                columns(5 * tile),
                columns(3 * tile),
            ],
            scratch_shapes=[pltpu.VMEM((3 * tile, quad), BF16)],
        ),
        compiler_params=params(56),
        name="attention_forward",
    )(lens, tok_all, tok_own, tok_short, qkv_full, qkv_full, qkv_full, qv_bias)


def row_mean(value):
    return jnp.mean(value, axis=-1, keepdims=True)


def middle_kernel(
    tile,
    chunk,
    o_ref,
    tok_all,
    tok_own,
    cot_pair,
    cot_own,
    wo_hbm,
    w1_hbm,
    w2_hbm,
    vectors,
    b1_ref,
    out_ref,
    gres_ref,
    gatt_ref,
    sums_ref,
    sums1_ref,
    wo,
    w1,
    w2,
    norm1,
    spread1,
    acc,
    slope,
    low,
    gtwo,
    sems,
):
    core = lax.axis_index("head") % 2
    width = o_ref.shape[1]
    hidden = b1_ref.shape[1]
    row_tiles = 3
    bo, g1, s1, b2, g2, s2 = (vectors[i : i + 1, :] for i in range(6))
    copies = [pltpu.make_async_copy(wo_hbm, wo, sems.at[0]), pltpu.make_async_copy(w1_hbm, w1, sems.at[1])]
    copies.append(pltpu.make_async_copy(w2_hbm, w2, sems.at[2]))
    for copy in copies:
        copy.start()
    copies[0].wait()
    for block in range(row_tiles):
        rows = pl.ds(block * tile, tile)
        token = tok_own[...] if block == 2 else tok_all[block, core]
        branch = mm(o_ref[rows, :], wo[...].reshape(width, width)) + bo
        value = token.astype(F32) + branch
        centre = value - row_mean(value)
        rstd = lax.rsqrt(row_mean(centre * centre) + epsilon)
        normal = centre * rstd
        norm1[rows, :] = normal
        spread1[rows, :] = jnp.broadcast_to(rstd, (tile, LANES))
        low[rows, :] = (normal * g1 + s1).astype(BF16)
        acc[rows, :] = jnp.zeros((tile, width), F32)
    copies[1].wait()
    copies[2].wait()

    def w1_piece(index):
        return w1[:, :, :, pl.ds(pl.multiple_of(index * chunk, chunk), chunk)].reshape(width, chunk)

    w2_rows = w2.shape[2]
    per = w2_rows // chunk

    def w2_piece(index):
        shard = index // per
        start = pl.multiple_of((index % per) * chunk, chunk)
        return w2[shard // 2, shard % 2, pl.ds(start, chunk), :]

    def up(index, _):
        span = pl.ds(pl.multiple_of(index * chunk, chunk), chunk)
        first, second = w1_piece(index), w2_piece(index)
        bias = b1_ref[:, span]
        for block in range(row_tiles):
            rows = pl.ds(block * tile, tile)
            value = mm(low[rows, :], first) + bias
            share = 0.5 * (1.0 + lax.erf(value * 0.7071067811865476))
            slope[rows, span] = (
                share + value * (0.3989422804014327 * jnp.exp(-0.5 * value * value))
            ).astype(BF16)
            acc[rows, :] += mm((value * share).astype(BF16), second)
        return 0

    lax.fori_loop(0, hidden // chunk, up, 0)
    totals = [jnp.zeros((1, width), F32)] * 4
    for block in range(row_tiles):
        rows = pl.ds(block * tile, tile)
        value = norm1[rows, :] * g1 + s1 + acc[rows, :] + b2
        centre = value - row_mean(value)
        rstd = lax.rsqrt(row_mean(centre * centre) + epsilon)
        normal = centre * rstd
        out_ref[block] = (normal * g2 + s2).astype(BF16)
        grad = (cot_own[...] if block == 2 else cot_pair[block]).astype(F32)
        upper = grad * g2
        result = rstd * (upper - row_mean(upper) - normal * row_mean(upper * normal))
        gtwo[rows, :] = result
        small = result.astype(BF16)
        low[rows, :] = small
        totals[0] = totals[0] + jnp.sum(grad, axis=0, keepdims=True)
        totals[1] = totals[1] + jnp.sum(small.astype(F32), axis=0, keepdims=True)
        acc[rows, :] = jnp.zeros((tile, width), F32)

    def down(index, _):
        span = pl.ds(pl.multiple_of(index * chunk, chunk), chunk)
        first, second = w1_piece(index), w2_piece(index)
        total = jnp.zeros((1, chunk), F32)
        for block in range(row_tiles):
            rows = pl.ds(block * tile, tile)
            grad = mm_nt(low[rows, :], second) * slope[rows, span].astype(F32)
            small = grad.astype(BF16)
            total = total + jnp.sum(small.astype(F32), axis=0, keepdims=True)
            acc[rows, :] += mm_nt(small, first)
        sums1_ref[:, span] = total
        return 0

    lax.fori_loop(0, hidden // chunk, down, 0)
    for block in range(row_tiles):
        rows = pl.ds(block * tile, tile)
        grad = acc[rows, :] + gtwo[rows, :]
        totals[2] = totals[2] + jnp.sum(grad, axis=0, keepdims=True)
        normal = norm1[rows, :]
        upper = grad * g1
        result = spread1[rows, 0:1] * (upper - row_mean(upper) - normal * row_mean(upper * normal))
        gres_ref[block] = result
        small = result.astype(BF16)
        totals[3] = totals[3] + jnp.sum(small.astype(F32), axis=0, keepdims=True)
        gatt_ref[rows, :] = mm_nt(small, wo[...].reshape(width, width)).astype(BF16)
    for number, total in enumerate(totals):
        sums_ref[number : number + 1, :] = total


def middle(attended, tok_all, tok_own, cot_pair, cot_own, weights, vectors, ffn_in_bias):
    rows, width = attended.shape
    tile = rows // 3
    hidden = ffn_in_bias.shape[-1]
    chunk = 512
    vmem = pl.BlockSpec(memory_space=pltpu.VMEM)
    out = jax.ShapeDtypeStruct
    return pl.pallas_call(
        functools.partial(middle_kernel, tile, chunk),
        out_shape=[
            out((3, tile, width), BF16),
            out((3, tile, width), F32),
            out((rows, width), BF16),
            out((4, width), F32),
            out((1, hidden), F32),
        ],
        in_specs=[vmem] * 5 + [ANY] * 3 + [vmem] * 2,
        out_specs=[vmem] * 5,
        scratch_shapes=[pltpu.VMEM(w.shape, BF16) for w in weights]
        + [
            pltpu.VMEM((rows, width), F32),
            pltpu.VMEM((rows, LANES), F32),
            pltpu.VMEM((rows, width), F32),
            pltpu.VMEM((rows, hidden), BF16),
            pltpu.VMEM((rows, width), BF16),
            pltpu.VMEM((rows, width), F32),
            pltpu.SemaphoreType.DMA((3,)),
        ],
        compiler_params=params(62),
        name="middle",
    )(attended, tok_all, tok_own, cot_pair, cot_own, *weights, vectors, ffn_in_bias.reshape(1, hidden))


def backward_kernel(tile, lens_ref, q_ref, k_ref, v_ref, o_ref, g_ref, dq_ref, dk_ref, dv_ref, sum_ref):
    length = lens_ref[2 - lax.axis_index("head") // 2]
    long_keys = 4 * tile
    masked = mask_column(length, long_keys)
    for pair in range(k_ref.shape[1] // LANES):
        columns = pl.ds(pair * LANES, LANES)
        for group in range(2):
            k_rows = pl.ds(long_keys, tile) if group else pl.ds(0, long_keys)
            blocks = [2] if group else [0, 1]
            key_pair = k_ref[k_rows, columns]
            key_turned = key_pair.astype(F32).T
            grad_keys, grad_values = [], []
            grad_queries = {block: [] for block in blocks}
            for half in range(2):
                mine = head_lanes(half)
                key = key_pair.astype(F32) * mine + spare(half, 0) + spare(half, 1) + spare(half, 2)
                if not group:
                    key = key + masked * spare(half, 3)
                key = key.astype(BF16)
                value = v_ref[k_rows, columns].astype(F32) * mine
                value = (value - (spare(half, 0) + spare(half, 1) + spare(half, 2))).astype(BF16)
                turned = key_turned[half * HEAD_DIM : (half + 1) * HEAD_DIM, :].astype(BF16)
                key_sum = value_sum = None
                for block in blocks:
                    q_rows = pl.ds(block * tile, tile)
                    query = q_ref[2 * pair + half, q_rows, :]
                    grad = g_ref[q_rows, columns].astype(F32) * mine
                    centre = jnp.sum(grad * o_ref[q_rows, columns].astype(F32), axis=-1, keepdims=True)
                    high, middle_part, low = split_three(centre)
                    grad = grad + high * spare(half, 0) + middle_part * spare(half, 1) + low * spare(half, 2)
                    grad = grad.astype(BF16)
                    probs = jnp.exp(mm_nt(key, query))
                    scores = (probs * mm_nt(value, grad)).astype(BF16)
                    key_part = mm(scores, query)
                    value_part = mm(probs.astype(BF16), grad)
                    key_sum = key_part if key_sum is None else key_sum + key_part
                    value_sum = value_part if value_sum is None else value_sum + value_part
                    grad_queries[block].append(mm(turned, scores))
                grad_keys.append(key_sum)
                grad_values.append(value_sum)
            low_half = head_lanes(0) > 0
            dk_ref[k_rows, columns] = jnp.where(low_half, grad_keys[0], grad_keys[1]).astype(BF16)
            grad_value = jnp.where(low_half, grad_values[0], grad_values[1])
            dv_ref[k_rows, columns] = grad_value.astype(BF16)
            value_total = jnp.sum(grad_value, axis=0, keepdims=True)
            query_total = jnp.zeros((1, LANES), F32)
            for block in blocks:
                grad_query = jnp.concatenate(grad_queries[block], axis=0).T * (1.0 / math.sqrt(HEAD_DIM))
                grad_query = grad_query.astype(BF16)
                dq_ref[pl.ds(block * tile, tile), columns] = grad_query
                query_total = query_total + jnp.sum(grad_query.astype(F32), axis=0, keepdims=True)
            if group:
                sum_ref[0:1, columns] += query_total
                sum_ref[1:2, columns] += value_total
            else:
                sum_ref[0:1, columns] = query_total
                sum_ref[1:2, columns] = value_total


def attention_backward(lens, queries, keys, values, attended, grad_attended):
    rows, width = attended.shape
    tile = rows // 3
    quad = 4 * HEAD_DIM

    def columns(count):
        return pl.BlockSpec((count, quad), lambda i, lens: (0, i))

    out = jax.ShapeDtypeStruct
    return pl.pallas_call(
        functools.partial(backward_kernel, tile),
        out_shape=[
            out((rows, width), BF16),
            out((5 * tile, width), BF16),
            out((5 * tile, width), BF16),
            out((2, width), F32),
        ],
        grid_spec=pltpu.PrefetchScalarGridSpec(
            num_scalar_prefetch=1,
            grid=(width // quad,),
            in_specs=[
                pl.BlockSpec((4, rows, LANES), lambda i, lens: (i, 0, 0)),
                columns(5 * tile),
                columns(5 * tile),
                columns(rows),
                columns(rows),
            ],
            out_specs=[columns(rows), columns(5 * tile), columns(5 * tile), columns(2)],
        ),
        compiler_params=params(56),
        name="attention_backward",
    )(lens, queries, keys, values, attended, grad_attended)


def finish_kernel(
    z_count,
    tile,
    wqkv,
    dq,
    dk,
    dv,
    gres,
    sums_mid,
    sums_hidden,
    sums_qv,
    out_rows,
    grad_out,
    layer_out,
    sums_out,
    pair_recv,
    short_recv,
    short_send,
    home_send,
    part,
    part_recv,
    part_z,
    k_send,
    k_recv,
    s_send,
    s_recv,
    o_send,
    o_recv,
    r_send,
    r_recv,
    local,
):
    place = Place(z_count)
    x, core, z = place.x, place.core, place.z
    width = dq.shape[-1]
    keep = 2 - x
    meet(place)
    kinds = (dk, dv)

    def to_sibling(kind, block):
        return push(
            kinds[kind].at[2 * block + 1 - core],
            pair_recv.at[kind, block],
            k_send.at[kind, block],
            k_recv.at[kind, block],
            place.other_core(),
        )

    pair = {
        (kind, turn): to_sibling(kind, 1 - x if turn == 0 else x) for turn in range(2) for kind in range(2)
    }
    for copy in pair.values():
        copy.start()
    short_core = [
        push(kinds[kind].at[4], short_recv.at[0, kind], s_send.at[0, kind], s_recv.at[0, kind], place.other_core())
        for kind in range(2)
    ]
    short_x = [
        push(short_send.at[kind], short_recv.at[1, kind], s_send.at[1, kind], s_recv.at[1, kind], place.other_x())
        for kind in range(2)
    ]

    @pl.when(core == 1)
    def _():
        for copy in short_core:
            copy.start()

    layer_home = push(out_rows.at[1 - x], layer_out.at[keep], o_send.at[0], o_recv.at[0], place.other_x())
    layer_own = [
        pltpu.make_async_copy(out_rows.at[x], layer_out.at[keep], local.at[0]),
        pltpu.make_async_copy(out_rows.at[2], layer_out.at[0], local.at[1]),
    ]

    part[0] = jnp.zeros(part.shape[1:], F32)
    part[0, 0:2, :] = sums_qv[...]
    part[0, 2:3, :] = sums_mid[3:4, :]
    part[0, 3:4, :] = sums_mid[2:3, :]
    for i in range(4):
        part[0, 4 + i : 5 + i, :] = sums_hidden[:, i * width : (i + 1) * width]
    part[0, 8:9, :] = sums_mid[1:2, :]
    part[0, 9:10, :] = sums_mid[0:1, :]
    targets = (place.other_core(), place.other_x(), place.other_y())
    hops = [
        push(part.at[i], part_recv.at[i], r_send.at[i], r_recv.at[i], target) for i, target in enumerate(targets)
    ]
    hops_z = [
        push(part.at[3], part_z.at[z], r_send.at[2 + step], r_recv.at[2 + step], place.along_z(step))
        for step in range(1, z_count)
    ]

    def hop(i):
        hops[i].wait_recv()
        part[i + 1] = part[i] + part_recv[i]
        if i < 2:
            hops[i + 1].start()
        else:
            for copy in hops_z:
                copy.start()

    hops[0].start()

    @pl.when((x == 1) & (core == 0))
    def _():
        for kind in range(2):
            short_core[kind].wait_recv()
            total = kinds[kind][4].astype(F32) + short_recv[0, kind].astype(F32)
            short_send[kind] = total.astype(BF16)
            short_x[kind].start()

    weight = wqkv[...].reshape(width, 3 * width)
    wq, wk, wv = (weight[:, i * width : (i + 1) * width] for i in range(3))

    grad_home = push(home_send.at[0], grad_out.at[keep], o_send.at[1], o_recv.at[1], place.other_x())
    grad_own = [
        pltpu.make_async_copy(home_send.at[1], grad_out.at[keep], local.at[2]),
        pltpu.make_async_copy(home_send.at[2], grad_out.at[0], local.at[3]),
    ]

    def with_pair(turn):
        block = 1 - x if turn == 0 else x
        grad = gres[block] + mm_nt(dq[block], wq)
        totals = []
        for kind in range(2):
            pair[kind, turn].wait_recv()
            total = kinds[kind][2 * block + core].astype(F32) + pair_recv[kind, block].astype(F32)
            totals.append(total.astype(BF16))
        grad = grad + mm_nt(totals[0], wk) + mm_nt(totals[1], wv)
        home_send[turn] = grad.astype(BF16)

    hop(0)
    with_pair(0)
    grad_home.start()
    hop(1)
    layer_home.start()
    for copy in layer_own:
        copy.start()
    with_pair(1)
    grad_own[0].start()
    hop(2)
    grad = gres[2] + mm_nt(dq[2], wq)
    first = (x == 0) & (core == 0)

    @pl.when(jnp.logical_not(first))
    def _():
        home_send[2] = grad.astype(BF16)

    @pl.when(first)
    def _():
        more = grad
        for kind, part_weight in enumerate((wk, wv)):
            short_core[kind].wait_recv()
            short_x[kind].wait_recv()
            total = kinds[kind][4].astype(F32) + short_recv[0, kind].astype(F32)
            total = total + short_recv[1, kind].astype(F32)
            more = more + mm_nt(total.astype(BF16), part_weight)
        home_send[2] = more.astype(BF16)

    grad_own[1].start()
    part_z[z] = part[3]
    for copy in hops_z:
        copy.wait_recv()
    total = part_z[0]
    for i in range(1, z_count):
        total = total + part_z[i]
    sums_out[...] = total
    for copy in hops + hops_z:
        copy.wait_send()
    for copy in pair.values():
        copy.wait_send()

    @pl.when(core == 1)
    def _():
        for copy in short_core:
            copy.wait_send()

    @pl.when((x == 1) & (core == 0))
    def _():
        for copy in short_x:
            copy.wait_send()

    for copy in layer_own + grad_own:
        copy.wait()
    layer_home.wait()
    grad_home.wait()


def finish(qkv_full, dq, dk, dv, gres, sums, out_rows, dp_count):
    rows, width = dq.shape
    tile = rows // 3
    z_count = dp_count // 2
    vmem = pl.BlockSpec(memory_space=pltpu.VMEM)
    out, dma = jax.ShapeDtypeStruct, pltpu.SemaphoreType.DMA
    return pl.pallas_call(
        functools.partial(finish_kernel, z_count, tile),
        out_shape=[out((3, tile, width), BF16), out((3, tile, width), BF16), out((16, width), F32)],
        in_specs=[vmem] * 8 + [ANY],
        out_specs=[ANY, ANY, vmem],
        scratch_shapes=[
            pltpu.VMEM((2, 2, tile, width), BF16),
            pltpu.VMEM((2, 2, tile, width), BF16),
            pltpu.VMEM((2, tile, width), BF16),
            pltpu.VMEM((3, tile, width), BF16),
            pltpu.VMEM((4, 16, width), F32),
            pltpu.VMEM((3, 16, width), F32),
            pltpu.VMEM((z_count, 16, width), F32),
            dma((2, 2)),
            dma((2, 2)),
            dma((2, 2)),
            dma((2, 2)),
            dma((2,)),
            dma((2,)),
            dma((2 + z_count,)),
            dma((2 + z_count,)),
            dma((4,)),
        ],
        compiler_params=params(60, collective_id=1, has_side_effects=True),
        name="finish",
    )(
        qkv_full,
        dq.reshape(3, tile, width),
        dk.reshape(5, tile, width),
        dv.reshape(5, tile, width),
        gres,
        *sums,
        out_rows,
    )


def paired_chips(
    tokens,
    out_cotangent,
    lengths,
    qkv_weight,
    out_weight,
    ffn_in_weight,
    ffn_out_weight,
    qv_bias,
    out_bias,
    ln1_gain,
    ln1_bias,
    ffn_in_bias,
    ffn_out_bias,
    ln2_gain,
    ln2_bias,
    dp_count,
):
    width = tokens.shape[-1]
    hidden = ffn_in_bias.shape[0]
    perm, lens = order_of(lengths)
    tok, cot = permute_pair(perm, tokens, out_cotangent, False)
    shards = (qkv_weight, out_weight, ffn_in_weight, ffn_out_weight)
    qkv_full, wo_full, w1_full, w2_full, tok_all, tok_short, cot_pair = gather(shards, tok, cot, dp_count)
    tok_own, cot_own = tok[0], cot[0]
    queries, keys, values, attended = attention_forward(lens, tok_all, tok_own, tok_short, qkv_full, qv_bias)
    vectors = jnp.stack([out_bias, ln1_gain, ln1_bias, ffn_out_bias, ln2_gain, ln2_bias])
    out_rows, gres, grad_attended, sums_mid, sums_hidden = middle(
        attended, tok_all, tok_own, cot_pair, cot_own, (wo_full, w1_full, w2_full), vectors, ffn_in_bias
    )
    dq, dk, dv, sums_qv = attention_backward(lens, queries, keys, values, attended, grad_attended)
    grad_sorted, out_sorted, sums = finish(
        qkv_full, dq, dk, dv, gres, (sums_mid, sums_hidden, sums_qv), out_rows, dp_count
    )
    layer_output, grad_input = permute_pair(perm, out_sorted, grad_sorted, True)
    return (
        layer_output,
        grad_input,
        sums[0:2],
        sums[2],
        sums[3],
        sums[4 : 4 + hidden // width].reshape(hidden),
        sums[8],
        sums[9],
    )


def body_for(mesh):
    dp_count, head_count = mesh.shape["dp"], mesh.shape["head"]

    def body(*arrays):
        tokens = arrays[0]
        seqs, tile, width = tokens.shape
        fits = head_count == 4 and seqs == 3 and dp_count % 2 == 0 and width == 1024 and tile == 256
        if fits:
            return paired_chips(*arrays, dp_count)
        return on_device(*arrays)

    return body


def solution(mesh):
    return jax.shard_map(
        body_for(mesh),
        mesh=mesh,
        in_specs=(
            P("dp", "head", None),
            P("dp", "head", None),
            P("dp"),
            P("dp", None),
            P("dp", None),
            P("dp", None),
            P("dp", None),
            P(),
            P(),
            P(),
            P(),
            P(),
            P(),
            P(),
            P(),
        ),
        out_specs=(P("dp", "head", None), P("dp", "head", None), P(), P(), P(), P(), P(), P()),
        check_vma=False,
    )
```

```python
import functools
import math

import jax
import jax.numpy as jnp
from jax import lax
from jax.experimental import pallas as pl
from jax.experimental.pallas import tpu as pltpu
from jax.sharding import PartitionSpec as P

HEAD_DIM = 64


epsilon = 1e-12


def layer_norm(inputs, gain, shift):
    centre = inputs - jnp.mean(inputs, axis=-1, keepdims=True)
    spread = jnp.mean(centre * centre, axis=-1, keepdims=True)
    return centre * lax.rsqrt(spread + epsilon) * gain + shift


def gelu_exact(inputs):
    return 0.5 * inputs * (1.0 + jax.scipy.special.erf(inputs * 0.7071067811865476))


def back_product(grads, weight):
    return lax.dot_general(
        grads, weight, (((1,), (1,)), ((), ())), preferred_element_type=jnp.float32
    )


def on_device(
    tokens,
    out_cotangent,
    lengths,
    qkv_weight,
    out_weight,
    ffn_in_weight,
    ffn_out_weight,
    qv_bias,
    out_bias,
    ln1_gain,
    ln1_bias,
    ffn_in_bias,
    ffn_out_bias,
    ln2_gain,
    ln2_bias,
):
    seqs_here, tok_part, width = tokens.shape
    row_count = seqs_here * tok_part
    flat_rows = tokens.reshape(row_count, width)
    gathered = (
        lax.all_gather(qkv_weight, "dp", axis=0, tiled=True),
        lax.all_gather(out_weight, "dp", axis=0, tiled=True),
        lax.all_gather(ffn_in_weight, "dp", axis=0, tiled=True),
        lax.all_gather(ffn_out_weight, "dp", axis=0, tiled=True),
    )
    qkv_full, attn_full, first_full, second_full = gathered
    projected = jnp.dot(flat_rows, qkv_full, preferred_element_type=jnp.float32)
    tok_shape = (seqs_here, tok_part, width)
    queries = (projected[:, :width] + qv_bias[0]).astype(jnp.bfloat16).reshape(tok_shape)
    keys_tok = projected[:, width : 2 * width].astype(jnp.bfloat16).reshape(tok_shape)
    values_tok = (projected[:, 2 * width :] + qv_bias[1]).astype(jnp.bfloat16).reshape(tok_shape)
    head_q, head_k, head_v = (
        lax.all_to_all(queries, "head", split_axis=2, concat_axis=1, tiled=True),
        lax.all_to_all(keys_tok, "head", split_axis=2, concat_axis=1, tiled=True),
        lax.all_to_all(values_tok, "head", split_axis=2, concat_axis=1, tiled=True),
    )
    seq_len = head_q.shape[1]
    head_part = head_q.shape[2]
    local_heads = head_part // HEAD_DIM
    block_rows = min(512, seq_len)
    block_count = seq_len // block_rows
    score_scale = 1.0 / math.sqrt(HEAD_DIM)
    head_shape = (seqs_here, seq_len, local_heads, HEAD_DIM)
    query_heads = head_q.reshape(head_shape)
    key_heads = head_k.reshape(head_shape)
    value_heads = head_v.reshape(head_shape)
    key_index = lax.iota(jnp.int32, seq_len)

    def seq_forward(seq_items):
        query_seq, key_seq, value_seq, length = seq_items
        visible = key_index < length
        query_blocks = query_seq.reshape(block_count, block_rows, local_heads, HEAD_DIM)

        def block_forward(query_block):
            scores = (
                jnp.einsum("qhd,khd->hqk", query_block, key_seq, preferred_element_type=jnp.float32)
                * score_scale
            )
            scores = jnp.where(visible[None, None, :], scores, -1000000000.0)
            highest = jnp.max(scores, axis=-1, keepdims=True)
            raised = jnp.exp(scores - highest)
            totals = jnp.sum(raised, axis=-1, keepdims=True)
            attn_probs = (raised / totals).astype(jnp.bfloat16)
            attended = jnp.einsum(
                "hqk,khd->qhd", attn_probs, value_seq, preferred_element_type=jnp.float32
            )
            return (attended.astype(jnp.bfloat16), (highest + jnp.log(totals))[:, :, 0])

        attended, log_block = lax.map(block_forward, query_blocks)
        return (attended.reshape(seq_len, head_part), log_block)

    head_out, log_totals = lax.map(seq_forward, (query_heads, key_heads, value_heads, lengths))
    tok_attn = lax.all_to_all(head_out, "head", split_axis=1, concat_axis=2, tiled=True)
    branch = (
        jnp.dot(tok_attn.reshape(row_count, width), attn_full, preferred_element_type=jnp.float32)
        + out_bias
    )
    residual_one = flat_rows.astype(jnp.float32) + branch
    normed_one, norm_one_back = jax.vjp(
        lambda inputs: layer_norm(inputs, ln1_gain, ln1_bias), residual_one
    )
    hidden = (
        jnp.dot(normed_one.astype(jnp.bfloat16), first_full, preferred_element_type=jnp.float32)
        + ffn_in_bias
    )
    active, gelu_back = jax.vjp(gelu_exact, hidden)
    ffn_out = (
        jnp.dot(active.astype(jnp.bfloat16), second_full, preferred_element_type=jnp.float32)
        + ffn_out_bias
    )
    result, norm_two_back = jax.vjp(
        lambda inputs: layer_norm(inputs, ln2_gain, ln2_bias), normed_one + ffn_out
    )
    layer_output = result.astype(jnp.bfloat16).reshape(tok_shape)
    qkv_back, attn_back, first_back, second_back = (
        lax.all_gather(qkv_weight, "dp", axis=0, tiled=True),
        lax.all_gather(out_weight, "dp", axis=0, tiled=True),
        lax.all_gather(ffn_in_weight, "dp", axis=0, tiled=True),
        lax.all_gather(ffn_out_weight, "dp", axis=0, tiled=True),
    )
    grad_out = out_cotangent.reshape(row_count, width).astype(jnp.float32)
    grad_ln2_bias = jnp.sum(grad_out, axis=0)
    (grad_res_two,) = norm_two_back(grad_out)
    grad_ffn_out = grad_res_two.astype(jnp.bfloat16)
    grad_ffn_out_bias = jnp.sum(grad_ffn_out.astype(jnp.float32), axis=0)
    grad_active = back_product(grad_ffn_out, second_back)
    (grad_hidden,) = gelu_back(grad_active)
    grad_hidden = grad_hidden.astype(jnp.bfloat16)
    grad_ffn_in_bias = jnp.sum(grad_hidden.astype(jnp.float32), axis=0)
    grad_normed = back_product(grad_hidden, first_back) + grad_res_two
    grad_ln1_bias = jnp.sum(grad_normed, axis=0)
    (grad_res_one,) = norm_one_back(grad_normed)
    grad_branch = grad_res_one.astype(jnp.bfloat16)
    grad_out_bias = jnp.sum(grad_branch.astype(jnp.float32), axis=0)
    grad_attended = back_product(grad_branch, attn_back).astype(jnp.bfloat16).reshape(tok_shape)
    grad_heads = lax.all_to_all(
        grad_attended, "head", split_axis=2, concat_axis=1, tiled=True
    ).reshape(head_shape)

    def seq_backward(seq_items):
        query_seq, key_seq, value_seq, grad_seq, log_seq, length = seq_items
        visible = key_index < length
        query_blocks = query_seq.reshape(block_count, block_rows, local_heads, HEAD_DIM)
        grad_blocks = grad_seq.reshape(block_count, block_rows, local_heads, HEAD_DIM)

        def block_backward(carry, block_items):
            key_acc, value_acc = carry
            query_block, grad_block, log_block = block_items
            scores = (
                jnp.einsum("qhd,khd->hqk", query_block, key_seq, preferred_element_type=jnp.float32)
                * score_scale
            )
            scores = jnp.where(visible[None, None, :], scores, -1000000000.0)
            attn_probs = jnp.exp(scores - log_block[:, :, None])
            grad_probs = jnp.einsum(
                "qhd,khd->hqk", grad_block, value_seq, preferred_element_type=jnp.float32
            )
            centre = jnp.sum(attn_probs * grad_probs, axis=-1, keepdims=True)
            grad_scores = (attn_probs * (grad_probs - centre)).astype(jnp.bfloat16)
            grad_query = (
                jnp.einsum("hqk,khd->qhd", grad_scores, key_seq, preferred_element_type=jnp.float32)
                * score_scale
            )
            key_acc = key_acc + jnp.einsum(
                "hqk,qhd->khd", grad_scores, query_block, preferred_element_type=jnp.float32
            )
            value_acc = value_acc + jnp.einsum(
                "hqk,qhd->khd",
                attn_probs.astype(jnp.bfloat16),
                grad_block,
                preferred_element_type=jnp.float32,
            )
            return ((key_acc, value_acc), grad_query.astype(jnp.bfloat16))

        zero_acc = jnp.zeros((seq_len, local_heads, HEAD_DIM), jnp.float32)
        (key_acc, value_acc), grad_queries = lax.scan(
            block_backward, (zero_acc, zero_acc), (query_blocks, grad_blocks, log_seq)
        )
        return (
            grad_queries.reshape(seq_len, head_part),
            (key_acc * score_scale).astype(jnp.bfloat16).reshape(seq_len, head_part),
            value_acc.astype(jnp.bfloat16).reshape(seq_len, head_part),
        )

    grad_q_heads, grad_k_heads, grad_v_heads = lax.map(
        seq_backward, (query_heads, key_heads, value_heads, grad_heads, log_totals, lengths)
    )
    grad_q_tok, grad_k_tok, grad_v_tok = (
        lax.all_to_all(grad_q_heads, "head", split_axis=1, concat_axis=2, tiled=True),
        lax.all_to_all(grad_k_heads, "head", split_axis=1, concat_axis=2, tiled=True),
        lax.all_to_all(grad_v_heads, "head", split_axis=1, concat_axis=2, tiled=True),
    )
    grad_q_rows = grad_q_tok.reshape(row_count, width)
    grad_k_rows = grad_k_tok.reshape(row_count, width)
    grad_v_rows = grad_v_tok.reshape(row_count, width)
    grad_input = (
        grad_res_one
        + back_product(grad_q_rows, qkv_back[:, :width])
        + back_product(grad_k_rows, qkv_back[:, width : 2 * width])
        + back_product(grad_v_rows, qkv_back[:, 2 * width :])
    )
    grad_qv = jnp.stack(
        [
            jnp.sum(grad_q_rows.astype(jnp.float32), axis=0),
            jnp.sum(grad_v_rows.astype(jnp.float32), axis=0),
        ]
    )
    bias_totals = lax.psum(
        (grad_qv, grad_out_bias, grad_ln1_bias, grad_ffn_in_bias, grad_ffn_out_bias, grad_ln2_bias),
        ("dp", "head"),
    )
    return (
        layer_output,
        grad_input.astype(jnp.bfloat16).reshape(tok_shape),
        bias_totals[0],
        bias_totals[1],
        bias_totals[2],
        bias_totals[3],
        bias_totals[4],
        bias_totals[5],
    )


MESH_IDS = pl.DeviceIdType.MESH
BF16, F32 = jnp.bfloat16, jnp.float32
ANY = pl.BlockSpec(memory_space=pl.ANY)
LANES = 128
NT = (((1,), (1,)), ((), ()))


def mm(left, right):
    return jnp.dot(left, right, preferred_element_type=F32)


def mm_nt(left, right):
    return lax.dot_general(left, right, NT, preferred_element_type=F32)


def whole(shape, memory_space=pltpu.VMEM):
    return pl.BlockSpec(memory_space=memory_space)


def params(vmem, **more):
    return pltpu.CompilerParams(vmem_limit_bytes=vmem << 20, **more)


def order_of(lengths):
    count = lengths.shape[0]
    place = lax.iota(jnp.int32, count)
    before = (lengths[None, :] < lengths[:, None]) | (
        (lengths[None, :] == lengths[:, None]) & (place[None, :] < place[:, None])
    )
    rank = jnp.sum(before.astype(jnp.int32), axis=1)
    hit = rank[None, :] == place[:, None]
    perm = jnp.sum(jnp.where(hit, place[None, :], 0), axis=1)
    lens = jnp.sum(jnp.where(hit, lengths[None, :], 0), axis=1)
    return perm.astype(jnp.int32), lens.astype(jnp.int32)


def pair_copy_kernel(perm_ref, a_ref, b_ref, a_out, b_out):
    a_out[...] = a_ref[...]
    b_out[...] = b_ref[...]


def permute_pair(perm, first, second, scatter):
    count, rows, width = first.shape
    here = pl.BlockSpec((1, rows, width), lambda i, perm: (i, 0, 0))
    there = pl.BlockSpec((1, rows, width), lambda i, perm: (perm[i], 0, 0))
    ins, outs = (here, there) if scatter else (there, here)
    return pl.pallas_call(
        pair_copy_kernel,
        out_shape=[jax.ShapeDtypeStruct(first.shape, first.dtype)] * 2,
        grid_spec=pltpu.PrefetchScalarGridSpec(
            num_scalar_prefetch=1, grid=(count,), in_specs=[ins] * 2, out_specs=[outs] * 2
        ),
        name="unsort" if scatter else "sort",
    )(perm, first, second)


class Place:
    def __init__(self, z_count):
        self.dp, self.head = lax.axis_index("dp"), lax.axis_index("head")
        self.z, self.y = self.dp // 2, self.dp % 2
        self.x, self.core = self.head // 2, self.head % 2
        self.z_count = z_count

    def along_z(self, step):
        return (((self.z + step) % self.z_count) * 2 + self.y, self.head)

    def other_y(self):
        return (self.z * 2 + (1 - self.y), self.head)

    def other_x(self):
        return (self.dp, (1 - self.x) * 2 + self.core)

    def other_core(self):
        return (self.dp, self.x * 2 + (1 - self.core))

    def peers(self):
        steps = [self.along_z(step) for step in range(1, self.z_count)]
        return steps + [self.other_y(), self.other_x(), self.other_core()]


def meet(place):
    barrier = pltpu.get_barrier_semaphore()
    peers = place.peers()
    for peer in peers:
        pl.semaphore_signal(barrier, inc=1, device_id=peer, device_id_type=MESH_IDS)
    pl.semaphore_wait(barrier, len(peers))


def push(src, dst, send, recv, target):
    return pltpu.make_async_remote_copy(
        src_ref=src, dst_ref=dst, send_sem=send, recv_sem=recv, device_id=target, device_id_type=MESH_IDS
    )


class Gather:
    def __init__(self, place, chunks, sems):
        z_send, z_recv, h_send, h_recv, local = sems
        x, core, z, y = place.x, place.core, place.z, place.y
        self.plans = []
        for number, (shard, full, row, rows, col, cols) in enumerate(chunks):
            base = row + core * (rows // 2)
            role = pl.ds(pl.multiple_of(base + x * (rows // 8), 16), rows * 3 // 8)
            own = pl.ds(pl.multiple_of(base + x * (rows * 3 // 8), 16), rows // 8)
            half = pl.ds(pl.multiple_of(base, 16), rows // 2)
            span = pl.ds(col, cols)
            along = [
                push(
                    shard.at[role, span],
                    full.at[z, y, role, span],
                    z_send.at[number, step - 1],
                    z_recv.at[number, step - 1],
                    place.along_z(step),
                )
                for step in range(1, place.z_count)
            ]
            here = pltpu.make_async_copy(shard.at[role, span], full.at[z, y, role, span], local.at[number])
            hops = []
            for hop, (view, target) in enumerate(
                (
                    (full.at[:, y, role, span], place.other_y()),
                    (full.at[:, :, own, span], place.other_x()),
                    (full.at[:, :, half, span], place.other_core()),
                )
            ):
                hops.append(push(view, view, h_send.at[number, hop], h_recv.at[number, hop], target))
            self.plans.append((along, here, hops))
        self.count = len(self.plans)

    def step(self, step):
        if 0 <= step < self.count:
            along, here, _ = self.plans[step]
            for copy in along:
                copy.start()
            here.start()
        if 0 <= step - 1 < self.count:
            along, here, hops = self.plans[step - 1]
            for copy in along:
                copy.wait_recv()
            here.wait()
            hops[0].start()
        for hop in (1, 2):
            if 0 <= step - 1 - hop < self.count:
                hops = self.plans[step - 1 - hop][2]
                hops[hop - 1].wait_recv()
                hops[hop].start()

    def arrived(self, number):
        self.plans[number][2][2].wait_recv()

    def sent(self):
        for along, _, hops in self.plans:
            for copy in along + hops:
                copy.wait_send()


def lane_row(pick):
    lane = lax.broadcasted_iota(jnp.int32, (1, LANES), 1)
    return jnp.where(pick(lane), 1.0, 0.0).astype(F32)


def head_lanes(half):
    return lane_row(lambda lane: (lane >= half * HEAD_DIM) & (lane < (half + 1) * HEAD_DIM))


def spare_lane(half, index):
    return (1 - half) * HEAD_DIM + index


def spare(half, index):
    return lane_row(lambda lane: lane == spare_lane(half, index))


def split_three(value):
    high = value.astype(BF16).astype(F32)
    rest = value - high
    middle = rest.astype(BF16).astype(F32)
    return high, middle, rest - middle


def mask_column(length, keys):
    return jnp.where(lax.broadcasted_iota(jnp.int32, (keys, 1), 0) < length, 0.0, -1000000000.0)


def attend(tile, pair, block, masked, q_tmp, k_all, v_all, q_out, o_out):
    columns = pl.ds(pl.multiple_of(pair * LANES, LANES), LANES)
    long_keys = 4 * tile
    q_rows = pl.ds(block * tile, tile)
    k_rows = pl.ds(long_keys, tile) if block == 2 else pl.ds(0, long_keys)
    outs = []
    for half in range(2):
        mine = head_lanes(half)
        key = k_all[k_rows, columns].astype(F32) * mine
        if block < 2:
            key = key + masked * spare(half, 0)
        value = (v_all[k_rows, columns].astype(F32) * mine + (1.0 - mine)).astype(BF16)
        query = q_tmp[q_rows, columns].astype(F32) * mine
        scores = mm_nt((query + spare(half, 0)).astype(BF16), key.astype(BF16))
        highest = jnp.max(scores, axis=-1, keepdims=True)
        raised = jnp.exp(scores - highest).astype(BF16)
        summed = mm(raised, value)
        outs.append(summed / pltpu.roll(summed, HEAD_DIM, 1))
        column = spare_lane(half, 0)
        log_total = highest + jnp.log(summed[:, column : column + 1])
        high, middle, low = split_three(-log_total)
        query = query + high * spare(half, 0) + middle * spare(half, 1) + low * spare(half, 2) + spare(half, 3)
        q_out[2 * pair + half, q_rows, :] = query.astype(BF16)
    o_out[q_rows, columns] = jnp.where(head_lanes(0) > 0, outs[0], outs[1]).astype(BF16)


def row_mean(value):
    return jnp.mean(value, axis=-1, keepdims=True)


def normalise(value):
    centre = value - row_mean(value)
    rstd = lax.rsqrt(row_mean(centre * centre) + epsilon)
    return centre * rstd, rstd


def normalise_back(grad, normal, rstd):
    return rstd * (grad - row_mean(grad) - normal * row_mean(grad * normal))


def column_sum(value):
    return jnp.sum(value.astype(F32), axis=0, keepdims=True)


def main_kernel(z_count, tile, chunks_of, *refs):
    lens_ref, refs = refs[0], refs[1:]
    shards, (tok, cot, qv_bias, vectors, b1_ref), refs = refs[:4], refs[4:9], refs[9:]
    fulls, (q_hbm, k_hbm, v_hbm, o_hbm, layer_hbm, gres_hbm, gatt_hbm, sums_ref, sums1_ref), refs = (
        refs[:4],
        refs[4:13],
        refs[13:],
    )
    (tok_v, own_v, cot_v, big, wo, w1, w2, q_tmp, k_all, v_all, q_ext, att, norm1, spread1, acc, low, act), refs = (
        refs[:17],
        refs[17:],
    )
    sems, (t_send, t_recv, t_local, load, store) = refs[:5], refs[5:]
    place = Place(z_count)
    x, core = place.x, place.core
    width = att.shape[1]
    hidden = b1_ref.shape[1]
    keep, give = 2 - x, 1 + x
    length = lens_ref[keep]
    wqkv_hbm, wo_hbm, w1_hbm, w2_hbm = fulls
    meet(place)
    comm = Gather(place, chunks_of(shards, fulls), sems)
    comm.step(0)

    first = (x == 0) & (core == 0)
    tok_x = push(tok.at[give], tok_v.at[2 * x + core], t_send.at[0], t_recv.at[0], place.other_x())
    tok_core = [
        push(tok_v.at[2 * i + core], tok_v.at[2 * i + core], t_send.at[1 + i], t_recv.at[1 + i], place.other_core())
        for i in range(2)
    ]
    cot_x = push(cot.at[give], cot_v.at[x], t_send.at[3], t_recv.at[3], place.other_x())
    short_x = push(tok.at[0], tok_v.at[4], t_send.at[4], t_recv.at[4], place.other_x())
    short_core = push(tok_v.at[4], tok_v.at[4], t_send.at[5], t_recv.at[5], place.other_core())
    own = [
        pltpu.make_async_copy(tok.at[keep], tok_v.at[2 * x + core], t_local.at[0]),
        pltpu.make_async_copy(tok.at[0], own_v, t_local.at[1]),
        pltpu.make_async_copy(cot.at[keep], cot_v.at[x], t_local.at[2]),
        pltpu.make_async_copy(cot.at[0], cot_v.at[2], t_local.at[3]),
    ]
    short_own = pltpu.make_async_copy(tok.at[0], tok_v.at[4], t_local.at[4])
    tok_x.start()
    for copy in own:
        copy.start()

    @pl.when(first)
    def _():
        short_x.start()
        short_own.start()

    comm.step(1)
    own[0].wait()
    tok_x.wait_recv()
    for copy in tok_core:
        copy.start()

    @pl.when((x == 1) & (core == 0))
    def _():
        short_x.wait_recv()

    @pl.when(first)
    def _():
        short_own.wait()

    @pl.when(core == 0)
    def _():
        short_core.start()

    comm.step(2)
    cot_x.start()
    comm.step(3)

    def load_qkv(part):
        return [
            pltpu.make_async_copy(
                wqkv_hbm.at[i, :, :, pl.ds(part * width, width)],
                big.at[pl.ds(8 * part + 2 * i, 2)],
                load.at[4 * part + i],
            )
            for i in range(z_count)
        ]

    def load_all(copies):
        for copy in copies:
            copy.start()
        for copy in copies:
            copy.wait()

    def qkv_part(part):
        return big[8 * part : 8 * part + 8].reshape(width, width)

    def project(part, result, bias_row):
        bias = None if bias_row is None else qv_bias[bias_row : bias_row + 1, :]

        def one(block, _):
            value = mm(tok_v[block], qkv_part(part))
            if bias is not None:
                value = value + bias
            result[pl.ds(pl.multiple_of(block * tile, tile), tile), :] = value.astype(BF16)
            return 0

        lax.fori_loop(0, 5, one, 0)

    comm.arrived(0)
    load_all(load_qkv(1))
    for copy in tok_core:
        copy.wait_recv()

    @pl.when(core == 1)
    def _():
        short_core.wait_recv()

    project(1, k_all, None)
    comm.step(4)
    comm.arrived(1)
    load_all(load_qkv(2))
    project(2, v_all, 1)
    comm.step(5)
    comm.arrived(2)
    load_all(load_qkv(0))
    own[1].wait()
    scale = 1.0 / math.sqrt(HEAD_DIM)
    for block in range(3):
        rows = own_v[...] if block == 2 else tok_v[2 * block + core]
        query = (mm(rows, qkv_part(0)) + qv_bias[0:1, :]).astype(BF16).astype(F32) * scale
        q_tmp[block * tile : (block + 1) * tile, :] = query.astype(BF16)
    stores = [
        pltpu.make_async_copy(src, dst, store.at[i])
        for i, (src, dst) in enumerate(((k_all, k_hbm), (v_all, v_hbm), (q_ext, q_hbm), (att, o_hbm)))
    ]
    stores[0].start()
    stores[1].start()
    masked = mask_column(length, 4 * tile)
    when_pair = {1: 6, 4: 7, 7: 8}

    def pair_step(pair, _):
        for at, step in when_pair.items():

            @pl.when(pair == at)
            def _():
                comm.step(step)

        for block in range(3):
            attend(tile, pair, block, masked, q_tmp, k_all, v_all, q_ext, att)
        return 0

    lax.fori_loop(0, width // LANES, pair_step, 0)
    stores[2].start()
    stores[3].start()

    bo, g1, s1, b2, g2, s2 = (vectors[i : i + 1, :] for i in range(6))
    comm.step(9)
    comm.arrived(3)
    wo_load = pltpu.make_async_copy(wo_hbm, wo, load.at[12])
    load_all([wo_load])
    for block in range(3):
        rows = pl.ds(block * tile, tile)
        token = own_v[...] if block == 2 else tok_v[2 * block + core]
        branch = mm(att[rows, :], wo[...].reshape(width, width)) + bo
        normal, rstd = normalise(token.astype(F32) + branch)
        norm1[rows, :] = normal
        spread1[rows, :] = jnp.broadcast_to(rstd, (tile, LANES))
        low[rows, :] = (normal * g1 + s1).astype(BF16)
        acc[rows, :] = jnp.zeros((tile, width), F32)

    block_width = w2.shape[2]
    blocks = hidden // block_width
    per = width // block_width
    w1_loads = [
        pltpu.make_async_copy(
            w1_hbm.at[:, :, :, pl.ds(i * width, width)], w1.at[:, :, :, pl.ds(i * width, width)], load.at[13 + i]
        )
        for i in range(hidden // width)
    ]
    w2_loads = [
        pltpu.make_async_copy(
            w2_hbm.at[:, :, pl.ds(i * 128, 128), :], w2.at[:, :, pl.ds(i * 128, 128), :], load.at[17 + i]
        )
        for i in range(block_width // 128)
    ]

    def w1_piece(index):
        span = pl.ds(pl.multiple_of(index * block_width, block_width), block_width)
        return w1[:, :, :, span].reshape(width, block_width)

    def slope_at(index, block):
        start = (index // per) * (3 * tile // 128) + block * (tile // 128)
        columns = pl.ds(pl.multiple_of((index % per) * block_width, block_width), block_width)
        return pl.ds(start, tile // 128), columns

    def up(index, _):
        for i in range(hidden // width):

            @pl.when(index == i * per)
            def _():
                if i < 3:
                    comm.step(10 + i)
                comm.arrived(4 + i)
                load_all([w1_loads[i]])

        span = pl.ds(pl.multiple_of(index * block_width, block_width), block_width)
        first_piece = w1_piece(index)
        bias = b1_ref[:, span]
        for block in range(3):
            rows = pl.ds(block * tile, tile)
            value = mm(low[rows, :], first_piece) + bias
            share = 0.5 * (1.0 + lax.erf(value * 0.7071067811865476))
            slope = share + value * (0.3989422804014327 * jnp.exp(-0.5 * value * value))
            at, columns = slope_at(index, block)
            big[at, :, columns] = slope.astype(BF16).reshape(tile // 128, 128, block_width)
            active = (value * share).astype(BF16)
            for part in range(block_width // 128):
                at = pl.ds(pl.multiple_of(index * 128, 128), 128)
                act[part, rows, at] = active[:, part * 128 : (part + 1) * 128]
        return 0

    lax.fori_loop(0, blocks, up, 0)

    def widen(part, _):
        for i in range(block_width // 128):

            @pl.when(part == i)
            def _():
                comm.step(13 + i)
                comm.arrived(8 + i)
                load_all([w2_loads[i]])

        second = w2[:, :, pl.ds(pl.multiple_of(part * 128, 128), 128), :].reshape(width, width)
        for block in range(3):
            rows = pl.ds(block * tile, tile)
            acc[rows, :] += mm(act[part, rows, :], second)
        return 0

    lax.fori_loop(0, block_width // 128, widen, 0)

    stores[3].wait()
    for copy in own[2:]:
        copy.wait()
    cot_x.wait_recv()
    totals = [jnp.zeros((1, width), F32)] * 4
    for block in range(3):
        rows = pl.ds(block * tile, tile)
        normal, rstd = normalise(norm1[rows, :] * g1 + s1 + acc[rows, :] + b2)
        att[rows, :] = (normal * g2 + s2).astype(BF16)
        grad = cot_v[block].astype(F32)
        result = normalise_back(grad * g2, normal, rstd)
        acc[rows, :] = result
        small = result.astype(BF16)
        low[rows, :] = small
        totals[0] = totals[0] + column_sum(grad)
        totals[1] = totals[1] + column_sum(small)

    def att_rows(block):
        return att.at[pl.ds(pl.multiple_of(block * tile, tile), tile), :]

    layer_home = push(att_rows(1 - x), layer_hbm.at[keep], t_send.at[6], t_recv.at[6], place.other_x())
    layer_own = [
        pltpu.make_async_copy(att_rows(x), layer_hbm.at[keep], t_local.at[5]),
        pltpu.make_async_copy(att_rows(2), layer_hbm.at[0], t_local.at[6]),
    ]
    layer_home.start()
    for copy in layer_own:
        copy.start()

    def down(index, _):
        span = pl.ds(pl.multiple_of(index * block_width, block_width), block_width)
        first_piece, second = w1_piece(index), w2[index // 2, index % 2]
        total = jnp.zeros((1, block_width), F32)
        for block in range(3):
            rows = pl.ds(block * tile, tile)
            at, columns = slope_at(index, block)
            slope = big[at, :, columns].reshape(tile, block_width).astype(F32)
            small = (mm_nt(low[rows, :], second) * slope).astype(BF16)
            total = total + column_sum(small)
            acc[rows, :] += mm_nt(small, first_piece)
        sums1_ref[:, span] = total
        return 0

    lax.fori_loop(0, blocks, down, 0)
    stores[2].wait()
    for block in range(3):
        rows = pl.ds(block * tile, tile)
        grad = acc[rows, :]
        totals[2] = totals[2] + column_sum(grad)
        result = normalise_back(grad * g1, norm1[rows, :], spread1[rows, 0:1])
        acc[rows, :] = result
        small = result.astype(BF16)
        totals[3] = totals[3] + column_sum(small)
        q_tmp[rows, :] = mm_nt(small, wo[...].reshape(width, width)).astype(BF16)
    for number, total in enumerate(totals):
        sums_ref[number : number + 1, :] = total
    results = [
        pltpu.make_async_copy(acc, gres_hbm, store.at[4]),
        pltpu.make_async_copy(q_tmp, gatt_hbm, store.at[5]),
    ]
    for copy in results:
        copy.start()
    comm.sent()
    for copy in tok_core:
        copy.wait_send()
    tok_x.wait_send()
    cot_x.wait_send()

    @pl.when(first)
    def _():
        short_x.wait_send()

    @pl.when(core == 0)
    def _():
        short_core.wait_send()

    for copy in layer_own + stores[:2] + results:
        copy.wait()
    layer_home.wait()


def main(lens, shards, tok, cot, qv_bias, vectors, ffn_in_bias, dp_count):
    z_count = dp_count // 2
    tile, width = tok.shape[1:]
    rows = 3 * tile
    hidden = ffn_in_bias.shape[0]
    out, dma, vmem = jax.ShapeDtypeStruct, pltpu.SemaphoreType.DMA, pltpu.VMEM

    def chunks_of(shards, fulls):
        qkv, wo, w1, w2 = zip(shards, fulls)
        chunks = [(*qkv, 0, 128, part * width, width) for part in (1, 2, 0)]
        chunks.append((*wo, 0, 128, 0, width))
        chunks += [(*w1, 0, 128, col, width) for col in range(0, hidden, width)]
        chunks += [(*w2, row, 128, 0, width) for row in range(0, w2[0].shape[0], 128)]
        return chunks

    count = len(chunks_of(shards, shards))
    whole = pl.BlockSpec(memory_space=pltpu.VMEM)
    weights = [out((z_count, 2, *shard.shape), BF16) for shard in shards]
    return pl.pallas_call(
        functools.partial(main_kernel, z_count, tile, chunks_of),
        out_shape=weights
        + [
            out((width // HEAD_DIM, rows, LANES), BF16),
            out((5 * tile, width), BF16),
            out((5 * tile, width), BF16),
            out((rows, width), BF16),
            out((3, tile, width), BF16),
            out((rows, width), F32),
            out((rows, width), BF16),
            out((4, width), F32),
            out((1, hidden), F32),
        ],
        in_specs=[pl.BlockSpec(memory_space=pltpu.SMEM)] + [ANY] * 6 + [whole] * 3,
        out_specs=[ANY] * 11 + [whole] * 2,
        scratch_shapes=[
            vmem((5, tile, width), BF16),
            vmem((tile, width), BF16),
            vmem((3, tile, width), BF16),
            vmem((24, 128, width), BF16),
            vmem(weights[1].shape, BF16),
            vmem(weights[2].shape, BF16),
            vmem(weights[3].shape, BF16),
            vmem((rows, width), BF16),
            vmem((5 * tile, width), BF16),
            vmem((5 * tile, width), BF16),
            vmem((width // HEAD_DIM, rows, LANES), BF16),
            vmem((rows, width), BF16),
            vmem((rows, width), F32),
            vmem((rows, LANES), F32),
            vmem((rows, width), F32),
            vmem((rows, width), BF16),
            vmem((4, rows, width), BF16),
            dma((count, z_count - 1)),
            dma((count, z_count - 1)),
            dma((count, 3)),
            dma((count, 3)),
            dma((count,)),
            dma((7,)),
            dma((7,)),
            dma((7,)),
            dma((21,)),
            dma((6,)),
        ],
        compiler_params=params(63, collective_id=0, has_side_effects=True),
        name="main",
    )(lens, *shards, tok, cot, qv_bias, vectors, ffn_in_bias.reshape(1, hidden))


def backward_kernel(tile, lens_ref, q_ref, k_ref, v_ref, o_ref, g_ref, dq_ref, dk_ref, dv_ref, sum_ref):
    length = lens_ref[2 - lax.axis_index("head") // 2]
    long_keys = 4 * tile
    masked = mask_column(length, long_keys)
    for pair in range(k_ref.shape[1] // LANES):
        columns = pl.ds(pair * LANES, LANES)
        for group in range(2):
            k_rows = pl.ds(long_keys, tile) if group else pl.ds(0, long_keys)
            blocks = [2] if group else [0, 1]
            key_pair = k_ref[k_rows, columns]
            key_turned = key_pair.astype(F32).T
            grad_keys, grad_values = [], []
            grad_queries = {block: [] for block in blocks}
            for half in range(2):
                mine = head_lanes(half)
                key = key_pair.astype(F32) * mine + spare(half, 0) + spare(half, 1) + spare(half, 2)
                if not group:
                    key = key + masked * spare(half, 3)
                key = key.astype(BF16)
                value = v_ref[k_rows, columns].astype(F32) * mine
                value = (value - (spare(half, 0) + spare(half, 1) + spare(half, 2))).astype(BF16)
                turned = key_turned[half * HEAD_DIM : (half + 1) * HEAD_DIM, :].astype(BF16)
                key_sum = value_sum = None
                for block in blocks:
                    q_rows = pl.ds(block * tile, tile)
                    query = q_ref[2 * pair + half, q_rows, :]
                    grad = g_ref[q_rows, columns].astype(F32) * mine
                    centre = jnp.sum(grad * o_ref[q_rows, columns].astype(F32), axis=-1, keepdims=True)
                    high, middle_part, low = split_three(centre)
                    grad = grad + high * spare(half, 0) + middle_part * spare(half, 1) + low * spare(half, 2)
                    grad = grad.astype(BF16)
                    probs = jnp.exp(mm_nt(key, query))
                    scores = (probs * mm_nt(value, grad)).astype(BF16)
                    key_part = mm(scores, query)
                    value_part = mm(probs.astype(BF16), grad)
                    key_sum = key_part if key_sum is None else key_sum + key_part
                    value_sum = value_part if value_sum is None else value_sum + value_part
                    grad_queries[block].append(mm(turned, scores))
                grad_keys.append(key_sum)
                grad_values.append(value_sum)
            low_half = head_lanes(0) > 0
            dk_ref[k_rows, columns] = jnp.where(low_half, grad_keys[0], grad_keys[1]).astype(BF16)
            grad_value = jnp.where(low_half, grad_values[0], grad_values[1])
            dv_ref[k_rows, columns] = grad_value.astype(BF16)
            value_total = jnp.sum(grad_value, axis=0, keepdims=True)
            query_total = jnp.zeros((1, LANES), F32)
            for block in blocks:
                grad_query = jnp.concatenate(grad_queries[block], axis=0).T * (1.0 / math.sqrt(HEAD_DIM))
                grad_query = grad_query.astype(BF16)
                dq_ref[pl.ds(block * tile, tile), columns] = grad_query
                query_total = query_total + jnp.sum(grad_query.astype(F32), axis=0, keepdims=True)
            if group:
                sum_ref[0:1, columns] += query_total
                sum_ref[1:2, columns] += value_total
            else:
                sum_ref[0:1, columns] = query_total
                sum_ref[1:2, columns] = value_total


def attention_backward(lens, queries, keys, values, attended, grad_attended):
    rows, width = attended.shape
    tile = rows // 3
    quad = 4 * HEAD_DIM

    def columns(count):
        return pl.BlockSpec((count, quad), lambda i, lens: (0, i))

    out = jax.ShapeDtypeStruct
    return pl.pallas_call(
        functools.partial(backward_kernel, tile),
        out_shape=[
            out((rows, width), BF16),
            out((5 * tile, width), BF16),
            out((5 * tile, width), BF16),
            out((2, width), F32),
        ],
        grid_spec=pltpu.PrefetchScalarGridSpec(
            num_scalar_prefetch=1,
            grid=(width // quad,),
            in_specs=[
                pl.BlockSpec((4, rows, LANES), lambda i, lens: (i, 0, 0)),
                columns(5 * tile),
                columns(5 * tile),
                columns(rows),
                columns(rows),
            ],
            out_specs=[columns(rows), columns(5 * tile), columns(5 * tile), columns(2)],
        ),
        compiler_params=params(56),
        name="attention_backward",
    )(lens, queries, keys, values, attended, grad_attended)


def finish_kernel(
    z_count,
    tile,
    wqkv,
    dq,
    dk,
    dv,
    gres,
    sums_mid,
    sums_hidden,
    sums_qv,
    grad_out,
    sums_out,
    pair_recv,
    short_recv,
    short_send,
    home_send,
    part,
    part_recv,
    part_z,
    k_send,
    k_recv,
    s_send,
    s_recv,
    o_send,
    o_recv,
    r_send,
    r_recv,
    local,
):
    place = Place(z_count)
    x, core, z = place.x, place.core, place.z
    width = dq.shape[-1]
    keep = 2 - x
    meet(place)
    kinds = (dk, dv)

    def to_sibling(kind, block):
        return push(
            kinds[kind].at[2 * block + 1 - core],
            pair_recv.at[kind, block],
            k_send.at[kind, block],
            k_recv.at[kind, block],
            place.other_core(),
        )

    pair = {
        (kind, turn): to_sibling(kind, 1 - x if turn == 0 else x) for turn in range(2) for kind in range(2)
    }
    for copy in pair.values():
        copy.start()
    short_core = [
        push(kinds[kind].at[4], short_recv.at[0, kind], s_send.at[0, kind], s_recv.at[0, kind], place.other_core())
        for kind in range(2)
    ]
    short_x = [
        push(short_send.at[kind], short_recv.at[1, kind], s_send.at[1, kind], s_recv.at[1, kind], place.other_x())
        for kind in range(2)
    ]

    @pl.when(core == 1)
    def _():
        for copy in short_core:
            copy.start()

    part[0] = jnp.zeros(part.shape[1:], F32)
    part[0, 0:2, :] = sums_qv[...]
    part[0, 2:3, :] = sums_mid[3:4, :]
    part[0, 3:4, :] = sums_mid[2:3, :]
    for i in range(4):
        part[0, 4 + i : 5 + i, :] = sums_hidden[:, i * width : (i + 1) * width]
    part[0, 8:9, :] = sums_mid[1:2, :]
    part[0, 9:10, :] = sums_mid[0:1, :]
    targets = (place.other_core(), place.other_x(), place.other_y())
    hops = [
        push(part.at[i], part_recv.at[i], r_send.at[i], r_recv.at[i], target) for i, target in enumerate(targets)
    ]
    hops_z = [
        push(part.at[3], part_z.at[z], r_send.at[2 + step], r_recv.at[2 + step], place.along_z(step))
        for step in range(1, z_count)
    ]

    def hop(i):
        hops[i].wait_recv()
        part[i + 1] = part[i] + part_recv[i]
        if i < 2:
            hops[i + 1].start()
        else:
            for copy in hops_z:
                copy.start()

    hops[0].start()

    @pl.when((x == 1) & (core == 0))
    def _():
        for kind in range(2):
            short_core[kind].wait_recv()
            total = kinds[kind][4].astype(F32) + short_recv[0, kind].astype(F32)
            short_send[kind] = total.astype(BF16)
            short_x[kind].start()

    weight = wqkv[...].reshape(width, 3 * width)
    wq, wk, wv = (weight[:, i * width : (i + 1) * width] for i in range(3))

    grad_home = push(home_send.at[0], grad_out.at[keep], o_send.at[0], o_recv.at[0], place.other_x())
    grad_own = [
        pltpu.make_async_copy(home_send.at[1], grad_out.at[keep], local.at[0]),
        pltpu.make_async_copy(home_send.at[2], grad_out.at[0], local.at[1]),
    ]

    def with_pair(turn):
        block = 1 - x if turn == 0 else x
        grad = gres[block] + mm_nt(dq[block], wq)
        totals = []
        for kind in range(2):
            pair[kind, turn].wait_recv()
            total = kinds[kind][2 * block + core].astype(F32) + pair_recv[kind, block].astype(F32)
            totals.append(total.astype(BF16))
        grad = grad + mm_nt(totals[0], wk) + mm_nt(totals[1], wv)
        home_send[turn] = grad.astype(BF16)

    hop(0)
    with_pair(0)
    grad_home.start()
    hop(1)
    with_pair(1)
    grad_own[0].start()
    hop(2)
    grad = gres[2] + mm_nt(dq[2], wq)
    first = (x == 0) & (core == 0)

    @pl.when(jnp.logical_not(first))
    def _():
        home_send[2] = grad.astype(BF16)

    @pl.when(first)
    def _():
        more = grad
        for kind, part_weight in enumerate((wk, wv)):
            short_core[kind].wait_recv()
            short_x[kind].wait_recv()
            total = kinds[kind][4].astype(F32) + short_recv[0, kind].astype(F32)
            total = total + short_recv[1, kind].astype(F32)
            more = more + mm_nt(total.astype(BF16), part_weight)
        home_send[2] = more.astype(BF16)

    grad_own[1].start()
    part_z[z] = part[3]
    for copy in hops_z:
        copy.wait_recv()
    total = part_z[0]
    for i in range(1, z_count):
        total = total + part_z[i]
    sums_out[...] = total
    for copy in hops + hops_z:
        copy.wait_send()
    for copy in pair.values():
        copy.wait_send()

    @pl.when(core == 1)
    def _():
        for copy in short_core:
            copy.wait_send()

    @pl.when((x == 1) & (core == 0))
    def _():
        for copy in short_x:
            copy.wait_send()

    for copy in grad_own:
        copy.wait()
    grad_home.wait()


def finish(qkv_full, dq, dk, dv, gres, sums, dp_count):
    rows, width = dq.shape
    tile = rows // 3
    z_count = dp_count // 2
    vmem = pl.BlockSpec(memory_space=pltpu.VMEM)
    out, dma = jax.ShapeDtypeStruct, pltpu.SemaphoreType.DMA
    return pl.pallas_call(
        functools.partial(finish_kernel, z_count, tile),
        out_shape=[out((3, tile, width), BF16), out((16, width), F32)],
        in_specs=[vmem] * 8,
        out_specs=[ANY, vmem],
        scratch_shapes=[
            pltpu.VMEM((2, 2, tile, width), BF16),
            pltpu.VMEM((2, 2, tile, width), BF16),
            pltpu.VMEM((2, tile, width), BF16),
            pltpu.VMEM((3, tile, width), BF16),
            pltpu.VMEM((4, 16, width), F32),
            pltpu.VMEM((3, 16, width), F32),
            pltpu.VMEM((z_count, 16, width), F32),
            dma((2, 2)),
            dma((2, 2)),
            dma((2, 2)),
            dma((2, 2)),
            dma((1,)),
            dma((1,)),
            dma((2 + z_count,)),
            dma((2 + z_count,)),
            dma((2,)),
        ],
        compiler_params=params(60, collective_id=1, has_side_effects=True),
        name="finish",
    )(
        qkv_full,
        dq.reshape(3, tile, width),
        dk.reshape(5, tile, width),
        dv.reshape(5, tile, width),
        gres.reshape(3, tile, width),
        *sums,
    )


def paired_chips(
    tokens,
    out_cotangent,
    lengths,
    qkv_weight,
    out_weight,
    ffn_in_weight,
    ffn_out_weight,
    qv_bias,
    out_bias,
    ln1_gain,
    ln1_bias,
    ffn_in_bias,
    ffn_out_bias,
    ln2_gain,
    ln2_bias,
    dp_count,
):
    width = tokens.shape[-1]
    hidden = ffn_in_bias.shape[0]
    perm, lens = order_of(lengths)
    tok, cot = permute_pair(perm, tokens, out_cotangent, False)
    shards = (qkv_weight, out_weight, ffn_in_weight, ffn_out_weight)
    vectors = jnp.stack([out_bias, ln1_gain, ln1_bias, ffn_out_bias, ln2_gain, ln2_bias])
    results = main(lens, shards, tok, cot, qv_bias, vectors, ffn_in_bias, dp_count)
    qkv_full = results[0]
    queries, keys, values, attended, out_sorted, gres, grad_attended, sums_mid, sums_hidden = results[4:]
    dq, dk, dv, sums_qv = attention_backward(lens, queries, keys, values, attended, grad_attended)
    grad_sorted, sums = finish(qkv_full, dq, dk, dv, gres, (sums_mid, sums_hidden, sums_qv), dp_count)
    layer_output, grad_input = permute_pair(perm, out_sorted, grad_sorted, True)
    return (
        layer_output,
        grad_input,
        sums[0:2],
        sums[2],
        sums[3],
        sums[4 : 4 + hidden // width].reshape(hidden),
        sums[8],
        sums[9],
    )


def body_for(mesh):
    dp_count, head_count = mesh.shape["dp"], mesh.shape["head"]

    def body(*arrays):
        tokens = arrays[0]
        seqs, tile, width = tokens.shape
        fits = head_count == 4 and seqs == 3 and dp_count % 2 == 0 and width == 1024 and tile == 256
        if fits:
            return paired_chips(*arrays, dp_count)
        return on_device(*arrays)

    return body


def solution(mesh):
    return jax.shard_map(
        body_for(mesh),
        mesh=mesh,
        in_specs=(
            P("dp", "head", None),
            P("dp", "head", None),
            P("dp"),
            P("dp", None),
            P("dp", None),
            P("dp", None),
            P("dp", None),
            P(),
            P(),
            P(),
            P(),
            P(),
            P(),
            P(),
            P(),
        ),
        out_specs=(P("dp", "head", None), P("dp", "head", None), P(), P(), P(), P(), P(), P()),
        check_vma=False,
    )
```

```python
import functools
import math

import jax
import jax.numpy as jnp
from jax import lax
from jax.experimental import pallas as pl
from jax.experimental.pallas import tpu as pltpu
from jax.sharding import PartitionSpec as P

HEAD_DIM = 64


epsilon = 1e-12


def layer_norm(inputs, gain, shift):
    centre = inputs - jnp.mean(inputs, axis=-1, keepdims=True)
    spread = jnp.mean(centre * centre, axis=-1, keepdims=True)
    return centre * lax.rsqrt(spread + epsilon) * gain + shift


def gelu_exact(inputs):
    return 0.5 * inputs * (1.0 + jax.scipy.special.erf(inputs * 0.7071067811865476))


def back_product(grads, weight):
    return lax.dot_general(
        grads, weight, (((1,), (1,)), ((), ())), preferred_element_type=jnp.float32
    )


def on_device(
    tokens,
    out_cotangent,
    lengths,
    qkv_weight,
    out_weight,
    ffn_in_weight,
    ffn_out_weight,
    qv_bias,
    out_bias,
    ln1_gain,
    ln1_bias,
    ffn_in_bias,
    ffn_out_bias,
    ln2_gain,
    ln2_bias,
):
    seqs_here, tok_part, width = tokens.shape
    row_count = seqs_here * tok_part
    flat_rows = tokens.reshape(row_count, width)
    gathered = (
        lax.all_gather(qkv_weight, "dp", axis=0, tiled=True),
        lax.all_gather(out_weight, "dp", axis=0, tiled=True),
        lax.all_gather(ffn_in_weight, "dp", axis=0, tiled=True),
        lax.all_gather(ffn_out_weight, "dp", axis=0, tiled=True),
    )
    qkv_full, attn_full, first_full, second_full = gathered
    projected = jnp.dot(flat_rows, qkv_full, preferred_element_type=jnp.float32)
    tok_shape = (seqs_here, tok_part, width)
    queries = (projected[:, :width] + qv_bias[0]).astype(jnp.bfloat16).reshape(tok_shape)
    keys_tok = projected[:, width : 2 * width].astype(jnp.bfloat16).reshape(tok_shape)
    values_tok = (projected[:, 2 * width :] + qv_bias[1]).astype(jnp.bfloat16).reshape(tok_shape)
    head_q, head_k, head_v = (
        lax.all_to_all(queries, "head", split_axis=2, concat_axis=1, tiled=True),
        lax.all_to_all(keys_tok, "head", split_axis=2, concat_axis=1, tiled=True),
        lax.all_to_all(values_tok, "head", split_axis=2, concat_axis=1, tiled=True),
    )
    seq_len = head_q.shape[1]
    head_part = head_q.shape[2]
    local_heads = head_part // HEAD_DIM
    block_rows = min(512, seq_len)
    block_count = seq_len // block_rows
    score_scale = 1.0 / math.sqrt(HEAD_DIM)
    head_shape = (seqs_here, seq_len, local_heads, HEAD_DIM)
    query_heads = head_q.reshape(head_shape)
    key_heads = head_k.reshape(head_shape)
    value_heads = head_v.reshape(head_shape)
    key_index = lax.iota(jnp.int32, seq_len)

    def seq_forward(seq_items):
        query_seq, key_seq, value_seq, length = seq_items
        visible = key_index < length
        query_blocks = query_seq.reshape(block_count, block_rows, local_heads, HEAD_DIM)

        def block_forward(query_block):
            scores = (
                jnp.einsum("qhd,khd->hqk", query_block, key_seq, preferred_element_type=jnp.float32)
                * score_scale
            )
            scores = jnp.where(visible[None, None, :], scores, -1000000000.0)
            highest = jnp.max(scores, axis=-1, keepdims=True)
            raised = jnp.exp(scores - highest)
            totals = jnp.sum(raised, axis=-1, keepdims=True)
            attn_probs = (raised / totals).astype(jnp.bfloat16)
            attended = jnp.einsum(
                "hqk,khd->qhd", attn_probs, value_seq, preferred_element_type=jnp.float32
            )
            return (attended.astype(jnp.bfloat16), (highest + jnp.log(totals))[:, :, 0])

        attended, log_block = lax.map(block_forward, query_blocks)
        return (attended.reshape(seq_len, head_part), log_block)

    head_out, log_totals = lax.map(seq_forward, (query_heads, key_heads, value_heads, lengths))
    tok_attn = lax.all_to_all(head_out, "head", split_axis=1, concat_axis=2, tiled=True)
    branch = (
        jnp.dot(tok_attn.reshape(row_count, width), attn_full, preferred_element_type=jnp.float32)
        + out_bias
    )
    residual_one = flat_rows.astype(jnp.float32) + branch
    normed_one, norm_one_back = jax.vjp(
        lambda inputs: layer_norm(inputs, ln1_gain, ln1_bias), residual_one
    )
    hidden = (
        jnp.dot(normed_one.astype(jnp.bfloat16), first_full, preferred_element_type=jnp.float32)
        + ffn_in_bias
    )
    active, gelu_back = jax.vjp(gelu_exact, hidden)
    ffn_out = (
        jnp.dot(active.astype(jnp.bfloat16), second_full, preferred_element_type=jnp.float32)
        + ffn_out_bias
    )
    result, norm_two_back = jax.vjp(
        lambda inputs: layer_norm(inputs, ln2_gain, ln2_bias), normed_one + ffn_out
    )
    layer_output = result.astype(jnp.bfloat16).reshape(tok_shape)
    qkv_back, attn_back, first_back, second_back = (
        lax.all_gather(qkv_weight, "dp", axis=0, tiled=True),
        lax.all_gather(out_weight, "dp", axis=0, tiled=True),
        lax.all_gather(ffn_in_weight, "dp", axis=0, tiled=True),
        lax.all_gather(ffn_out_weight, "dp", axis=0, tiled=True),
    )
    grad_out = out_cotangent.reshape(row_count, width).astype(jnp.float32)
    grad_ln2_bias = jnp.sum(grad_out, axis=0)
    (grad_res_two,) = norm_two_back(grad_out)
    grad_ffn_out = grad_res_two.astype(jnp.bfloat16)
    grad_ffn_out_bias = jnp.sum(grad_ffn_out.astype(jnp.float32), axis=0)
    grad_active = back_product(grad_ffn_out, second_back)
    (grad_hidden,) = gelu_back(grad_active)
    grad_hidden = grad_hidden.astype(jnp.bfloat16)
    grad_ffn_in_bias = jnp.sum(grad_hidden.astype(jnp.float32), axis=0)
    grad_normed = back_product(grad_hidden, first_back) + grad_res_two
    grad_ln1_bias = jnp.sum(grad_normed, axis=0)
    (grad_res_one,) = norm_one_back(grad_normed)
    grad_branch = grad_res_one.astype(jnp.bfloat16)
    grad_out_bias = jnp.sum(grad_branch.astype(jnp.float32), axis=0)
    grad_attended = back_product(grad_branch, attn_back).astype(jnp.bfloat16).reshape(tok_shape)
    grad_heads = lax.all_to_all(
        grad_attended, "head", split_axis=2, concat_axis=1, tiled=True
    ).reshape(head_shape)

    def seq_backward(seq_items):
        query_seq, key_seq, value_seq, grad_seq, log_seq, length = seq_items
        visible = key_index < length
        query_blocks = query_seq.reshape(block_count, block_rows, local_heads, HEAD_DIM)
        grad_blocks = grad_seq.reshape(block_count, block_rows, local_heads, HEAD_DIM)

        def block_backward(carry, block_items):
            key_acc, value_acc = carry
            query_block, grad_block, log_block = block_items
            scores = (
                jnp.einsum("qhd,khd->hqk", query_block, key_seq, preferred_element_type=jnp.float32)
                * score_scale
            )
            scores = jnp.where(visible[None, None, :], scores, -1000000000.0)
            attn_probs = jnp.exp(scores - log_block[:, :, None])
            grad_probs = jnp.einsum(
                "qhd,khd->hqk", grad_block, value_seq, preferred_element_type=jnp.float32
            )
            centre = jnp.sum(attn_probs * grad_probs, axis=-1, keepdims=True)
            grad_scores = (attn_probs * (grad_probs - centre)).astype(jnp.bfloat16)
            grad_query = (
                jnp.einsum("hqk,khd->qhd", grad_scores, key_seq, preferred_element_type=jnp.float32)
                * score_scale
            )
            key_acc = key_acc + jnp.einsum(
                "hqk,qhd->khd", grad_scores, query_block, preferred_element_type=jnp.float32
            )
            value_acc = value_acc + jnp.einsum(
                "hqk,qhd->khd",
                attn_probs.astype(jnp.bfloat16),
                grad_block,
                preferred_element_type=jnp.float32,
            )
            return ((key_acc, value_acc), grad_query.astype(jnp.bfloat16))

        zero_acc = jnp.zeros((seq_len, local_heads, HEAD_DIM), jnp.float32)
        (key_acc, value_acc), grad_queries = lax.scan(
            block_backward, (zero_acc, zero_acc), (query_blocks, grad_blocks, log_seq)
        )
        return (
            grad_queries.reshape(seq_len, head_part),
            (key_acc * score_scale).astype(jnp.bfloat16).reshape(seq_len, head_part),
            value_acc.astype(jnp.bfloat16).reshape(seq_len, head_part),
        )

    grad_q_heads, grad_k_heads, grad_v_heads = lax.map(
        seq_backward, (query_heads, key_heads, value_heads, grad_heads, log_totals, lengths)
    )
    grad_q_tok, grad_k_tok, grad_v_tok = (
        lax.all_to_all(grad_q_heads, "head", split_axis=1, concat_axis=2, tiled=True),
        lax.all_to_all(grad_k_heads, "head", split_axis=1, concat_axis=2, tiled=True),
        lax.all_to_all(grad_v_heads, "head", split_axis=1, concat_axis=2, tiled=True),
    )
    grad_q_rows = grad_q_tok.reshape(row_count, width)
    grad_k_rows = grad_k_tok.reshape(row_count, width)
    grad_v_rows = grad_v_tok.reshape(row_count, width)
    grad_input = (
        grad_res_one
        + back_product(grad_q_rows, qkv_back[:, :width])
        + back_product(grad_k_rows, qkv_back[:, width : 2 * width])
        + back_product(grad_v_rows, qkv_back[:, 2 * width :])
    )
    grad_qv = jnp.stack(
        [
            jnp.sum(grad_q_rows.astype(jnp.float32), axis=0),
            jnp.sum(grad_v_rows.astype(jnp.float32), axis=0),
        ]
    )
    bias_totals = lax.psum(
        (grad_qv, grad_out_bias, grad_ln1_bias, grad_ffn_in_bias, grad_ffn_out_bias, grad_ln2_bias),
        ("dp", "head"),
    )
    return (
        layer_output,
        grad_input.astype(jnp.bfloat16).reshape(tok_shape),
        bias_totals[0],
        bias_totals[1],
        bias_totals[2],
        bias_totals[3],
        bias_totals[4],
        bias_totals[5],
    )


MESH_IDS = pl.DeviceIdType.MESH
BF16, F32 = jnp.bfloat16, jnp.float32
ANY = pl.BlockSpec(memory_space=pl.ANY)
LANES = 128
COT_PIECES = 8
NT = (((1,), (1,)), ((), ()))


def mm(left, right):
    return jnp.dot(left, right, preferred_element_type=F32)


def mm_nt(left, right):
    return lax.dot_general(left, right, NT, preferred_element_type=F32)


def whole(shape, memory_space=pltpu.VMEM):
    return pl.BlockSpec(memory_space=memory_space)


def params(vmem, **more):
    return pltpu.CompilerParams(vmem_limit_bytes=vmem << 20, **more)


def relay(jobs, held, sems):
    ways = [
        [pltpu.make_async_copy(src, held.at[i], sems.at[0, i]), pltpu.make_async_copy(held.at[i], dst, sems.at[1, i])]
        for i, (src, dst) in enumerate(jobs)
    ]
    for way in ways:
        way[0].start()
    for way in ways:
        way[0].wait()
        way[1].start()
    return [way[1] for way in ways]


def relay_scratch(array):
    count = 4 * array.shape[0]
    shape = (count, array.shape[1] // 2, *array.shape[2:])
    return [pltpu.VMEM(shape, array.dtype), pltpu.SemaphoreType.DMA((2, count))]


def halves(src, dst):
    rows = src.shape[0] // 2
    return [(src.at[pl.ds(i * rows, rows)], dst.at[pl.ds(i * rows, rows)]) for i in range(2)]


def sort_kernel(lengths, tok, cot, tok_out, cot_out, perm, lens, held, sems):
    count = tok.shape[0]
    jobs = []
    for i in range(count):
        rank = 0
        for j in range(count):
            before = lengths[j] <= lengths[i] if j < i else lengths[j] < lengths[i]
            rank = rank + (before.astype(jnp.int32) if j != i else 0)
        perm[i] = rank
        lens[rank] = lengths[i]
        jobs += halves(tok.at[i], tok_out.at[rank]) + halves(cot.at[i], cot_out.at[rank])
    for copy in relay(jobs, held, sems):
        copy.wait()


def sort_sequences(lengths, tok, cot):
    smem = pl.BlockSpec(memory_space=pltpu.SMEM)
    count = lengths.shape[0]
    index = jax.ShapeDtypeStruct((count,), jnp.int32)
    return pl.pallas_call(
        sort_kernel,
        out_shape=[jax.ShapeDtypeStruct(tok.shape, BF16), jax.ShapeDtypeStruct(cot.shape, BF16), index, index],
        in_specs=[smem, ANY, ANY],
        out_specs=[ANY, ANY, smem, smem],
        scratch_shapes=relay_scratch(tok),
        name="sort",
    )(lengths, tok, cot)


def unsort_kernel(perm, layer, grad, sums, q_sums, layer_out, grad_out, qv, *rest):
    biases, (held, sems) = rest[:-2], rest[-2:]
    jobs = []
    for i in range(layer.shape[0]):
        jobs += halves(layer.at[perm[i]], layer_out.at[i]) + halves(grad.at[perm[i]], grad_out.at[i])
    copies = relay(jobs, held, sems)
    width = sums.shape[1]
    qv[0:1, :] = q_sums[0:1, :]
    qv[1:2, :] = sums[1:2, :]
    row = 2
    for bias in biases:
        for at in range(bias.shape[0] // width):
            bias[pl.ds(at * width, width)] = sums[row, :]
            row += 1
    for copy in copies:
        copy.wait()


def unsort_sequences(perm, layer, grad, sums, q_sums, hidden):
    whole = pl.BlockSpec(memory_space=pltpu.VMEM)
    out = jax.ShapeDtypeStruct
    count, width = layer.shape[0], layer.shape[2]
    sizes = (width, width, hidden, width, width)
    return pl.pallas_call(
        unsort_kernel,
        out_shape=[out(layer.shape, BF16), out(grad.shape, BF16), out((2, width), F32)]
        + [out((size,), F32) for size in sizes],
        in_specs=[pl.BlockSpec(memory_space=pltpu.SMEM), ANY, ANY, whole, whole],
        out_specs=[ANY, ANY] + [whole] * 6,
        scratch_shapes=relay_scratch(layer),
        name="unsort",
    )(perm, layer, grad, sums, q_sums)


class Place:
    def __init__(self, z_count):
        self.dp, self.head = lax.axis_index("dp"), lax.axis_index("head")
        self.z, self.y = self.dp // 2, self.dp % 2
        self.x, self.core = self.head // 2, self.head % 2
        self.z_count = z_count

    def along_z(self, step):
        return (((self.z + step) % self.z_count) * 2 + self.y, self.head)

    def other_y(self):
        return (self.z * 2 + (1 - self.y), self.head)

    def other_x(self):
        return (self.dp, (1 - self.x) * 2 + self.core)

    def other_core(self):
        return (self.dp, self.x * 2 + (1 - self.core))

    def peers(self):
        steps = [self.along_z(step) for step in range(1, self.z_count)]
        return steps + [self.other_y(), self.other_x(), self.other_core()]


def meet(place):
    barrier = pltpu.get_barrier_semaphore()
    peers = place.peers()
    for peer in peers:
        pl.semaphore_signal(barrier, inc=1, device_id=peer, device_id_type=MESH_IDS)
    pl.semaphore_wait(barrier, len(peers))


def push(src, dst, send, recv, target):
    return pltpu.make_async_remote_copy(
        src_ref=src, dst_ref=dst, send_sem=send, recv_sem=recv, device_id=target, device_id_type=MESH_IDS
    )


class Gather:
    def __init__(self, place, chunks, sems):
        z_send, z_recv, h_send, h_recv, local = sems
        x, core, z, y = place.x, place.core, place.z, place.y
        self.plans = []
        for number, (shard, full, row, rows, col, cols) in enumerate(chunks):
            base = row + core * (rows // 2)
            role = pl.ds(pl.multiple_of(base + x * (rows // 8), 16), rows * 3 // 8)
            own = pl.ds(pl.multiple_of(base + x * (rows * 3 // 8), 16), rows // 8)
            half = pl.ds(pl.multiple_of(base, 16), rows // 2)
            span = pl.ds(col, cols)
            along = [
                push(
                    shard.at[role, span],
                    full.at[z, y, role, span],
                    z_send.at[number, step - 1],
                    z_recv.at[number, step - 1],
                    place.along_z(step),
                )
                for step in range(1, place.z_count)
            ]
            here = pltpu.make_async_copy(shard.at[role, span], full.at[z, y, role, span], local.at[number])
            hops = []
            for hop, (view, target) in enumerate(
                (
                    (full.at[:, y, role, span], place.other_y()),
                    (full.at[:, :, own, span], place.other_x()),
                    (full.at[:, :, half, span], place.other_core()),
                )
            ):
                hops.append(push(view, view, h_send.at[number, hop], h_recv.at[number, hop], target))
            self.plans.append((along, here, hops))
        self.count = len(self.plans)

    def along_z(self, step):
        if 0 <= step < self.count:
            along, here, _ = self.plans[step]
            for copy in along:
                copy.start()
            here.start()

    def step(self, step):
        if step == 0:
            self.along_z(0)
        self.along_z(step + 1)
        if 0 <= step - 1 < self.count:
            along, here, hops = self.plans[step - 1]
            for copy in along:
                copy.wait_recv()
            here.wait()
            hops[0].start()
        for hop in (1, 2):
            if 0 <= step - 1 - hop < self.count:
                hops = self.plans[step - 1 - hop][2]
                hops[hop - 1].wait_recv()
                hops[hop].start()

    def arrived(self, number):
        self.plans[number][2][2].wait_recv()

    def sent(self, first, last):
        for along, _, hops in self.plans[first:last]:
            for copy in along + hops:
                copy.wait_send()


def lane_row(pick):
    lane = lax.broadcasted_iota(jnp.int32, (1, LANES), 1)
    return jnp.where(pick(lane), 1.0, 0.0).astype(F32)


def head_lanes(half):
    return lane_row(lambda lane: (lane >= half * HEAD_DIM) & (lane < (half + 1) * HEAD_DIM))


def spare_lane(half, index):
    return (1 - half) * HEAD_DIM + index


def spare(half, index):
    return lane_row(lambda lane: lane == spare_lane(half, index))


def split_three(value):
    high = value.astype(BF16).astype(F32)
    rest = value - high
    middle = rest.astype(BF16).astype(F32)
    return high, middle, rest - middle


def mask_column(length, keys):
    return jnp.where(lax.broadcasted_iota(jnp.int32, (keys, 1), 0) < length, 0.0, -1000000000.0)


def attend(tile, pair, q_tmp, kv_ext, key_at, value_at, q_ext, att):
    columns = pl.ds(pl.multiple_of(pair * LANES, LANES), LANES)
    for block in range(3):
        q_rows = pl.ds(block * tile, tile)
        outs = []
        for half in range(2):
            head = 2 * pair + half
            query = q_tmp[q_rows, columns].astype(F32) * head_lanes(half) + spare(half, 3)
            scores = mm_nt(query.astype(BF16), kv_ext[key_at(head, block), :])
            highest = jnp.max(scores, axis=-1, keepdims=True)
            raised = jnp.exp(scores - highest).astype(BF16)
            summed = mm(raised, kv_ext[value_at(head, block), :])
            outs.append(summed / pltpu.roll(summed, HEAD_DIM, 1))
            column = spare_lane(half, 0)
            log_total = highest + jnp.log(summed[:, column : column + 1])
            high, middle, low = split_three(-log_total)
            query = query + high * spare(half, 0) + middle * spare(half, 1) + low * spare(half, 2)
            q_ext[head, q_rows, :] = query.astype(BF16)
        att[q_rows, columns] = jnp.where(head_lanes(0) > 0, outs[0], outs[1]).astype(BF16)


def row_mean(value):
    return jnp.mean(value, axis=-1, keepdims=True)


def normalise(value):
    centre = value - row_mean(value)
    rstd = lax.rsqrt(row_mean(centre * centre) + epsilon)
    return centre * rstd, rstd


def normalise_back(grad, normal, rstd):
    return rstd * (grad - row_mean(grad) - normal * row_mean(grad * normal))


def column_sum(value):
    return jnp.sum(value.astype(F32), axis=0, keepdims=True)


def slot_table():
    names = "k0 v0 a00 a01 a02 a03 k1 v1 a10 a11 a12 a13 o u0 u1 u2 u3 u4 u5 u6 w0 w1 w2"
    table = {name: [4 + i] for i, name in enumerate(names.split())}
    return table


def main_kernel(z_count, tile, chunks_of, *refs):
    lens_ref, refs = refs[0], refs[1:]
    shards, (tok, cot, qv_bias, b1_ref), vectors, refs = refs[:4], refs[4:8], refs[8:14], refs[14:]
    (wqkv_hbm, q_hbm, kv_hbm, turn_hbm, o_hbm, layer_hbm, gres_hbm, gatt_hbm, sums_ref, sums1_ref), refs = (
        refs[:10],
        refs[10:],
    )
    (tok_v, own_v, cot_v, big, wo, w1, w2, q_tmp, kv_ext, k_turn, q_ext, att, norm1, spread1, acc, low), refs = (
        refs[:16],
        refs[16:],
    )
    sems, (t_send, t_recv, t_local, c_send, c_recv, store) = refs[:5], refs[5:]
    place = Place(z_count)
    x, core = place.x, place.core
    width = att.shape[1]
    hidden = b1_ref.shape[0]
    keep, give = 2 - x, 1 + x
    length = lens_ref[keep]
    meet(place)
    comm = Gather(place, chunks_of(shards, (big, wo, w1, w2)), sems)
    comm.step(0)

    first = (x == 0) & (core == 0)
    tok_x = push(tok.at[give], tok_v.at[2 * x + core], t_send.at[0], t_recv.at[0], place.other_x())
    tok_core = [
        push(tok_v.at[2 * i + core], tok_v.at[2 * i + core], t_send.at[1 + i], t_recv.at[1 + i], place.other_core())
        for i in range(2)
    ]
    cot_rows = [pl.ds(i * (tile // COT_PIECES), tile // COT_PIECES) for i in range(COT_PIECES)]
    cot_x = [
        push(cot.at[give, rows], cot_v.at[x, rows], c_send.at[i], c_recv.at[i], place.other_x())
        for i, rows in enumerate(cot_rows)
    ]
    short_x = push(tok.at[0], tok_v.at[4], t_send.at[4], t_recv.at[4], place.other_x())
    short_core = push(tok_v.at[4], tok_v.at[4], t_send.at[5], t_recv.at[5], place.other_core())
    own = [
        pltpu.make_async_copy(tok.at[keep], tok_v.at[2 * x + core], t_local.at[0]),
        pltpu.make_async_copy(tok.at[0], own_v, t_local.at[1]),
        pltpu.make_async_copy(cot.at[keep], cot_v.at[x], t_local.at[2]),
        pltpu.make_async_copy(cot.at[0], cot_v.at[2], t_local.at[3]),
    ]
    short_own = pltpu.make_async_copy(tok.at[0], tok_v.at[4], t_local.at[4])
    tok_x.start()
    for copy in own:
        copy.start()

    @pl.when(first)
    def _():
        short_x.start()
        short_own.start()

    comm.step(1)
    own[0].wait()
    tok_x.wait_recv()
    for copy in tok_core:
        copy.start()

    @pl.when((x == 1) & (core == 0))
    def _():
        short_x.wait_recv()

    @pl.when(first)
    def _():
        short_own.wait()

    @pl.when(core == 0)
    def _():
        short_core.start()

    comm.step(2)
    comm.step(3)
    slots = slot_table()

    def slot(name):
        for step in slots.get(name, ()):
            comm.step(step)
            if step >= 8 and step % 2 == 0 and step // 2 - 4 < COT_PIECES:
                cot_x[step // 2 - 4].start()

    part_cols = width // 2

    def qkv_part(part, which):
        start = pl.multiple_of(part * width + which * part_cols, part_cols)
        return big[:, :, :, pl.ds(start, part_cols)].reshape(width, part_cols)

    keys_count = 5 * tile

    def key_at(head, block):
        start, count = (4 * tile, tile) if block == 2 else (0, 4 * tile)
        return pl.ds(pl.multiple_of(head * keys_count + start, tile), count)

    def value_at(head, block):
        start, count = (4 * tile, tile) if block == 2 else (0, 4 * tile)
        return pl.ds(pl.multiple_of((width // HEAD_DIM + head) * keys_count + start, tile), count)

    def lanes_of(pair):
        return pl.ds(pl.multiple_of(pair * LANES, LANES), LANES)

    def project_keys(side, which, block):
        value = mm(tok_v[block], qkv_part(1, which)).astype(BF16).astype(F32)
        row = lax.broadcasted_iota(jnp.int32, (tile, 1), 0) + block * tile
        hidden_keys = jnp.where((row < length) | (block == 4), 0.0, -1000000000.0)
        for i in range(part_cols // LANES):
            pair = which * (part_cols // LANES) + i
            both = value[:, i * LANES : (i + 1) * LANES]
            for half in range(2):
                ones = spare(half, 0) + spare(half, 1) + spare(half, 2)
                key = both * head_lanes(half) + ones + hidden_keys * spare(half, 3)
                at = (2 * pair + half) * keys_count + block * tile
                kv_ext[pl.ds(pl.multiple_of(at, tile), tile), :] = key.astype(BF16)
            k_turn[pair, :, pl.ds(pl.multiple_of(block * tile, tile), tile)] = both.T.astype(BF16)

    def project_values(side, which, block):
        value = mm(tok_v[block], qkv_part(2, which))
        value = (value + qv_bias[1:2, side]).astype(BF16).astype(F32)
        for i in range(part_cols // LANES):
            pair = which * (part_cols // LANES) + i
            both = value[:, i * LANES : (i + 1) * LANES]
            for half in range(2):
                mine = head_lanes(half)
                at = (width // HEAD_DIM + 2 * pair + half) * keys_count + block * tile
                kv_ext[pl.ds(pl.multiple_of(at, tile), tile), :] = (both * mine + (1.0 - mine)).astype(BF16)

    scale = 1.0 / math.sqrt(HEAD_DIM)
    own[1].wait()
    half_rows = kv_ext.shape[0] // 4
    kv_stores = [
        [
            pltpu.make_async_copy(
                kv_ext.at[pl.ds((2 * kind + at) * half_rows, half_rows)],
                kv_hbm.at[pl.ds((2 * kind + at) * half_rows, half_rows)],
                store.at[2 * at + kind],
            )
            for kind in range(2)
        ]
        for at in range(2)
    ]

    stores = [
        pltpu.make_async_copy(src, dst, store.at[4 + i])
        for i, (src, dst) in enumerate(((big, wqkv_hbm), (k_turn, turn_hbm), (q_ext, q_hbm), (att, o_hbm)))
    ]

    def heads_half(which, _):
        side = pl.ds(pl.multiple_of(which * part_cols, part_cols), part_cols)
        for at in range(2):

            @pl.when(which == at)
            def _():
                slot(f"k{at}")
                comm.arrived(3 * at)
                if at == 0:
                    for copy in tok_core:
                        copy.wait_recv()

                    @pl.when(core == 1)
                    def _():
                        short_core.wait_recv()

        def keys_block(block, _):
            project_keys(side, which, block)
            return 0

        lax.fori_loop(0, 5, keys_block, 0)
        for at in range(2):

            @pl.when(which == at)
            def _():
                slot(f"v{at}")
                comm.arrived(3 * at + 1)

        def values_block(block, _):
            project_values(side, which, block)
            return 0

        lax.fori_loop(0, 5, values_block, 0)
        for at in range(2):

            @pl.when(which == at)
            def _():
                slot(f"q{at}")
                comm.arrived(3 * at + 2)
                if at == 1:
                    stores[0].start()

        for block in range(3):
            rows = own_v[...] if block == 2 else tok_v[2 * block + core]
            query = (mm(rows, qkv_part(0, which)) + qv_bias[0:1, side]).astype(BF16).astype(F32) * scale
            q_tmp[block * tile : (block + 1) * tile, side] = query.astype(BF16)

        for at in range(2):

            @pl.when(which == at)
            def _():
                for copy in kv_stores[at]:
                    copy.start()

        def pair_step(i, _):
            for at in range(2):
                for j in range(part_cols // LANES):
                    if f"a{at}{j}" in slots:

                        @pl.when((which == at) & (i == j))
                        def _():
                            slot(f"a{at}{j}")

            attend(tile, which * (part_cols // LANES) + i, q_tmp, kv_ext, key_at, value_at, q_ext, att)
            return 0

        lax.fori_loop(0, part_cols // LANES, pair_step, 0)
        return 0

    lax.fori_loop(0, 2, heads_half, 0)
    for copy in stores[1:]:
        copy.start()

    bo, g1, s1, b2, g2, s2 = (vector[...].reshape(1, width) for vector in vectors)
    slot("o")
    comm.arrived(6)
    comm.arrived(7)
    for block in range(3):
        rows = pl.ds(block * tile, tile)
        token = own_v[...] if block == 2 else tok_v[2 * block + core]
        branch = mm(att[rows, :], wo[...].reshape(width, width)) + bo
        normal, rstd = normalise(token.astype(F32) + branch)
        norm1[rows, :] = normal
        spread1[rows, :] = jnp.broadcast_to(rstd, (tile, LANES))
        low[rows, :] = (normal * g1 + s1).astype(BF16)
        acc[rows, :] = jnp.zeros((tile, width), F32)

    block_width = w2.shape[2]
    blocks = hidden // block_width
    per = width // block_width
    def w1_piece(index):
        span = pl.ds(pl.multiple_of(index * block_width, block_width), block_width)
        return w1[:, :, :, span].reshape(width, block_width)

    def slope_at(index, block, part):
        return index // 2, index % 2, slice(None), pl.ds((2 * block + part) * block_width, block_width)

    def up(index, _):
        for i in range(blocks):

            @pl.when(index == i)
            def _():
                slot(f"u{i}")
                comm.arrived(8 + i)
                if i == 0:
                    stores[0].wait()
                    for copy in kv_stores[0] + kv_stores[1]:
                        copy.wait()
                    comm.sent(0, 6)

        span = pl.ds(pl.multiple_of(index * block_width, block_width), block_width)
        first_piece = w1_piece(index)
        bias = b1_ref[span].reshape(1, block_width)
        for block in range(3):
            rows = pl.ds(block * tile, tile)
            value = mm(low[rows, :], first_piece) + bias
            share = 0.5 * (1.0 + lax.erf(value * 0.7071067811865476))
            slope = share + value * (0.3989422804014327 * jnp.exp(-0.5 * value * value))
            for part in range(2):
                big[slope_at(index, block, part)] = slope[part * 128 : (part + 1) * 128].astype(BF16)
            active = (value * share).astype(BF16)
            for part in range(block_width // 128):
                at = (part * blocks + index) * (3 * tile) + block * tile
                kv_ext[pl.ds(pl.multiple_of(at, tile), tile), :] = active[:, part * 128 : (part + 1) * 128]
        return 0

    lax.fori_loop(0, blocks, up, 0)

    def widen(part, _):
        for i in range(block_width // 128):

            @pl.when(part == i)
            def _():
                slot(f"w{i}")
                comm.arrived(8 + blocks + 2 * i)
                comm.arrived(9 + blocks + 2 * i)

        second = w2[:, :, pl.ds(pl.multiple_of(part * 128, 128), 128), :].reshape(width, width)
        for block in range(3):
            rows = pl.ds(block * tile, tile)
            starts = [(part * blocks + i) * (3 * tile) + block * tile for i in range(blocks)]
            active = [kv_ext[pl.ds(pl.multiple_of(start, tile), tile), :] for start in starts]
            acc[rows, :] += mm(jnp.concatenate(active, axis=1), second)
        return 0

    lax.fori_loop(0, block_width // 128, widen, 0)

    stores[3].wait()
    for copy in own[2:]:
        copy.wait()
    for copy in cot_x:
        copy.wait_recv()
    totals = [jnp.zeros((1, width), F32)] * 5
    for block in range(3):
        rows = pl.ds(block * tile, tile)
        normal, rstd = normalise(norm1[rows, :] * g1 + s1 + acc[rows, :] + b2)
        att[rows, :] = (normal * g2 + s2).astype(BF16)
        grad = cot_v[block].astype(F32)
        result = normalise_back(grad * g2, normal, rstd)
        acc[rows, :] = result
        small = result.astype(BF16)
        low[rows, :] = small
        totals[0] = totals[0] + column_sum(grad)
        totals[1] = totals[1] + column_sum(small)

    def att_rows(block):
        return att.at[pl.ds(pl.multiple_of(block * tile, tile), tile), :]

    layer_home = push(att_rows(1 - x), layer_hbm.at[keep], t_send.at[6], t_recv.at[6], place.other_x())
    layer_own = [
        pltpu.make_async_copy(att_rows(x), layer_hbm.at[keep], t_local.at[5]),
        pltpu.make_async_copy(att_rows(2), layer_hbm.at[0], t_local.at[6]),
    ]
    layer_home.start()
    for copy in layer_own:
        copy.start()

    def down(index, _):
        span = pl.ds(pl.multiple_of(index * block_width, block_width), block_width)
        first_piece, second = w1_piece(index), w2[index // 2, index % 2]
        total = jnp.zeros((1, block_width), F32)
        for block in range(3):
            rows = pl.ds(block * tile, tile)
            slope = jnp.concatenate([big[slope_at(index, block, part)] for part in range(2)], axis=0).astype(F32)
            small = (mm_nt(low[rows, :], second) * slope).astype(BF16)
            total = total + column_sum(small)
            acc[rows, :] += mm_nt(small, first_piece)
        sums1_ref[:, span] = total
        return 0

    lax.fori_loop(0, blocks, down, 0)
    stores[2].wait()
    for block in range(3):
        rows = pl.ds(block * tile, tile)
        grad = acc[rows, :]
        totals[2] = totals[2] + column_sum(grad)
        result = normalise_back(grad * g1, norm1[rows, :], spread1[rows, 0:1])
        acc[rows, :] = result
        small = result.astype(BF16)
        totals[3] = totals[3] + column_sum(small)
        grad_att = mm_nt(small, wo[...].reshape(width, width)).astype(BF16)
        totals[4] = totals[4] + column_sum(grad_att)
        q_tmp[rows, :] = grad_att
    for number, total in enumerate(totals):
        sums_ref[number : number + 1, :] = total
    results = [
        pltpu.make_async_copy(acc, gres_hbm, store.at[8]),
        pltpu.make_async_copy(q_tmp, gatt_hbm, store.at[9]),
    ]
    for copy in results:
        copy.start()
    comm.sent(6, comm.count)
    for copy in tok_core:
        copy.wait_send()
    tok_x.wait_send()
    for copy in cot_x:
        copy.wait_send()

    @pl.when(first)
    def _():
        short_x.wait_send()

    @pl.when(core == 0)
    def _():
        short_core.wait_send()

    for copy in layer_own + stores[1:2] + results:
        copy.wait()
    layer_home.wait()


def main(lens, shards, tok, cot, qv_bias, vectors, ffn_in_bias, dp_count):
    z_count = dp_count // 2
    tile, width = tok.shape[1:]
    rows = 3 * tile
    hidden = ffn_in_bias.shape[0]
    out, dma, vmem = jax.ShapeDtypeStruct, pltpu.SemaphoreType.DMA, pltpu.VMEM

    def chunks_of(shards, fulls):
        qkv, wo, w1, w2 = zip(shards, fulls)
        side = width // 2
        chunks = [(*qkv, 0, 128, part * width + i * side, side) for i in range(2) for part in (1, 2, 0)]
        chunks += [(*wo, 0, 128, i * side, side) for i in range(2)]
        chunks += [(*w1, 0, 128, col, side) for col in range(0, hidden, side)]
        chunks += [(*w2, row, 128, i * side, side) for row in range(0, w2[0].shape[0], 128) for i in range(2)]
        return chunks

    count = len(chunks_of(shards, shards))
    whole = pl.BlockSpec(memory_space=pltpu.VMEM)
    weights = [out((z_count, 2, *shard.shape), BF16) for shard in shards]
    return pl.pallas_call(
        functools.partial(main_kernel, z_count, tile, chunks_of),
        out_shape=[
            weights[0],
            out((width // HEAD_DIM, rows, LANES), BF16),
            out((2 * (width // HEAD_DIM) * 5 * tile, LANES), BF16),
            out((width // LANES, LANES, 5 * tile), BF16),
            out((rows, width), BF16),
            out((3, tile, width), BF16),
            out((rows, width), F32),
            out((rows, width), BF16),
            out((5, width), F32),
            out((1, hidden), F32),
        ],
        in_specs=[pl.BlockSpec(memory_space=pltpu.SMEM)] + [ANY] * 6 + [whole] * 8,
        out_specs=[ANY] * 8 + [whole] * 2,
        scratch_shapes=[
            vmem((5, tile, width), BF16),
            vmem((tile, width), BF16),
            vmem((3, tile, width), BF16),
            vmem(weights[0].shape, BF16),
            vmem(weights[1].shape, BF16),
            vmem(weights[2].shape, BF16),
            vmem(weights[3].shape, BF16),
            vmem((rows, width), BF16),
            vmem((2 * (width // HEAD_DIM) * 5 * tile, LANES), BF16),
            vmem((width // LANES, LANES, 5 * tile), BF16),
            vmem((width // HEAD_DIM, rows, LANES), BF16),
            vmem((rows, width), BF16),
            vmem((rows, width), F32),
            vmem((rows, LANES), F32),
            vmem((rows, width), F32),
            vmem((rows, width), BF16),
            dma((count, z_count - 1)),
            dma((count, z_count - 1)),
            dma((count, 3)),
            dma((count, 3)),
            dma((count,)),
            dma((7,)),
            dma((7,)),
            dma((7,)),
            dma((COT_PIECES,)),
            dma((COT_PIECES,)),
            dma((10,)),
        ],
        compiler_params=params(63, collective_id=0, has_side_effects=True),
        name="main",
    )(lens, *shards, tok, cot, qv_bias, ffn_in_bias, *vectors)


def back_kernel(z_count, tile, *refs):
    (q_hbm, kv_hbm, turn_hbm, o_hbm, g_hbm, gres_hbm, wqkv_hbm), (sums_mid, sums_hidden), refs = (
        refs[:7],
        refs[7:9],
        refs[9:],
    )
    grad_out, sums_out, q_sum_out, refs = refs[0], refs[1], refs[2], refs[3:]
    q_ext, k_ext, v_ext, k_turn, o_all, g_all, g_ext, gres, big, dq, dk, dv, turned_sum = refs[:13]
    k_sum, v_sum, pair_recv, short_recv, short_send, home, part, part_recv, part_z = refs[13:22]
    tail, tail_recv, tail_z, q_total = refs[22:26]
    load, k_send, k_recv, s_send, s_recv, o_send, o_recv, r_send, r_recv, u_send, u_recv, local = refs[26:]
    place = Place(z_count)
    x, core, z = place.x, place.core, place.z
    keep = 2 - x
    width = o_all.shape[1]
    long_keys = 4 * tile
    pairs = width // LANES
    short_rows, long_rows = pl.ds(2 * tile, tile), pl.ds(0, 2 * tile)
    short_at, long_at = pl.ds(long_keys, tile), pl.ds(0, long_keys)
    loads = []

    def fetch(src, dst):
        copy = pltpu.make_async_copy(src, dst, load.at[len(loads)])
        copy.start()
        loads.append(copy)

    for at, rows in ((short_at, short_rows), (long_at, long_rows)):
        fetch(kv_hbm.at[0, :, at], k_ext.at[:, at])
        fetch(kv_hbm.at[1, :, at], v_ext.at[:, at])
        fetch(turn_hbm.at[:, :, at], k_turn.at[:, :, at])
        fetch(o_hbm.at[rows], o_all.at[rows])
        fetch(g_hbm.at[rows], g_all.at[rows])
        fetch(q_hbm.at[:, rows], q_ext.at[:, rows])
    fetch(gres_hbm, gres)
    for piece in range(3):
        for i in range(z_count):
            fetch(
                wqkv_hbm.at[i, :, :, pl.ds(piece * width, width)],
                big.at[pl.ds(8 * piece + 2 * i, 2)],
            )
    meet(place)

    targets = (place.other_core(), place.other_y(), place.other_x())

    class AllSum:
        def __init__(self, mine, recv, by_z, send_sems, recv_sems):
            self.mine, self.recv, self.by_z = mine, recv, by_z
            self.hops = [
                push(mine.at[i + i // 2], recv.at[i], send_sems.at[i], recv_sems.at[i], target)
                for i, target in enumerate(targets)
            ]
            self.along = [
                push(mine.at[2], by_z.at[z], send_sems.at[2 + step], recv_sems.at[2 + step], place.along_z(step))
                for step in range(1, z_count)
            ]

        def begin(self):
            self.hops[0].start()

        def hop(self, i):
            if i < 2:
                self.hops[i].wait_recv()
                self.mine[i + 1] = self.mine[i] + self.recv[i]
                for copy in self.hops[1:2] if i == 0 else self.along:
                    copy.start()
            else:
                self.by_z[z] = self.mine[2]
                for copy in self.along:
                    copy.wait_recv()
                total = self.by_z[0]
                for step in range(1, z_count):
                    total = total + self.by_z[step]
                self.mine[3] = total
                self.hops[2].start()

        def result(self):
            self.hops[2].wait_recv()
            return self.mine[3] + self.recv[2]

        def sent(self):
            for copy in self.hops + self.along:
                copy.wait_send()

    early = AllSum(part, part_recv, part_z, r_send, r_recv)
    late = AllSum(tail, tail_recv, tail_z, u_send, u_recv)
    part[0] = jnp.zeros(part.shape[1:], F32)
    part[0, 1:2, :] = sums_mid[4:5, :]
    part[0, 2:3, :] = sums_mid[3:4, :]
    part[0, 3:4, :] = sums_mid[2:3, :]
    for i in range(sums_hidden.shape[1] // width):
        part[0, 4 + i : 5 + i, :] = sums_hidden[:, i * width : (i + 1) * width]
    part[0, 8:9, :] = sums_mid[1:2, :]
    part[0, 9:10, :] = sums_mid[0:1, :]
    early.begin()
    q_total[...] = jnp.zeros(q_total.shape, F32)

    kinds = (dk, dv)

    def to_sibling(kind, block):
        return push(
            kinds[kind].at[2 * block + 1 - core],
            pair_recv.at[kind, block],
            k_send.at[kind, block],
            k_recv.at[kind, block],
            place.other_core(),
        )

    pair_copies = [[to_sibling(kind, block) for kind in range(2)] for block in (1 - x, x)]
    short_core = [
        push(kinds[kind].at[4], short_recv.at[0, kind], s_send.at[0, kind], s_recv.at[0, kind], place.other_core())
        for kind in range(2)
    ]
    short_x = [
        push(short_send.at[kind], short_recv.at[1, kind], s_send.at[1, kind], s_recv.at[1, kind], place.other_x())
        for kind in range(2)
    ]
    grad_home = push(home.at[0], grad_out.at[keep], o_send.at[0], o_recv.at[0], place.other_x())
    grad_own = [
        pltpu.make_async_copy(home.at[1], grad_out.at[keep], local.at[0]),
        pltpu.make_async_copy(home.at[2], grad_out.at[0], local.at[1]),
    ]
    low_half = head_lanes(0) > 0
    scale = 1.0 / math.sqrt(HEAD_DIM)

    def columns_of(pair):
        return pl.ds(pl.multiple_of(pair * LANES, LANES), LANES)

    def prepare(pair, rows):
        columns = columns_of(pair)
        for half in range(2):
            grad = g_all[rows, columns].astype(F32) * head_lanes(half)
            centre = jnp.sum(grad * o_all[rows, columns].astype(F32), axis=-1, keepdims=True)
            high, middle, low = split_three(-centre)
            grad = grad + high * spare(half, 0) + middle * spare(half, 1) + low * spare(half, 2)
            g_ext[2 * pair + half, rows, :] = grad.astype(BF16)

    def unit(pair, half, at, rows):
        head = 2 * pair + half
        key, value, turned = k_ext[head, at, :], v_ext[head, at, :], k_turn[pair, half * HEAD_DIM : (half + 1) * HEAD_DIM, at]
        query, grad = q_ext[head, rows, :], g_ext[head, rows, :]
        probs = jnp.exp(mm_nt(key, query))
        scores = (probs * mm_nt(value, grad)).astype(BF16)
        return mm(scores, query), mm(probs.astype(BF16), grad), mm(turned, scores)

    def join(parts):
        return jnp.where(low_half, parts[0], parts[1])

    def put_queries(pair, block, turned_parts):
        grad_query = (jnp.concatenate(turned_parts, axis=0).T * scale).astype(BF16)
        columns = columns_of(pair)
        dq[block, :, columns] = grad_query
        q_total[:, columns] += column_sum(grad_query)

    def turned_rows(head):
        return pl.ds(pl.multiple_of(head * HEAD_DIM, HEAD_DIM), HEAD_DIM)

    def short_pair(pair, _):
        prepare(pair, short_rows)
        results = [unit(pair, half, short_at, short_rows) for half in range(2)]
        columns = columns_of(pair)
        dk[4, :, columns] = join([result[0] for result in results]).astype(BF16)
        dv[4, :, columns] = join([result[1] for result in results]).astype(BF16)
        put_queries(pair, 2, [result[2] for result in results])
        return 0

    for copy in loads[:6]:
        copy.wait()
    lax.fori_loop(0, pairs, short_pair, 0)

    @pl.when(core == 1)
    def _():
        for copy in short_core:
            copy.start()

    early.hop(0)
    for copy in loads[6:12]:
        copy.wait()

    def half_keys(block):
        return pl.ds(pl.multiple_of(block * 2 * tile, 2 * tile), 2 * tile)

    def q_tile(block):
        return pl.ds(pl.multiple_of(block * tile, tile), tile)

    def store_keys(ref, block, columns, value):
        for i in range(2):
            ref[2 * block + i, :, columns] = value[i * tile : (i + 1) * tile].astype(BF16)

    def pass_one(pair, _):
        prepare(pair, long_rows)
        columns = columns_of(pair)
        results = [unit(pair, half, long_at, q_tile(1 - x)) for half in range(2)]
        k_sum[:, columns] = join([result[0] for result in results])
        v_sum[:, columns] = join([result[1] for result in results])
        put_queries(pair, 1 - x, [result[2] for result in results])

        @pl.when((pair == 1) & (x == 1) & (core == 0))
        def _():
            for kind in range(2):
                short_core[kind].wait_recv()
                total = kinds[kind][4].astype(F32) + short_recv[0, kind].astype(F32)
                short_send[kind] = total.astype(BF16)
                short_x[kind].start()

        return 0

    lax.fori_loop(0, pairs, pass_one, 0)
    early.hop(1)

    def more_keys(pair, block):
        at = half_keys(block)
        columns = columns_of(pair)
        results = [unit(pair, half, at, q_tile(x)) for half in range(2)]
        store_keys(dk, block, columns, k_sum[at, columns] + join([result[0] for result in results]))
        store_keys(dv, block, columns, v_sum[at, columns] + join([result[1] for result in results]))
        return results

    def pass_two(pair, _):
        results = more_keys(pair, 1 - x)
        for half in range(2):
            turned_sum[turned_rows(2 * pair + half), :] = results[half][2]
        return 0

    lax.fori_loop(0, pairs, pass_two, 0)
    for copy in pair_copies[0]:
        copy.start()
    early.hop(2)
    for copy in loads[12:]:
        copy.wait()

    def weight(piece):
        return big[8 * piece : 8 * piece + 8].reshape(width, width)

    def from_queries(block):
        return gres[q_tile(block), :] + mm_nt(dq[block], weight(0))

    def from_keys(block, grad, copies):
        for kind in range(2):
            copies[kind].wait_recv()
            total = kinds[kind][2 * block + core].astype(F32) + pair_recv[kind, block].astype(F32)
            grad = grad + mm_nt(total.astype(BF16), weight(1 + kind))
        return grad

    home[0] = from_keys(1 - x, from_queries(1 - x), pair_copies[0]).astype(BF16)
    grad_home.start()

    def pass_three(pair, _):
        results = more_keys(pair, x)
        put_queries(pair, x, [results[half][2] + turned_sum[turned_rows(2 * pair + half), :] for half in range(2)])
        return 0

    lax.fori_loop(0, pairs, pass_three, 0)
    for copy in pair_copies[1]:
        copy.start()
    tail[0] = jnp.broadcast_to(q_total[...], tail.shape[1:])
    late.begin()
    sums_out[...] = early.result()
    first = (x == 0) & (core == 0)
    home[2] = from_queries(2).astype(BF16)

    @pl.when(first)
    def _():
        grad = from_queries(2)
        for kind in range(2):
            short_core[kind].wait_recv()
            short_x[kind].wait_recv()
            total = kinds[kind][4].astype(F32) + short_recv[0, kind].astype(F32)
            total = total + short_recv[1, kind].astype(F32)
            grad = grad + mm_nt(total.astype(BF16), weight(1 + kind))
        home[2] = grad.astype(BF16)

    grad_own[1].start()
    late.hop(0)
    grad = from_queries(x)
    late.hop(1)
    home[1] = from_keys(x, grad, pair_copies[1]).astype(BF16)
    grad_own[0].start()
    late.hop(2)
    q_sum_out[...] = late.result()
    early.sent()
    late.sent()
    for copies in pair_copies:
        for copy in copies:
            copy.wait_send()

    @pl.when(core == 1)
    def _():
        for copy in short_core:
            copy.wait_send()

    @pl.when((x == 1) & (core == 0))
    def _():
        for copy in short_x:
            copy.wait_send()

    for copy in grad_own:
        copy.wait()
    grad_home.wait()


def back(queries, keys_values, turned, attended, grad_attended, gres, qkv_full, sums_mid, sums_hidden, dp_count):
    rows, width = attended.shape
    tile = rows // 3
    z_count = dp_count // 2
    heads = width // HEAD_DIM
    whole = pl.BlockSpec(memory_space=pltpu.VMEM)
    out, dma, vmem = jax.ShapeDtypeStruct, pltpu.SemaphoreType.DMA, pltpu.VMEM
    return pl.pallas_call(
        functools.partial(back_kernel, z_count, tile),
        out_shape=[out((3, tile, width), BF16), out((16, width), F32), out((8, width), F32)],
        in_specs=[ANY] * 7 + [whole] * 2,
        out_specs=[ANY, whole, whole],
        scratch_shapes=[
            vmem((heads, rows, LANES), BF16),
            vmem((heads, 5 * tile, LANES), BF16),
            vmem((heads, 5 * tile, LANES), BF16),
            vmem((heads // 2, LANES, 5 * tile), BF16),
            vmem((rows, width), BF16),
            vmem((rows, width), BF16),
            vmem((heads, rows, LANES), BF16),
            vmem((rows, width), F32),
            vmem((24, 128, width), BF16),
            vmem((3, tile, width), BF16),
            vmem((5, tile, width), BF16),
            vmem((5, tile, width), BF16),
            vmem((width, tile), F32),
            vmem((4 * tile, width), F32),
            vmem((4 * tile, width), F32),
            vmem((2, 2, tile, width), BF16),
            vmem((2, 2, tile, width), BF16),
            vmem((2, tile, width), BF16),
            vmem((3, tile, width), BF16),
            vmem((4, 16, width), F32),
            vmem((3, 16, width), F32),
            vmem((z_count, 16, width), F32),
            vmem((4, 8, width), F32),
            vmem((3, 8, width), F32),
            vmem((z_count, 8, width), F32),
            vmem((1, width), F32),
            dma((13 + 3 * z_count,)),
            dma((2, 2)),
            dma((2, 2)),
            dma((2, 2)),
            dma((2, 2)),
            dma((1,)),
            dma((1,)),
            dma((2 + z_count,)),
            dma((2 + z_count,)),
            dma((2 + z_count,)),
            dma((2 + z_count,)),
            dma((2,)),
        ],
        compiler_params=params(63, collective_id=1, has_side_effects=True),
        name="back",
    )(
        queries,
        keys_values.reshape(2, heads, 5 * tile, LANES),
        turned,
        attended,
        grad_attended,
        gres,
        qkv_full,
        sums_mid,
        sums_hidden,
    )


def paired_chips(
    tokens,
    out_cotangent,
    lengths,
    qkv_weight,
    out_weight,
    ffn_in_weight,
    ffn_out_weight,
    qv_bias,
    out_bias,
    ln1_gain,
    ln1_bias,
    ffn_in_bias,
    ffn_out_bias,
    ln2_gain,
    ln2_bias,
    dp_count,
):
    hidden = ffn_in_bias.shape[0]
    tok, cot, perm, lens = sort_sequences(lengths, tokens, out_cotangent)
    shards = (qkv_weight, out_weight, ffn_in_weight, ffn_out_weight)
    vectors = (out_bias, ln1_gain, ln1_bias, ffn_out_bias, ln2_gain, ln2_bias)
    results = main(lens, shards, tok, cot, qv_bias, vectors, ffn_in_bias, dp_count)
    qkv_full = results[0]
    queries, keys_values, turned, attended, out_sorted, gres, grad_attended, sums_mid, sums_hidden = results[1:]
    grad_sorted, sums, q_sums = back(
        queries, keys_values, turned, attended, grad_attended, gres, qkv_full, sums_mid, sums_hidden, dp_count
    )
    return tuple(unsort_sequences(perm, out_sorted, grad_sorted, sums, q_sums, hidden))


def body_for(mesh):
    dp_count, head_count = mesh.shape["dp"], mesh.shape["head"]

    def body(*arrays):
        tokens = arrays[0]
        seqs, tile, width = tokens.shape
        fits = head_count == 4 and seqs == 3 and dp_count % 2 == 0 and width == 1024 and tile == 256
        if fits:
            return paired_chips(*arrays, dp_count)
        return on_device(*arrays)

    return body


def solution(mesh):
    return jax.shard_map(
        body_for(mesh),
        mesh=mesh,
        in_specs=(
            P("dp", "head", None),
            P("dp", "head", None),
            P("dp"),
            P("dp", None),
            P("dp", None),
            P("dp", None),
            P("dp", None),
            P(),
            P(),
            P(),
            P(),
            P(),
            P(),
            P(),
            P(),
        ),
        out_specs=(P("dp", "head", None), P("dp", "head", None), P(), P(), P(), P(), P(), P()),
        check_vma=False,
    )
```

```python
import functools
import math

import jax
import jax.numpy as jnp
from jax import lax
from jax.experimental import pallas as pl
from jax.experimental.pallas import tpu as pltpu
from jax.sharding import PartitionSpec as P

HEAD_DIM = 64


epsilon = 1e-12


def layer_norm(inputs, gain, shift):
    centre = inputs - jnp.mean(inputs, axis=-1, keepdims=True)
    spread = jnp.mean(centre * centre, axis=-1, keepdims=True)
    return centre * lax.rsqrt(spread + epsilon) * gain + shift


def gelu_exact(inputs):
    return 0.5 * inputs * (1.0 + jax.scipy.special.erf(inputs * 0.7071067811865476))


def back_product(grads, weight):
    return lax.dot_general(
        grads, weight, (((1,), (1,)), ((), ())), preferred_element_type=jnp.float32
    )


def on_device(
    tokens,
    out_cotangent,
    lengths,
    qkv_weight,
    out_weight,
    ffn_in_weight,
    ffn_out_weight,
    qv_bias,
    out_bias,
    ln1_gain,
    ln1_bias,
    ffn_in_bias,
    ffn_out_bias,
    ln2_gain,
    ln2_bias,
):
    seqs_here, tok_part, width = tokens.shape
    row_count = seqs_here * tok_part
    flat_rows = tokens.reshape(row_count, width)
    gathered = (
        lax.all_gather(qkv_weight, "dp", axis=0, tiled=True),
        lax.all_gather(out_weight, "dp", axis=0, tiled=True),
        lax.all_gather(ffn_in_weight, "dp", axis=0, tiled=True),
        lax.all_gather(ffn_out_weight, "dp", axis=0, tiled=True),
    )
    qkv_full, attn_full, first_full, second_full = gathered
    projected = jnp.dot(flat_rows, qkv_full, preferred_element_type=jnp.float32)
    tok_shape = (seqs_here, tok_part, width)
    queries = (projected[:, :width] + qv_bias[0]).astype(jnp.bfloat16).reshape(tok_shape)
    keys_tok = projected[:, width : 2 * width].astype(jnp.bfloat16).reshape(tok_shape)
    values_tok = (projected[:, 2 * width :] + qv_bias[1]).astype(jnp.bfloat16).reshape(tok_shape)
    head_q, head_k, head_v = (
        lax.all_to_all(queries, "head", split_axis=2, concat_axis=1, tiled=True),
        lax.all_to_all(keys_tok, "head", split_axis=2, concat_axis=1, tiled=True),
        lax.all_to_all(values_tok, "head", split_axis=2, concat_axis=1, tiled=True),
    )
    seq_len = head_q.shape[1]
    head_part = head_q.shape[2]
    local_heads = head_part // HEAD_DIM
    block_rows = min(512, seq_len)
    block_count = seq_len // block_rows
    score_scale = 1.0 / math.sqrt(HEAD_DIM)
    head_shape = (seqs_here, seq_len, local_heads, HEAD_DIM)
    query_heads = head_q.reshape(head_shape)
    key_heads = head_k.reshape(head_shape)
    value_heads = head_v.reshape(head_shape)
    key_index = lax.iota(jnp.int32, seq_len)

    def seq_forward(seq_items):
        query_seq, key_seq, value_seq, length = seq_items
        visible = key_index < length
        query_blocks = query_seq.reshape(block_count, block_rows, local_heads, HEAD_DIM)

        def block_forward(query_block):
            scores = (
                jnp.einsum("qhd,khd->hqk", query_block, key_seq, preferred_element_type=jnp.float32)
                * score_scale
            )
            scores = jnp.where(visible[None, None, :], scores, -1000000000.0)
            highest = jnp.max(scores, axis=-1, keepdims=True)
            raised = jnp.exp(scores - highest)
            totals = jnp.sum(raised, axis=-1, keepdims=True)
            attn_probs = (raised / totals).astype(jnp.bfloat16)
            attended = jnp.einsum(
                "hqk,khd->qhd", attn_probs, value_seq, preferred_element_type=jnp.float32
            )
            return (attended.astype(jnp.bfloat16), (highest + jnp.log(totals))[:, :, 0])

        attended, log_block = lax.map(block_forward, query_blocks)
        return (attended.reshape(seq_len, head_part), log_block)

    head_out, log_totals = lax.map(seq_forward, (query_heads, key_heads, value_heads, lengths))
    tok_attn = lax.all_to_all(head_out, "head", split_axis=1, concat_axis=2, tiled=True)
    branch = (
        jnp.dot(tok_attn.reshape(row_count, width), attn_full, preferred_element_type=jnp.float32)
        + out_bias
    )
    residual_one = flat_rows.astype(jnp.float32) + branch
    normed_one, norm_one_back = jax.vjp(
        lambda inputs: layer_norm(inputs, ln1_gain, ln1_bias), residual_one
    )
    hidden = (
        jnp.dot(normed_one.astype(jnp.bfloat16), first_full, preferred_element_type=jnp.float32)
        + ffn_in_bias
    )
    active, gelu_back = jax.vjp(gelu_exact, hidden)
    ffn_out = (
        jnp.dot(active.astype(jnp.bfloat16), second_full, preferred_element_type=jnp.float32)
        + ffn_out_bias
    )
    result, norm_two_back = jax.vjp(
        lambda inputs: layer_norm(inputs, ln2_gain, ln2_bias), normed_one + ffn_out
    )
    layer_output = result.astype(jnp.bfloat16).reshape(tok_shape)
    qkv_back, attn_back, first_back, second_back = (
        lax.all_gather(qkv_weight, "dp", axis=0, tiled=True),
        lax.all_gather(out_weight, "dp", axis=0, tiled=True),
        lax.all_gather(ffn_in_weight, "dp", axis=0, tiled=True),
        lax.all_gather(ffn_out_weight, "dp", axis=0, tiled=True),
    )
    grad_out = out_cotangent.reshape(row_count, width).astype(jnp.float32)
    grad_ln2_bias = jnp.sum(grad_out, axis=0)
    (grad_res_two,) = norm_two_back(grad_out)
    grad_ffn_out = grad_res_two.astype(jnp.bfloat16)
    grad_ffn_out_bias = jnp.sum(grad_ffn_out.astype(jnp.float32), axis=0)
    grad_active = back_product(grad_ffn_out, second_back)
    (grad_hidden,) = gelu_back(grad_active)
    grad_hidden = grad_hidden.astype(jnp.bfloat16)
    grad_ffn_in_bias = jnp.sum(grad_hidden.astype(jnp.float32), axis=0)
    grad_normed = back_product(grad_hidden, first_back) + grad_res_two
    grad_ln1_bias = jnp.sum(grad_normed, axis=0)
    (grad_res_one,) = norm_one_back(grad_normed)
    grad_branch = grad_res_one.astype(jnp.bfloat16)
    grad_out_bias = jnp.sum(grad_branch.astype(jnp.float32), axis=0)
    grad_attended = back_product(grad_branch, attn_back).astype(jnp.bfloat16).reshape(tok_shape)
    grad_heads = lax.all_to_all(
        grad_attended, "head", split_axis=2, concat_axis=1, tiled=True
    ).reshape(head_shape)

    def seq_backward(seq_items):
        query_seq, key_seq, value_seq, grad_seq, log_seq, length = seq_items
        visible = key_index < length
        query_blocks = query_seq.reshape(block_count, block_rows, local_heads, HEAD_DIM)
        grad_blocks = grad_seq.reshape(block_count, block_rows, local_heads, HEAD_DIM)

        def block_backward(carry, block_items):
            key_acc, value_acc = carry
            query_block, grad_block, log_block = block_items
            scores = (
                jnp.einsum("qhd,khd->hqk", query_block, key_seq, preferred_element_type=jnp.float32)
                * score_scale
            )
            scores = jnp.where(visible[None, None, :], scores, -1000000000.0)
            attn_probs = jnp.exp(scores - log_block[:, :, None])
            grad_probs = jnp.einsum(
                "qhd,khd->hqk", grad_block, value_seq, preferred_element_type=jnp.float32
            )
            centre = jnp.sum(attn_probs * grad_probs, axis=-1, keepdims=True)
            grad_scores = (attn_probs * (grad_probs - centre)).astype(jnp.bfloat16)
            grad_query = (
                jnp.einsum("hqk,khd->qhd", grad_scores, key_seq, preferred_element_type=jnp.float32)
                * score_scale
            )
            key_acc = key_acc + jnp.einsum(
                "hqk,qhd->khd", grad_scores, query_block, preferred_element_type=jnp.float32
            )
            value_acc = value_acc + jnp.einsum(
                "hqk,qhd->khd",
                attn_probs.astype(jnp.bfloat16),
                grad_block,
                preferred_element_type=jnp.float32,
            )
            return ((key_acc, value_acc), grad_query.astype(jnp.bfloat16))

        zero_acc = jnp.zeros((seq_len, local_heads, HEAD_DIM), jnp.float32)
        (key_acc, value_acc), grad_queries = lax.scan(
            block_backward, (zero_acc, zero_acc), (query_blocks, grad_blocks, log_seq)
        )
        return (
            grad_queries.reshape(seq_len, head_part),
            (key_acc * score_scale).astype(jnp.bfloat16).reshape(seq_len, head_part),
            value_acc.astype(jnp.bfloat16).reshape(seq_len, head_part),
        )

    grad_q_heads, grad_k_heads, grad_v_heads = lax.map(
        seq_backward, (query_heads, key_heads, value_heads, grad_heads, log_totals, lengths)
    )
    grad_q_tok, grad_k_tok, grad_v_tok = (
        lax.all_to_all(grad_q_heads, "head", split_axis=1, concat_axis=2, tiled=True),
        lax.all_to_all(grad_k_heads, "head", split_axis=1, concat_axis=2, tiled=True),
        lax.all_to_all(grad_v_heads, "head", split_axis=1, concat_axis=2, tiled=True),
    )
    grad_q_rows = grad_q_tok.reshape(row_count, width)
    grad_k_rows = grad_k_tok.reshape(row_count, width)
    grad_v_rows = grad_v_tok.reshape(row_count, width)
    grad_input = (
        grad_res_one
        + back_product(grad_q_rows, qkv_back[:, :width])
        + back_product(grad_k_rows, qkv_back[:, width : 2 * width])
        + back_product(grad_v_rows, qkv_back[:, 2 * width :])
    )
    grad_qv = jnp.stack(
        [
            jnp.sum(grad_q_rows.astype(jnp.float32), axis=0),
            jnp.sum(grad_v_rows.astype(jnp.float32), axis=0),
        ]
    )
    bias_totals = lax.psum(
        (grad_qv, grad_out_bias, grad_ln1_bias, grad_ffn_in_bias, grad_ffn_out_bias, grad_ln2_bias),
        ("dp", "head"),
    )
    return (
        layer_output,
        grad_input.astype(jnp.bfloat16).reshape(tok_shape),
        bias_totals[0],
        bias_totals[1],
        bias_totals[2],
        bias_totals[3],
        bias_totals[4],
        bias_totals[5],
    )


MESH_IDS = pl.DeviceIdType.MESH
BF16, F32 = jnp.bfloat16, jnp.float32
ANY = pl.BlockSpec(memory_space=pl.ANY)
LANES = 128
COT_PIECES = 8
NT = (((1,), (1,)), ((), ()))


def mm(left, right):
    return jnp.dot(left, right, preferred_element_type=F32)


def mm_nt(left, right):
    return lax.dot_general(left, right, NT, preferred_element_type=F32)


def whole(shape, memory_space=pltpu.VMEM):
    return pl.BlockSpec(memory_space=memory_space)


def params(vmem, **more):
    return pltpu.CompilerParams(vmem_limit_bytes=vmem << 20, **more)


def relay(jobs, held, sems):
    ways = [
        [pltpu.make_async_copy(src, held.at[i], sems.at[0, i]), pltpu.make_async_copy(held.at[i], dst, sems.at[1, i])]
        for i, (src, dst) in enumerate(jobs)
    ]
    for way in ways:
        way[0].start()
    for way in ways:
        way[0].wait()
        way[1].start()
    return [way[1] for way in ways]


def relay_scratch(array):
    count = 4 * array.shape[0]
    shape = (count, array.shape[1] // 2, *array.shape[2:])
    return [pltpu.VMEM(shape, array.dtype), pltpu.SemaphoreType.DMA((2, count))]


def halves(src, dst):
    rows = src.shape[0] // 2
    return [(src.at[pl.ds(i * rows, rows)], dst.at[pl.ds(i * rows, rows)]) for i in range(2)]


def unsort_kernel(perm, layer, grad, sums, q_sums, layer_out, grad_out, qv, *rest):
    biases, (held, sems) = rest[:-2], rest[-2:]
    jobs = []
    for i in range(layer.shape[0]):
        jobs += halves(layer.at[perm[i]], layer_out.at[i]) + halves(grad.at[perm[i]], grad_out.at[i])
    copies = relay(jobs, held, sems)
    width = sums.shape[1]
    qv[0:1, :] = q_sums[0:1, :]
    qv[1:2, :] = sums[1:2, :]
    row = 2
    for bias in biases:
        for at in range(bias.shape[0] // width):
            bias[pl.ds(at * width, width)] = sums[row, :]
            row += 1
    for copy in copies:
        copy.wait()


def unsort_sequences(perm, layer, grad, sums, q_sums, hidden):
    whole = pl.BlockSpec(memory_space=pltpu.VMEM)
    out = jax.ShapeDtypeStruct
    count, width = layer.shape[0], layer.shape[2]
    sizes = (width, width, hidden, width, width)
    return pl.pallas_call(
        unsort_kernel,
        out_shape=[out(layer.shape, BF16), out(grad.shape, BF16), out((2, width), F32)]
        + [out((size,), F32) for size in sizes],
        in_specs=[pl.BlockSpec(memory_space=pltpu.SMEM), ANY, ANY, whole, whole],
        out_specs=[ANY, ANY] + [whole] * 6,
        scratch_shapes=relay_scratch(layer),
        name="unsort",
    )(perm, layer, grad, sums, q_sums)


class Place:
    def __init__(self, z_count):
        self.dp, self.head = lax.axis_index("dp"), lax.axis_index("head")
        self.z, self.y = self.dp // 2, self.dp % 2
        self.x, self.core = self.head // 2, self.head % 2
        self.z_count = z_count

    def at_z(self, z):
        return (z * 2 + self.y, self.head)

    def along_z(self, step):
        return self.at_z((self.z + step) % self.z_count)

    def other_y(self):
        return (self.z * 2 + (1 - self.y), self.head)

    def other_x(self):
        return (self.dp, (1 - self.x) * 2 + self.core)

    def other_core(self):
        return (self.dp, self.x * 2 + (1 - self.core))

    def shifted(self, shift_z, shift_y):
        return (((self.z + shift_z) % self.z_count) * 2 + (self.y + shift_y) % 2, self.head)

    def beside(self, shift_x, shift_core):
        return (self.dp, ((self.x + shift_x) % 2) * 2 + (self.core + shift_core) % 2)

    def peers(self):
        steps = [self.along_z(step) for step in range(1, self.z_count)]
        return steps + [self.other_y(), self.other_x(), self.other_core()]

    def more_peers(self):
        steps = [self.shifted(z, y) for z in range(self.z_count) for y in range(2)][1:]
        return steps + [self.beside(x, core) for x in range(2) for core in range(2)][1:]


def meet(peers):
    barrier = pltpu.get_barrier_semaphore()
    for peer in peers:
        pl.semaphore_signal(barrier, inc=1, device_id=peer, device_id_type=MESH_IDS)
    pl.semaphore_wait(barrier, len(peers))


def push(src, dst, send, recv, target):
    return pltpu.make_async_remote_copy(
        src_ref=src, dst_ref=dst, send_sem=send, recv_sem=recv, device_id=target, device_id_type=MESH_IDS
    )


class Gather:
    def __init__(self, place, chunks, sems):
        z_send, z_recv, y_send, y_recv, h_send, h_recv, local = sems
        x, core, z, y = place.x, place.core, place.z, place.y
        near, across, far = z + 1 - 2 * (z % 2), (z + 2) % 4, 3 - z
        inner = 1 - ((z - 1) * (z - 2)) // 2
        self.inner = inner == 1
        second = near + inner * (far - near)
        fourth = far + inner * (near - far)
        passed = z + inner * (across - z)
        at = place.at_z
        self.plans = []
        for number, (shard, full, row, rows, col, cols, direct) in enumerate(chunks):
            base = row + core * (rows // 2)
            half = pl.ds(pl.multiple_of(base, 16), rows // 2)
            role = half if direct else pl.ds(pl.multiple_of(base + x * (rows // 8), 16), rows * 3 // 8)
            own = pl.ds(pl.multiple_of(base + x * (rows * 3 // 8), 16), rows // 8)
            span = pl.ds(col, cols)
            left, right = pl.ds(col, cols // 2), pl.ds(col + cols // 2, cols // 2)
            mine, there = shard.at[role, span], full.at[z, y, role, span]

            def along(index, src, dst, target):
                slot = min(index, 2)
                return push(src, dst, z_send.at[number, index], z_recv.at[number, slot], target)

            def beside(index, which, columns):
                view = full.at[which, y, role, columns]
                src = mine if index == 0 else view
                return push(src, view, y_send.at[number, index], y_recv.at[number, index], place.other_y())

            def hop(index, view, target):
                return push(view, view, h_send.at[number, index], h_recv.at[number, index], target)

            handed = full.at[across, y, role, span]
            self.plans.append(
                {
                    "here": pltpu.make_async_copy(mine, there, local.at[number]),
                    "near": along(0, mine, there, at(near)),
                    "across": along(1, mine, there, at(across)),
                    "far": along(2, mine, there, at(far)),
                    "handed": along(3, handed, handed, at(near)),
                    "y": [
                        beside(0, z, span),
                        beside(1, across, span),
                        beside(2, second, span),
                        beside(3, fourth, left),
                    ],
                    "passed": hop(0, full.at[passed, 1 - y, role, right], at(near)),
                    "x": None if direct else hop(1, full.at[:, :, own, span], place.other_x()),
                    "core": hop(2, full.at[:, :, half, span], place.other_core()),
                }
            )
        self.count = len(self.plans)

    def late(self, number):
        return 1 if 6 <= number < self.count - 4 else 0

    def begin(self, number):
        plan = self.plans[number]
        for copy in (plan["near"], plan["across"], plan["y"][0], plan["here"]):
            copy.start()

        @pl.when(self.inner)
        def _():
            plan["far"].start()

    def step(self, step):
        if step == 0:
            self.begin(0)
        if step + 1 < self.count:
            self.begin(step + 1)
        if 0 <= step - 1 < self.count:
            plan = self.plans[step - 1]
            plan["near"].wait_recv()
            plan["across"].wait_recv()

            @pl.when(self.inner)
            def _():
                plan["far"].wait_recv()
                plan["handed"].start()

            plan["here"].wait()
            plan["y"][1].start()
            plan["y"][2].start()
        for number, plan in enumerate(self.plans):
            late = self.late(number)
            if step == number + 2 + late:
                plan["y"][0].wait_recv()
                plan["y"][1].wait_recv()
                plan["passed"].start()

                @pl.when(jnp.logical_not(self.inner))
                def _():
                    plan["far"].wait_recv()

                plan["y"][3].start()
            if step == number + 3 + 2 * late:
                plan["y"][2].wait_recv()
                plan["y"][3].wait_recv()
                plan["passed"].wait_recv()
                if plan["x"] is not None:
                    plan["x"].start()
            if step == number + 4 + 3 * late:
                if plan["x"] is not None:
                    plan["x"].wait_recv()
                plan["core"].start()

    def arrived(self, number):
        self.plans[number]["core"].wait_recv()

    def sent(self, first, last):
        for plan in self.plans[first:last]:
            copies = [plan["near"], plan["across"], *plan["y"], plan["passed"], plan["core"]]
            for copy in copies if plan["x"] is None else copies + [plan["x"]]:
                copy.wait_send()

            @pl.when(self.inner)
            def _():
                plan["far"].wait_send()
                plan["handed"].wait_send()


def lane_row(pick):
    lane = lax.broadcasted_iota(jnp.int32, (1, LANES), 1)
    return jnp.where(pick(lane), 1.0, 0.0).astype(F32)


def head_lanes(half):
    return lane_row(lambda lane: (lane >= half * HEAD_DIM) & (lane < (half + 1) * HEAD_DIM))


def spare_lane(half, index):
    return (1 - half) * HEAD_DIM + index


def spare(half, index):
    return lane_row(lambda lane: lane == spare_lane(half, index))


def split_three(value):
    high = value.astype(BF16).astype(F32)
    rest = value - high
    middle = rest.astype(BF16).astype(F32)
    return high, middle, rest - middle


def mask_column(length, keys):
    return jnp.where(lax.broadcasted_iota(jnp.int32, (keys, 1), 0) < length, 0.0, -1000000000.0)


def attend(tile, pair, q_tmp, kv_ext, key_at, value_at, q_ext, att):
    columns = pl.ds(pl.multiple_of(pair * LANES, LANES), LANES)
    for block in range(3):
        q_rows = pl.ds(block * tile, tile)
        outs = []
        for half in range(2):
            head = 2 * pair + half
            query = q_tmp[q_rows, columns].astype(F32) * head_lanes(half) + spare(half, 3)
            scores = mm_nt(query.astype(BF16), kv_ext[key_at(head, block), :])
            highest = jnp.max(scores, axis=-1, keepdims=True)
            raised = jnp.exp(scores - highest).astype(BF16)
            summed = mm(raised, kv_ext[value_at(head, block), :])
            outs.append(summed / pltpu.roll(summed, HEAD_DIM, 1))
            column = spare_lane(half, 0)
            log_total = highest + jnp.log(summed[:, column : column + 1])
            high, middle, low = split_three(-log_total)
            query = query + high * spare(half, 0) + middle * spare(half, 1) + low * spare(half, 2)
            q_ext[head, q_rows, :] = query.astype(BF16)
        att[q_rows, columns] = jnp.where(head_lanes(0) > 0, outs[0], outs[1]).astype(BF16)


def row_mean(value):
    return jnp.mean(value, axis=-1, keepdims=True)


def normalise(value):
    centre = value - row_mean(value)
    rstd = lax.rsqrt(row_mean(centre * centre) + epsilon)
    return centre * rstd, rstd


def normalise_back(grad, normal, rstd):
    return rstd * (grad - row_mean(grad) - normal * row_mean(grad * normal))


def column_sum(value):
    return jnp.sum(value.astype(F32), axis=0, keepdims=True)


def slot_table():
    names = ("k0", "v0", "q0", "a00", "a01", "a02", "a03", "k1", "v1", "a10", "a11", "a12", "a13", "o")
    names = names + ("u0", "u1", "u2", "u3", "u4", "u5", "u6", "w0", "w1", "w2")
    table = {name: [4 + i] for i, name in enumerate(names)}
    return table


def main_kernel(z_count, tile, chunks_of, *refs):
    lengths, refs = refs[0], refs[1:]
    shards, (tok, cot, qv_bias, b1_ref), vectors, refs = refs[:4], refs[4:8], refs[8:14], refs[14:]
    perm_ref, refs = refs[0], refs[1:]
    (wqkv_hbm, q_hbm, kv_hbm, turn_hbm, o_hbm, layer_hbm, gres_hbm, gatt_hbm, sums_ref, sums1_ref), refs = (
        refs[:10],
        refs[10:],
    )
    (tok_v, own_v, cot_v, tok_give, cot_give, big, wo, w1, w2, q_tmp, kv_ext, k_turn, q_ext, att, norm1, spread1, acc, low), refs = (
        refs[:18],
        refs[18:],
    )
    sems, (t_send, t_recv, t_local, c_send, c_recv, store) = refs[:7], refs[7:]
    place = Place(z_count)
    x, core = place.x, place.core
    width = att.shape[1]
    hidden = b1_ref.shape[0]
    keep = 2 - x
    seqs = tok.shape[0]
    ranks = []
    for i in range(seqs):
        rank = 0
        for j in range(seqs):
            if j != i:
                before = lengths[j] <= lengths[i] if j < i else lengths[j] < lengths[i]
                rank = rank + before.astype(jnp.int32)
        ranks.append(rank)
        perm_ref[i] = rank
    length = sum(jnp.where(ranks[i] == keep, lengths[i], 0) for i in range(seqs))
    raw_tok = [pltpu.make_async_copy(tok.at[i], att.at[pl.ds(i * tile, tile)], t_local.at[i]) for i in range(seqs)]
    raw_cot = [pltpu.make_async_copy(cot.at[i], low.at[pl.ds(i * tile, tile)], t_local.at[3 + i]) for i in range(seqs)]
    for copy in raw_tok + raw_cot:
        copy.start()

    def pick(raw, place_in_order):
        rows = raw[0:tile, :]
        for i in range(1, seqs):
            rows = jnp.where(ranks[i] == place_in_order, raw[i * tile : (i + 1) * tile, :], rows)
        return rows

    meet(place.peers())
    comm = Gather(place, chunks_of(shards, (big, wo, w1, w2)), sems)
    comm.step(0)

    first = (x == 0) & (core == 0)
    tok_x = push(tok_give, tok_v.at[2 * x + core], t_send.at[0], t_recv.at[0], place.other_x())
    tok_core = [
        push(tok_v.at[2 * i + core], tok_v.at[2 * i + core], t_send.at[1 + i], t_recv.at[1 + i], place.other_core())
        for i in range(2)
    ]
    cot_rows = [pl.ds(i * (tile // COT_PIECES), tile // COT_PIECES) for i in range(COT_PIECES)]
    cot_x = [
        push(cot_give.at[rows], cot_v.at[x, rows], c_send.at[i], c_recv.at[i], place.other_x())
        for i, rows in enumerate(cot_rows)
    ]
    short_x = push(own_v, tok_v.at[4], t_send.at[4], t_recv.at[4], place.other_x())
    short_core = push(tok_v.at[4], tok_v.at[4], t_send.at[5], t_recv.at[5], place.other_core())
    for copy in raw_tok:
        copy.wait()
    tok_give[...] = pick(att, 1 + x)
    tok_x.start()
    own_v[...] = pick(att, 0)

    @pl.when(first)
    def _():
        short_x.start()
        tok_v[4] = own_v[...]

    tok_v[2 * x + core] = pick(att, keep)
    comm.step(1)
    tok_x.wait_recv()
    for copy in tok_core:
        copy.start()

    @pl.when((x == 1) & (core == 0))
    def _():
        short_x.wait_recv()

    @pl.when(core == 0)
    def _():
        short_core.start()

    comm.step(2)
    for copy in raw_cot:
        copy.wait()
    cot_give[...] = pick(low, 1 + x)
    cot_v[x] = pick(low, keep)
    cot_v[2] = pick(low, 0)
    comm.step(3)
    slots = slot_table()

    def slot(name):
        for step in slots.get(name, ()):
            comm.step(step)
            if step >= 8 and step % 2 == 0 and step // 2 - 4 < COT_PIECES:
                cot_x[step // 2 - 4].start()

    part_cols = width // 2

    def qkv_part(part, which):
        start = pl.multiple_of(part * width + which * part_cols, part_cols)
        return big[:, :, :, pl.ds(start, part_cols)].reshape(width, part_cols)

    keys_count = 5 * tile

    def key_at(head, block):
        start, count = (4 * tile, tile) if block == 2 else (0, 4 * tile)
        return pl.ds(pl.multiple_of(head * keys_count + start, tile), count)

    def value_at(head, block):
        start, count = (4 * tile, tile) if block == 2 else (0, 4 * tile)
        return pl.ds(pl.multiple_of((width // HEAD_DIM + head) * keys_count + start, tile), count)

    def lanes_of(pair):
        return pl.ds(pl.multiple_of(pair * LANES, LANES), LANES)

    def project_keys(side, which, block):
        value = mm(tok_v[block], qkv_part(1, which)).astype(BF16).astype(F32)
        row = lax.broadcasted_iota(jnp.int32, (tile, 1), 0) + block * tile
        hidden_keys = jnp.where((row < length) | (block == 4), 0.0, -1000000000.0)
        for i in range(part_cols // LANES):
            pair = which * (part_cols // LANES) + i
            both = value[:, i * LANES : (i + 1) * LANES]
            for half in range(2):
                ones = spare(half, 0) + spare(half, 1) + spare(half, 2)
                key = both * head_lanes(half) + ones + hidden_keys * spare(half, 3)
                at = (2 * pair + half) * keys_count + block * tile
                kv_ext[pl.ds(pl.multiple_of(at, tile), tile), :] = key.astype(BF16)
            k_turn[pair, :, pl.ds(pl.multiple_of(block * tile, tile), tile)] = both.T.astype(BF16)

    def project_values(side, which, block):
        value = mm(tok_v[block], qkv_part(2, which))
        value = (value + qv_bias[1:2, side]).astype(BF16).astype(F32)
        for i in range(part_cols // LANES):
            pair = which * (part_cols // LANES) + i
            both = value[:, i * LANES : (i + 1) * LANES]
            for half in range(2):
                mine = head_lanes(half)
                at = (width // HEAD_DIM + 2 * pair + half) * keys_count + block * tile
                kv_ext[pl.ds(pl.multiple_of(at, tile), tile), :] = (both * mine + (1.0 - mine)).astype(BF16)

    scale = 1.0 / math.sqrt(HEAD_DIM)
    half_rows = kv_ext.shape[0] // 4
    kv_stores = [
        [
            pltpu.make_async_copy(
                kv_ext.at[pl.ds((2 * kind + at) * half_rows, half_rows)],
                kv_hbm.at[pl.ds((2 * kind + at) * half_rows, half_rows)],
                store.at[2 * at + kind],
            )
            for kind in range(2)
        ]
        for at in range(2)
    ]

    stores = [
        pltpu.make_async_copy(src, dst, store.at[4 + i])
        for i, (src, dst) in enumerate(((big, wqkv_hbm), (k_turn, turn_hbm), (q_ext, q_hbm), (att, o_hbm)))
    ]

    def heads_half(which, _):
        side = pl.ds(pl.multiple_of(which * part_cols, part_cols), part_cols)
        for at in range(2):

            @pl.when(which == at)
            def _():
                slot(f"k{at}")
                comm.arrived(3 * at)
                if at == 0:
                    for copy in tok_core:
                        copy.wait_recv()

                    @pl.when(core == 1)
                    def _():
                        short_core.wait_recv()

        def keys_block(block, _):
            project_keys(side, which, block)
            return 0

        lax.fori_loop(0, 5, keys_block, 0)
        for at in range(2):

            @pl.when(which == at)
            def _():
                slot(f"v{at}")
                comm.arrived(3 * at + 1)

        def values_block(block, _):
            project_values(side, which, block)
            return 0

        lax.fori_loop(0, 5, values_block, 0)
        for at in range(2):

            @pl.when(which == at)
            def _():
                slot(f"q{at}")
                comm.arrived(3 * at + 2)
                if at == 1:
                    stores[0].start()

        for block in range(3):
            rows = own_v[...] if block == 2 else tok_v[2 * block + core]
            query = (mm(rows, qkv_part(0, which)) + qv_bias[0:1, side]).astype(BF16).astype(F32) * scale
            q_tmp[block * tile : (block + 1) * tile, side] = query.astype(BF16)

        for at in range(2):

            @pl.when(which == at)
            def _():
                for copy in kv_stores[at]:
                    copy.start()

        def pair_step(i, _):
            for at in range(2):
                for j in range(part_cols // LANES):
                    if f"a{at}{j}" in slots:

                        @pl.when((which == at) & (i == j))
                        def _():
                            slot(f"a{at}{j}")

            attend(tile, which * (part_cols // LANES) + i, q_tmp, kv_ext, key_at, value_at, q_ext, att)
            return 0

        lax.fori_loop(0, part_cols // LANES, pair_step, 0)
        return 0

    lax.fori_loop(0, 2, heads_half, 0)
    for copy in stores[1:]:
        copy.start()

    bo, g1, s1, b2, g2, s2 = (vector[...].reshape(1, width) for vector in vectors)
    slot("o")
    comm.arrived(6)
    comm.arrived(7)
    for block in range(3):
        rows = pl.ds(block * tile, tile)
        token = own_v[...] if block == 2 else tok_v[2 * block + core]
        branch = mm(att[rows, :], wo[...].reshape(width, width)) + bo
        normal, rstd = normalise(token.astype(F32) + branch)
        norm1[rows, :] = normal
        spread1[rows, :] = jnp.broadcast_to(rstd, (tile, LANES))
        low[rows, :] = (normal * g1 + s1).astype(BF16)
        acc[rows, :] = jnp.zeros((tile, width), F32)

    block_width = w2.shape[2]
    blocks = hidden // block_width
    per = width // block_width
    def w1_piece(index):
        span = pl.ds(pl.multiple_of(index * block_width, block_width), block_width)
        return w1[:, :, :, span].reshape(width, block_width)

    def slope_at(index, block, part):
        return index // 2, index % 2, slice(None), pl.ds((2 * block + part) * block_width, block_width)

    def up(index, _):
        for i in range(blocks):

            @pl.when(index == i)
            def _():
                slot(f"u{i}")
                comm.arrived(8 + i)
                if i == 0:
                    stores[0].wait()
                    for copy in kv_stores[0] + kv_stores[1]:
                        copy.wait()
                    comm.sent(0, 6)

        span = pl.ds(pl.multiple_of(index * block_width, block_width), block_width)
        first_piece = w1_piece(index)
        bias = b1_ref[span].reshape(1, block_width)
        for block in range(3):
            rows = pl.ds(block * tile, tile)
            value = mm(low[rows, :], first_piece) + bias
            share = 0.5 * (1.0 + lax.erf(value * 0.7071067811865476))
            slope = share + value * (0.3989422804014327 * jnp.exp(-0.5 * value * value))
            for part in range(2):
                big[slope_at(index, block, part)] = slope[part * 128 : (part + 1) * 128].astype(BF16)
            active = (value * share).astype(BF16)
            for part in range(block_width // 128):
                at = (part * blocks + index) * (3 * tile) + block * tile
                kv_ext[pl.ds(pl.multiple_of(at, tile), tile), :] = active[:, part * 128 : (part + 1) * 128]
        return 0

    lax.fori_loop(0, blocks, up, 0)

    def widen(part, _):
        for i in range(block_width // 128):

            @pl.when(part == i)
            def _():
                slot(f"w{i}")
                comm.arrived(8 + blocks + 2 * i)
                comm.arrived(9 + blocks + 2 * i)

        second = w2[:, :, pl.ds(pl.multiple_of(part * 128, 128), 128), :].reshape(width, width)
        for block in range(3):
            rows = pl.ds(block * tile, tile)
            starts = [(part * blocks + i) * (3 * tile) + block * tile for i in range(blocks)]
            active = [kv_ext[pl.ds(pl.multiple_of(start, tile), tile), :] for start in starts]
            acc[rows, :] += mm(jnp.concatenate(active, axis=1), second)
        return 0

    lax.fori_loop(0, block_width // 128, widen, 0)

    stores[3].wait()
    for copy in cot_x:
        copy.wait_recv()
    totals = [jnp.zeros((1, width), F32)] * 5
    for block in range(3):
        rows = pl.ds(block * tile, tile)
        normal, rstd = normalise(norm1[rows, :] * g1 + s1 + acc[rows, :] + b2)
        att[rows, :] = (normal * g2 + s2).astype(BF16)
        grad = cot_v[block].astype(F32)
        result = normalise_back(grad * g2, normal, rstd)
        acc[rows, :] = result
        small = result.astype(BF16)
        low[rows, :] = small
        totals[0] = totals[0] + column_sum(grad)
        totals[1] = totals[1] + column_sum(small)

    def att_rows(block):
        return att.at[pl.ds(pl.multiple_of(block * tile, tile), tile), :]

    layer_home = push(att_rows(1 - x), layer_hbm.at[keep], t_send.at[6], t_recv.at[6], place.other_x())
    layer_own = [
        pltpu.make_async_copy(att_rows(x), layer_hbm.at[keep], t_local.at[6]),
        pltpu.make_async_copy(att_rows(2), layer_hbm.at[0], t_local.at[7]),
    ]
    layer_home.start()
    for copy in layer_own:
        copy.start()

    def down(index, _):
        span = pl.ds(pl.multiple_of(index * block_width, block_width), block_width)
        first_piece, second = w1_piece(index), w2[index // 2, index % 2]
        total = jnp.zeros((1, block_width), F32)
        for block in range(3):
            rows = pl.ds(block * tile, tile)
            slope = jnp.concatenate([big[slope_at(index, block, part)] for part in range(2)], axis=0).astype(F32)
            small = (mm_nt(low[rows, :], second) * slope).astype(BF16)
            total = total + column_sum(small)
            acc[rows, :] += mm_nt(small, first_piece)
        sums1_ref[:, span] = total
        return 0

    lax.fori_loop(0, blocks, down, 0)
    stores[2].wait()
    for block in range(3):
        rows = pl.ds(block * tile, tile)
        grad = acc[rows, :]
        totals[2] = totals[2] + column_sum(grad)
        result = normalise_back(grad * g1, norm1[rows, :], spread1[rows, 0:1])
        acc[rows, :] = result
        small = result.astype(BF16)
        totals[3] = totals[3] + column_sum(small)
        grad_att = mm_nt(small, wo[...].reshape(width, width)).astype(BF16)
        totals[4] = totals[4] + column_sum(grad_att)
        q_tmp[rows, :] = grad_att
    for number, total in enumerate(totals):
        sums_ref[number : number + 1, :] = total
    results = [
        pltpu.make_async_copy(acc, gres_hbm, store.at[8]),
        pltpu.make_async_copy(q_tmp, gatt_hbm, store.at[9]),
    ]
    for copy in results:
        copy.start()
    comm.sent(6, comm.count)
    for copy in tok_core:
        copy.wait_send()
    tok_x.wait_send()
    for copy in cot_x:
        copy.wait_send()

    @pl.when(first)
    def _():
        short_x.wait_send()

    @pl.when(core == 0)
    def _():
        short_core.wait_send()

    for copy in layer_own + stores[1:2] + results:
        copy.wait()
    layer_home.wait()


def main(lengths, shards, tok, cot, qv_bias, vectors, ffn_in_bias, dp_count):
    z_count = dp_count // 2
    tile, width = tok.shape[1:]
    rows = 3 * tile
    hidden = ffn_in_bias.shape[0]
    out, dma, vmem = jax.ShapeDtypeStruct, pltpu.SemaphoreType.DMA, pltpu.VMEM

    def chunks_of(shards, fulls):
        qkv, wo, w1, w2 = zip(shards, fulls)
        side = width // 2
        chunks = [(*qkv, 0, 128, part * width + i * side, side) for i in range(2) for part in (1, 2, 0)]
        chunks += [(*wo, 0, 128, i * side, side) for i in range(2)]
        chunks += [(*w1, 0, 128, col, side) for col in range(0, hidden, side)]
        chunks += [(*w2, row, 128, i * side, side) for row in range(0, w2[0].shape[0], 128) for i in range(2)]
        return [(*chunk, number >= len(chunks) - 3) for number, chunk in enumerate(chunks)]

    count = len(chunks_of(shards, shards))
    whole = pl.BlockSpec(memory_space=pltpu.VMEM)
    weights = [out((z_count, 2, *shard.shape), BF16) for shard in shards]
    return pl.pallas_call(
        functools.partial(main_kernel, z_count, tile, chunks_of),
        out_shape=[
            out((tok.shape[0],), jnp.int32),
            weights[0],
            out((width // HEAD_DIM, rows, LANES), BF16),
            out((2 * (width // HEAD_DIM) * 5 * tile, LANES), BF16),
            out((width // LANES, LANES, 5 * tile), BF16),
            out((rows, width), BF16),
            out((3, tile, width), BF16),
            out((rows, width), F32),
            out((rows, width), BF16),
            out((5, width), F32),
            out((1, hidden), F32),
        ],
        in_specs=[pl.BlockSpec(memory_space=pltpu.SMEM)] + [ANY] * 6 + [whole] * 8,
        out_specs=[pl.BlockSpec(memory_space=pltpu.SMEM)] + [ANY] * 8 + [whole] * 2,
        scratch_shapes=[
            vmem((5, tile, width), BF16),
            vmem((tile, width), BF16),
            vmem((3, tile, width), BF16),
            vmem((tile, width), BF16),
            vmem((tile, width), BF16),
            vmem(weights[0].shape, BF16),
            vmem(weights[1].shape, BF16),
            vmem(weights[2].shape, BF16),
            vmem(weights[3].shape, BF16),
            vmem((rows, width), BF16),
            vmem((2 * (width // HEAD_DIM) * 5 * tile, LANES), BF16),
            vmem((width // LANES, LANES, 5 * tile), BF16),
            vmem((width // HEAD_DIM, rows, LANES), BF16),
            vmem((rows, width), BF16),
            vmem((rows, width), F32),
            vmem((rows, LANES), F32),
            vmem((rows, width), F32),
            vmem((rows, width), BF16),
            dma((count, 4)),
            dma((count, 3)),
            dma((count, 4)),
            dma((count, 4)),
            dma((count, 3)),
            dma((count, 3)),
            dma((count,)),
            dma((7,)),
            dma((7,)),
            dma((8,)),
            dma((COT_PIECES,)),
            dma((COT_PIECES,)),
            dma((10,)),
        ],
        compiler_params=params(63, collective_id=0, has_side_effects=True),
        name="main",
    )(lengths, *shards, tok, cot, qv_bias, ffn_in_bias, *vectors)


def back_kernel(z_count, tile, *refs):
    (q_hbm, kv_hbm, turn_hbm, o_hbm, g_hbm, gres_hbm, wqkv_hbm), (sums_mid, sums_hidden), refs = (
        refs[:7],
        refs[7:9],
        refs[9:],
    )
    grad_out, sums_out, q_sum_out, refs = refs[0], refs[1], refs[2], refs[3:]
    q_ext, k_ext, v_ext, k_turn, o_all, g_all, g_ext, gres, big, dq, dk, dv, turned_sum = refs[:13]
    k_sum, v_sum, pair_recv, short_recv, short_send, home, part, part_recv, part_z = refs[13:22]
    tail, tail_recv, tail_z, q_total = refs[22:26]
    load, k_send, k_recv, s_send, s_recv, o_send, o_recv, r_send, r_recv, u_send, u_recv, local = refs[26:]
    place = Place(z_count)
    x, core, z = place.x, place.core, place.z
    keep = 2 - x
    width = o_all.shape[1]
    long_keys = 4 * tile
    pairs = width // LANES
    short_rows, long_rows = pl.ds(2 * tile, tile), pl.ds(0, 2 * tile)
    short_at, long_at = pl.ds(long_keys, tile), pl.ds(0, long_keys)
    loads = []

    def fetch(src, dst):
        copy = pltpu.make_async_copy(src, dst, load.at[len(loads)])
        copy.start()
        loads.append(copy)

    for at, rows in ((short_at, short_rows), (long_at, long_rows)):
        fetch(kv_hbm.at[0, :, at], k_ext.at[:, at])
        fetch(kv_hbm.at[1, :, at], v_ext.at[:, at])
        fetch(turn_hbm.at[:, :, at], k_turn.at[:, :, at])
        fetch(o_hbm.at[rows], o_all.at[rows])
        fetch(g_hbm.at[rows], g_all.at[rows])
        fetch(q_hbm.at[:, rows], q_ext.at[:, rows])
    fetch(gres_hbm, gres)
    for piece in range(3):
        for i in range(z_count):
            fetch(
                wqkv_hbm.at[i, :, :, pl.ds(piece * width, width)],
                big.at[pl.ds(8 * piece + 2 * i, 2)],
            )
    meet(place.more_peers())

    plane = [(shift_z, shift_y) for shift_z in range(z_count) for shift_y in range(2)][1:]
    group = [(shift_x, shift_core) for shift_x in range(2) for shift_core in range(2)][1:]

    class AllSum:
        def __init__(self, mine, by_dp, by_head, send_sems, recv_sems):
            self.mine, self.by_dp, self.by_head = mine, by_dp, by_head
            self.first = [
                push(mine.at[0], by_dp.at[place.dp], send_sems.at[i], recv_sems.at[i], place.shifted(*shift))
                for i, shift in enumerate(plane)
            ]
            at = len(plane)
            self.second = [
                push(mine.at[1], by_head.at[place.head], send_sems.at[at + i], recv_sems.at[at + i], place.beside(*shift))
                for i, shift in enumerate(group)
            ]

        def begin(self):
            for copy in self.first:
                copy.start()
            self.by_dp[place.dp] = self.mine[0]

        def turn(self):
            for copy in self.first:
                copy.wait_recv()
            total = self.by_dp[0]
            for i in range(1, self.by_dp.shape[0]):
                total = total + self.by_dp[i]
            self.mine[1] = total
            for copy in self.second:
                copy.start()
            self.by_head[place.head] = total

        def result(self):
            for copy in self.second:
                copy.wait_recv()
            total = self.by_head[0]
            for i in range(1, self.by_head.shape[0]):
                total = total + self.by_head[i]
            return total

        def sent(self):
            for copy in self.first + self.second:
                copy.wait_send()

    early = AllSum(part, part_recv, part_z, r_send, r_recv)
    late = AllSum(tail, tail_recv, tail_z, u_send, u_recv)
    part[0] = jnp.zeros(part.shape[1:], F32)
    part[0, 1:2, :] = sums_mid[4:5, :]
    part[0, 2:3, :] = sums_mid[3:4, :]
    part[0, 3:4, :] = sums_mid[2:3, :]
    for i in range(sums_hidden.shape[1] // width):
        part[0, 4 + i : 5 + i, :] = sums_hidden[:, i * width : (i + 1) * width]
    part[0, 8:9, :] = sums_mid[1:2, :]
    part[0, 9:10, :] = sums_mid[0:1, :]
    early.begin()
    q_total[...] = jnp.zeros(q_total.shape, F32)

    kinds = (dk, dv)

    def to_sibling(kind, turn, block, side):
        columns = pl.ds(side * (width // 2), width // 2)
        return push(
            kinds[kind].at[2 * block + 1 - core, :, columns],
            pair_recv.at[kind, block, :, columns],
            k_send.at[kind, 2 * turn + side],
            k_recv.at[kind, 2 * turn + side],
            place.other_core(),
        )

    pair_copies = [
        [[to_sibling(kind, turn, block, side) for side in range(2)] for kind in range(2)]
        for turn, block in enumerate((1 - x, x))
    ]

    def start_side(turn, side):
        for copies in pair_copies[turn]:
            copies[side].start()
    short_core = [
        push(kinds[kind].at[4], short_recv.at[0, kind], s_send.at[0, kind], s_recv.at[0, kind], place.other_core())
        for kind in range(2)
    ]
    short_x = [
        push(short_send.at[kind], short_recv.at[1, kind], s_send.at[1, kind], s_recv.at[1, kind], place.other_x())
        for kind in range(2)
    ]
    grad_home = push(home.at[0], grad_out.at[keep], o_send.at[0], o_recv.at[0], place.other_x())
    grad_own = [
        pltpu.make_async_copy(home.at[1], grad_out.at[keep], local.at[0]),
        pltpu.make_async_copy(home.at[2], grad_out.at[0], local.at[1]),
    ]
    low_half = head_lanes(0) > 0
    scale = 1.0 / math.sqrt(HEAD_DIM)

    def columns_of(pair):
        return pl.ds(pl.multiple_of(pair * LANES, LANES), LANES)

    def prepare(pair, rows):
        columns = columns_of(pair)
        for half in range(2):
            grad = g_all[rows, columns].astype(F32) * head_lanes(half)
            centre = jnp.sum(grad * o_all[rows, columns].astype(F32), axis=-1, keepdims=True)
            high, middle, low = split_three(-centre)
            grad = grad + high * spare(half, 0) + middle * spare(half, 1) + low * spare(half, 2)
            g_ext[2 * pair + half, rows, :] = grad.astype(BF16)

    def unit(pair, half, at, rows):
        head = 2 * pair + half
        key, value, turned = k_ext[head, at, :], v_ext[head, at, :], k_turn[pair, half * HEAD_DIM : (half + 1) * HEAD_DIM, at]
        query, grad = q_ext[head, rows, :], g_ext[head, rows, :]
        probs = jnp.exp(mm_nt(key, query))
        scores = (probs * mm_nt(value, grad)).astype(BF16)
        return mm(scores, query), mm(probs.astype(BF16), grad), mm(turned, scores)

    def join(parts):
        return jnp.where(low_half, parts[0], parts[1])

    def put_queries(pair, block, turned_parts):
        grad_query = (jnp.concatenate(turned_parts, axis=0).T * scale).astype(BF16)
        columns = columns_of(pair)
        dq[block, :, columns] = grad_query
        q_total[:, columns] += column_sum(grad_query)

    def turned_rows(head):
        return pl.ds(pl.multiple_of(head * HEAD_DIM, HEAD_DIM), HEAD_DIM)

    def short_pair(pair, _):
        prepare(pair, short_rows)
        results = [unit(pair, half, short_at, short_rows) for half in range(2)]
        columns = columns_of(pair)
        dk[4, :, columns] = join([result[0] for result in results]).astype(BF16)
        dv[4, :, columns] = join([result[1] for result in results]).astype(BF16)
        put_queries(pair, 2, [result[2] for result in results])
        return 0

    for copy in loads[:6]:
        copy.wait()
    lax.fori_loop(0, pairs, short_pair, 0, unroll=2)

    @pl.when(core == 1)
    def _():
        for copy in short_core:
            copy.start()

    for copy in loads[6:12]:
        copy.wait()

    def half_keys(block):
        return pl.ds(pl.multiple_of(block * 2 * tile, 2 * tile), 2 * tile)

    def q_tile(block):
        return pl.ds(pl.multiple_of(block * tile, tile), tile)

    def store_keys(ref, block, columns, value):
        for i in range(2):
            ref[2 * block + i, :, columns] = value[i * tile : (i + 1) * tile].astype(BF16)

    def pass_one(pair, _):
        prepare(pair, long_rows)
        columns = columns_of(pair)
        results = [unit(pair, half, long_at, q_tile(1 - x)) for half in range(2)]
        k_sum[:, columns] = join([result[0] for result in results])
        v_sum[:, columns] = join([result[1] for result in results])
        put_queries(pair, 1 - x, [result[2] for result in results])

        @pl.when((pair == 1) & (x == 1) & (core == 0))
        def _():
            for kind in range(2):
                short_core[kind].wait_recv()
                total = kinds[kind][4].astype(F32) + short_recv[0, kind].astype(F32)
                short_send[kind] = total.astype(BF16)
                short_x[kind].start()

        return 0

    lax.fori_loop(0, pairs, pass_one, 0, unroll=2)
    early.turn()

    def more_keys(pair, block):
        at = half_keys(block)
        columns = columns_of(pair)
        results = [unit(pair, half, at, q_tile(x)) for half in range(2)]
        store_keys(dk, block, columns, k_sum[at, columns] + join([result[0] for result in results]))
        store_keys(dv, block, columns, v_sum[at, columns] + join([result[1] for result in results]))
        return results

    def pass_two(pair, _):
        results = more_keys(pair, 1 - x)
        for half in range(2):
            turned_sum[turned_rows(2 * pair + half), :] = results[half][2]

        @pl.when(pair == pairs // 2 - 1)
        def _():
            start_side(0, 0)

        return 0

    lax.fori_loop(0, pairs, pass_two, 0, unroll=2)
    start_side(0, 1)
    for copy in loads[12:]:
        copy.wait()

    def weight(piece):
        return big[8 * piece : 8 * piece + 8].reshape(width, width)

    def from_queries(block):
        return gres[q_tile(block), :] + mm_nt(dq[block], weight(0))

    def from_keys(block, grad, copies):
        for kind in range(2):
            for copy in copies[kind]:
                copy.wait_recv()
            total = kinds[kind][2 * block + core].astype(F32) + pair_recv[kind, block].astype(F32)
            grad = grad + mm_nt(total.astype(BF16), weight(1 + kind))
        return grad

    home[0] = from_keys(1 - x, from_queries(1 - x), pair_copies[0]).astype(BF16)
    grad_home.start()

    def pass_three(pair, _):
        results = more_keys(pair, x)
        put_queries(pair, x, [results[half][2] + turned_sum[turned_rows(2 * pair + half), :] for half in range(2)])

        @pl.when(pair == pairs // 2 - 1)
        def _():
            start_side(1, 0)

        return 0

    lax.fori_loop(0, pairs, pass_three, 0, unroll=2)
    start_side(1, 1)
    tail[0] = jnp.broadcast_to(q_total[...], tail.shape[1:])
    late.begin()
    sums_out[...] = early.result()
    first = (x == 0) & (core == 0)
    gres[q_tile(2), :] = from_queries(2)

    @pl.when(first)
    def _():
        grad = gres[q_tile(2), :]
        for kind in range(2):
            short_core[kind].wait_recv()
            short_x[kind].wait_recv()
            total = kinds[kind][4].astype(F32) + short_recv[0, kind].astype(F32)
            total = total + short_recv[1, kind].astype(F32)
            grad = grad + mm_nt(total.astype(BF16), weight(1 + kind))
        gres[q_tile(2), :] = grad

    home[2] = gres[q_tile(2), :].astype(BF16)
    grad_own[1].start()
    grad = from_queries(x)
    late.turn()
    home[1] = from_keys(x, grad, pair_copies[1]).astype(BF16)
    grad_own[0].start()
    q_sum_out[...] = late.result()
    early.sent()
    late.sent()
    for turn in pair_copies:
        for copies in turn:
            for copy in copies:
                copy.wait_send()

    @pl.when(core == 1)
    def _():
        for copy in short_core:
            copy.wait_send()

    @pl.when((x == 1) & (core == 0))
    def _():
        for copy in short_x:
            copy.wait_send()

    for copy in grad_own:
        copy.wait()
    grad_home.wait()


def back(queries, keys_values, turned, attended, grad_attended, gres, qkv_full, sums_mid, sums_hidden, dp_count):
    rows, width = attended.shape
    tile = rows // 3
    z_count = dp_count // 2
    heads = width // HEAD_DIM
    whole = pl.BlockSpec(memory_space=pltpu.VMEM)
    out, dma, vmem = jax.ShapeDtypeStruct, pltpu.SemaphoreType.DMA, pltpu.VMEM
    return pl.pallas_call(
        functools.partial(back_kernel, z_count, tile),
        out_shape=[out((3, tile, width), BF16), out((16, width), F32), out((8, width), F32)],
        in_specs=[ANY] * 7 + [whole] * 2,
        out_specs=[ANY, whole, whole],
        scratch_shapes=[
            vmem((heads, rows, LANES), BF16),
            vmem((heads, 5 * tile, LANES), BF16),
            vmem((heads, 5 * tile, LANES), BF16),
            vmem((heads // 2, LANES, 5 * tile), BF16),
            vmem((rows, width), BF16),
            vmem((rows, width), BF16),
            vmem((heads, rows, LANES), BF16),
            vmem((rows, width), F32),
            vmem((24, 128, width), BF16),
            vmem((3, tile, width), BF16),
            vmem((5, tile, width), BF16),
            vmem((5, tile, width), BF16),
            vmem((width, tile), F32),
            vmem((4 * tile, width), F32),
            vmem((4 * tile, width), F32),
            vmem((2, 2, tile, width), BF16),
            vmem((2, 2, tile, width), BF16),
            vmem((2, tile, width), BF16),
            vmem((3, tile, width), BF16),
            vmem((2, 16, width), F32),
            vmem((dp_count, 16, width), F32),
            vmem((4, 16, width), F32),
            vmem((2, 8, width), F32),
            vmem((dp_count, 8, width), F32),
            vmem((4, 8, width), F32),
            vmem((1, width), F32),
            dma((13 + 3 * z_count,)),
            dma((2, 4)),
            dma((2, 4)),
            dma((2, 2)),
            dma((2, 2)),
            dma((1,)),
            dma((1,)),
            dma((dp_count + 2,)),
            dma((dp_count + 2,)),
            dma((dp_count + 2,)),
            dma((dp_count + 2,)),
            dma((2,)),
        ],
        compiler_params=params(63, collective_id=1, has_side_effects=True),
        name="back",
    )(
        queries,
        keys_values.reshape(2, heads, 5 * tile, LANES),
        turned,
        attended,
        grad_attended,
        gres,
        qkv_full,
        sums_mid,
        sums_hidden,
    )


def paired_chips(
    tokens,
    out_cotangent,
    lengths,
    qkv_weight,
    out_weight,
    ffn_in_weight,
    ffn_out_weight,
    qv_bias,
    out_bias,
    ln1_gain,
    ln1_bias,
    ffn_in_bias,
    ffn_out_bias,
    ln2_gain,
    ln2_bias,
    dp_count,
):
    hidden = ffn_in_bias.shape[0]
    shards = (qkv_weight, out_weight, ffn_in_weight, ffn_out_weight)
    vectors = (out_bias, ln1_gain, ln1_bias, ffn_out_bias, ln2_gain, ln2_bias)
    results = main(lengths, shards, tokens, out_cotangent, qv_bias, vectors, ffn_in_bias, dp_count)
    perm, qkv_full = results[:2]
    queries, keys_values, turned, attended, out_sorted, gres, grad_attended, sums_mid, sums_hidden = results[2:]
    grad_sorted, sums, q_sums = back(
        queries, keys_values, turned, attended, grad_attended, gres, qkv_full, sums_mid, sums_hidden, dp_count
    )
    return tuple(unsort_sequences(perm, out_sorted, grad_sorted, sums, q_sums, hidden))


def body_for(mesh):
    dp_count, head_count = mesh.shape["dp"], mesh.shape["head"]

    def body(*arrays):
        tokens = arrays[0]
        seqs, tile, width = tokens.shape
        fits = head_count == 4 and seqs == 3 and dp_count == 8 and width == 1024 and tile == 256
        if fits:
            return paired_chips(*arrays, dp_count)
        return on_device(*arrays)

    return body


def solution(mesh):
    return jax.shard_map(
        body_for(mesh),
        mesh=mesh,
        in_specs=(
            P("dp", "head", None),
            P("dp", "head", None),
            P("dp"),
            P("dp", None),
            P("dp", None),
            P("dp", None),
            P("dp", None),
            P(),
            P(),
            P(),
            P(),
            P(),
            P(),
            P(),
            P(),
        ),
        out_specs=(P("dp", "head", None), P("dp", "head", None), P(), P(), P(), P(), P(), P()),
        check_vma=False,
    )
```
